32 devices in a mesh: gx: 8 (over z, x), yz: 4 (over y, core).
Axes of the slice: x: 2, y: 2, z: 4, core: 2. Of those that a mesh axis runs over, the one named last changes fastest.
Arguments:
- residuals: float32 [32, 3, 64, 32, 128], P(None, None, 'gx', 'yz'), may hold values from -6 to 6
- vectors: float32 [8, 3, 64, 32, 128], P(None, None, 'gx', 'yz'), may hold values from -0.05 to 1.6
- phases: int32 [64, 32, 128], P('gx', 'yz'), may hold values from 0 to 7
- stiffness: float32 [8], replicated, may hold values from 0.5 to 4
Outputs:
- coarse_coeffs: float32 [256, 32], P(('gx', 'yz'))
- preconditioned: float32 [32, 3, 64, 32, 128], P(None, None, 'gx', 'yz')
The draws below stay inside these ranges and needn't reach their ends.
All inputs are finite; a program needn't handle non-finite values.
Results may differ from the reference program's by a relative error of at most 0.0003.
Values sent between devices are 32-bit elements; how exact they have to be, the bound alone decides.
A program may use at most 192 MiB of HBM per device.

```python
import math
import jax
import jax.numpy as jnp
from jax import lax

K = 8
PHASES = 8
CX = 8
CY = 8
CZ = 128
RHS = 32
SWEEPS = 4
NX = 64
NY = 32
N_GX = 8
N_YZ = 4


def draw_vectors(key, part):
    first_key, second_key = jax.random.split(jax.random.fold_in(key, 17))
    means = jax.random.uniform(first_key, (K, 3, 1, 1, 1), jnp.float32, 0.2, 1.0)
    rough = jnp.clip(0.05 * jax.random.normal(second_key, (K, 3, NX, NY, CZ), jnp.float32), -0.25, 0.25)
    return means + rough


def set_ends(result, rng, smallest, top_value):
    spot = [jax.random.randint(jax.random.fold_in(rng, axis), (), 0, length) for axis, length in enumerate(result.shape)]
    main_axis = result.shape.index(max(result.shape))
    next_to = spot[:main_axis] + [(spot[main_axis] + 1) % result.shape[main_axis]] + spot[main_axis + 1:]
    return result.at[tuple(spot)].set(smallest).at[tuple(next_to)].set(top_value)


def level_of(own_key, shape, cuts, smallest, top_value):
    factor_of, own = 1.0, jax.random.fold_in(own_key, 6)
    for dim, blocks in cuts:
        steps = jnp.exp(jax.random.uniform(jax.random.fold_in(own, dim), (blocks,), jnp.float32, smallest / len(cuts), top_value / len(cuts)))
        factor_of = factor_of * jnp.repeat(steps, shape[dim] // blocks).reshape([-1 if axis == dim else 1 for axis in range(len(shape))])
    return factor_of


def scatter_about(rng, dims, deviation, limit, shards=(), held_as=jnp.bfloat16):
    drawn = jax.random.normal(rng, dims, jnp.float32) * deviation
    if len(shards) > 0:
        drawn = level_of(rng, dims, shards, -0.22, 0.18) * drawn
    return jnp.clip(drawn, min=-limit, max=limit).astype(held_as)


def setup_inputs(seed: int = 0) -> dict:
    arg_keys = jax.random.split(jax.random.key(seed), 5)
    return {
        "residuals": scatter_about(arg_keys[0], (RHS, 3, NX, NY, CZ), 1.0, 6.0, ((2, 8), (3, 4)), jnp.float32),
        "vectors": draw_vectors(jax.random.fold_in(arg_keys[4], 71), 0),
        "phases": set_ends(jax.random.randint(arg_keys[2], (NX, NY, CZ), 0, PHASES), jax.random.fold_in(arg_keys[2], 1), 0, PHASES - 1).astype(jnp.int32),
        "stiffness": jnp.clip(jnp.exp(jax.random.uniform(arg_keys[3], (PHASES,), jnp.float32, math.log(0.5), math.log(4.0))), 0.5, 4.0),
    }


HIGH = lax.Precision.HIGHEST

def face_weights(modulus_ext):
    centre = modulus_ext[1:-1, 1:-1, :]
    zpadded = jnp.pad(centre, ((0, 0), (0, 0), (1, 1)))
    west_side = 0.5 * (centre + modulus_ext[:-2, 1:-1, :])
    east_side = 0.5 * (centre + modulus_ext[2:, 1:-1, :])
    south_side = 0.5 * (centre + modulus_ext[1:-1, :-2, :])
    north_side = 0.5 * (centre + modulus_ext[1:-1, 2:, :])
    lower_side = 0.5 * (centre + zpadded[:, :, :-2])
    upper_side = 0.5 * (centre + zpadded[:, :, 2:])
    diagonal_sum = 0.002 + west_side + east_side + south_side + north_side + lower_side + upper_side
    return (diagonal_sum, west_side, east_side, south_side, north_side, lower_side, upper_side)

def operate(values, weights):
    diagonal_sum, west_side, east_side, south_side, north_side, lower_side, upper_side = weights
    centre = values[..., 1:-1, 1:-1, :]
    spacing = [(0, 0)] * (values.ndim - 1) + [(1, 1)]
    zpadded = jnp.pad(centre, spacing)
    beside = west_side * values[..., :-2, 1:-1, :] + east_side * values[..., 2:, 1:-1, :]
    beside = beside + south_side * values[..., 1:-1, :-2, :] + north_side * values[..., 1:-1, 2:, :]
    beside = beside + lower_side * zpadded[..., :-2] + upper_side * zpadded[..., 2:]
    return diagonal_sum * centre - beside

def coarse_blocks(vectors_ext, modulus_ext):
    weights = face_weights(modulus_ext[1:-1, 1:-1, :])
    own_cells = vectors_ext[:, :, 2:-2, 2:-2, :]
    isolated = jnp.pad(own_cells, ((0, 0), (0, 0), (1, 1), (1, 1), (0, 0)))
    applied = operate(isolated, weights)
    self_block = jnp.einsum('kcxyz,lcxyz->kl', own_cells, applied, precision=HIGH)
    west_block = -jnp.einsum('kcyz,lcyz->kl', weights[1][0] * own_cells[:, :, 0], vectors_ext[:, :, 1, 2:-2, :], precision=HIGH)
    east_block = -jnp.einsum('kcyz,lcyz->kl', weights[2][-1] * own_cells[:, :, -1], vectors_ext[:, :, -2, 2:-2, :], precision=HIGH)
    south_block = -jnp.einsum('kcxz,lcxz->kl', weights[3][:, 0] * own_cells[:, :, :, 0], vectors_ext[:, :, 2:-2, 1, :], precision=HIGH)
    north_block = -jnp.einsum('kcxz,lcxz->kl', weights[4][:, -1] * own_cells[:, :, :, -1], vectors_ext[:, :, 2:-2, -2, :], precision=HIGH)
    return jnp.stack([self_block, west_block, east_block, south_block, north_block])

def assemble(blocks, stride):
    count = blocks.shape[0]
    width = blocks.shape[2]
    rows_index = jnp.arange(count, dtype=jnp.int32)
    assembled = jnp.zeros((count, width, count, width), jnp.float32)
    for slot_index, offset in enumerate((0, -stride, stride, -1, 1)):
        select = (rows_index[None, :] == rows_index[:, None] + offset).astype(jnp.float32)
        assembled = assembled + blocks[:, slot_index][:, :, None, :] * select[:, None, :, None]
    return assembled.reshape(count * width, count * width)

def local_solve(deflated_ext, modulus_ext):
    weights = face_weights(modulus_ext)
    inner_mod = modulus_ext[1:-1, 1:-1, :]
    width_x = inner_mod.shape[0]
    width_y = inner_mod.shape[1]
    x_index = jnp.arange(width_x)[:, None]
    y_index = jnp.arange(width_y)[None, :]
    x_edge = (x_index == 0) | (x_index == width_x - 1)
    y_edge = (y_index == 0) | (y_index == width_y - 1)
    corner = x_edge & y_edge
    active = ((inner_mod > 0) & jnp.logical_not(corner[:, :, None])).astype(jnp.float32)
    approx = jnp.zeros_like(deflated_ext)
    for repeat in range(SWEEPS):
        padded = jnp.pad(approx, ((0, 0), (0, 0), (1, 1), (1, 1), (0, 0)))
        approx = active * (approx + 0.8 * (deflated_ext - operate(padded, weights)) / weights[0])
    return approx[:, :, 1:-1, 1:-1, :]

def reference(residuals, vectors, phases, stiffness):
    count = N_GX * N_YZ
    modulus = jnp.take(stiffness, phases, axis=0)
    modulus_pad = jnp.pad(modulus, ((2, 2), (2, 2), (0, 0)))
    vectors_pad = jnp.pad(vectors, ((0, 0), (0, 0), (2, 2), (2, 2), (0, 0)))
    zero_index = jnp.zeros((), jnp.int32)
    block_ids = jnp.arange(count, dtype=jnp.int32)

    def starts(block_index):
        x_start = (block_index // N_YZ * CX).astype(jnp.int32)
        y_start = (block_index % N_YZ * CY).astype(jnp.int32)
        return (x_start, y_start)

    def coarse_part(block_index):
        x_start, y_start = starts(block_index)
        modulus_ext = lax.dynamic_slice(modulus_pad, (x_start, y_start, zero_index), (CX + 4, CY + 4, CZ))
        vectors_ext = lax.dynamic_slice(vectors_pad, (zero_index, zero_index, x_start, y_start, zero_index), (K, 3, CX + 4, CY + 4, CZ))
        own_res = lax.dynamic_slice(residuals, (zero_index, zero_index, x_start, y_start, zero_index), (RHS, 3, CX, CY, CZ))
        own_vec = vectors_ext[:, :, 2:-2, 2:-2, :]
        rhs_part = jnp.einsum('kcxyz,rcxyz->kr', own_vec, own_res, precision=HIGH)
        return (coarse_blocks(vectors_ext, modulus_ext), rhs_part)
    blocks, rhs_parts = lax.map(coarse_part, block_ids)
    matrix = assemble(blocks, N_YZ)
    coarse_rhs = rhs_parts.reshape(count * K, RHS)
    factor = jnp.linalg.cholesky(matrix)
    coarse_coeffs = jax.scipy.linalg.cho_solve((factor, True), coarse_rhs)
    coeff_grid = coarse_coeffs.reshape(N_GX, N_YZ, K, RHS)
    vector_grid = vectors.reshape(K, 3, N_GX, CX, N_YZ, CY, CZ)
    correction = jnp.einsum('gqkr,kcgaqbz->rcgaqbz', coeff_grid, vector_grid, precision=HIGH).reshape(RHS, 3, NX, NY, CZ)
    corr_pad = jnp.pad(correction, ((0, 0), (0, 0), (2, 2), (2, 2), (0, 0)))
    res_pad = jnp.pad(residuals, ((0, 0), (0, 0), (1, 1), (1, 1), (0, 0)))

    def local_block(block_index):
        x_start, y_start = starts(block_index)
        modulus_ext = lax.dynamic_slice(modulus_pad, (x_start, y_start, zero_index), (CX + 4, CY + 4, CZ))
        corr_ext = lax.dynamic_slice(corr_pad, (zero_index, zero_index, x_start, y_start, zero_index), (RHS, 3, CX + 4, CY + 4, CZ))
        res_ext = lax.dynamic_slice(res_pad, (zero_index, zero_index, x_start, y_start, zero_index), (RHS, 3, CX + 2, CY + 2, CZ))
        deflated_ext = res_ext - operate(corr_ext, face_weights(modulus_ext))
        local_part = local_solve(deflated_ext, modulus_ext)
        return corr_ext[:, :, 2:-2, 2:-2, :] + local_part
    pieces = lax.map(local_block, block_ids)
    preconditioned = pieces.reshape(N_GX, N_YZ, RHS, 3, CX, CY, CZ).transpose(2, 3, 0, 4, 1, 5, 6).reshape(RHS, 3, NX, NY, CZ)
    return (coarse_coeffs, preconditioned)
```

```python
import functools

import jax
import jax.numpy as jnp
from jax import lax
from jax.experimental import pallas as pl
from jax.experimental.pallas import tpu as pltpu
from jax.sharding import PartitionSpec as P

SWEEPS = 4


HIGH = lax.Precision.HIGHEST


MESH = pl.DeviceIdType.MESH


def eliminate(rows, size):
    sublane = lax.broadcasted_iota(jnp.int32, rows[0].shape, 0)
    for p in range(size):
        reduced = []
        for a in rows:
            column = jnp.broadcast_to(a[:, p : p + 1], a.shape)
            pivot = a[p : p + 1, :] / column[p : p + 1, :]
            reduced.append(jnp.where(sublane == p, pivot, a - column * pivot))
        rows = reduced
    return rows


def product(a, b):
    return jnp.dot(a, b, precision=HIGH, preferred_element_type=jnp.float32)


def cyclic_solve(rows, size):
    count = len(rows)
    width = rows[0].shape[1]
    lane = lax.broadcasted_iota(jnp.int32, rows[0].shape, 1)
    is_own = lane < size
    is_low = (lane >= size) & (lane < 2 * size)
    is_high = (lane >= 2 * size) & (lane < 3 * size)
    is_rhs = lane >= 3 * size
    live = list(range(count))
    system = dict(enumerate(rows))
    levels = []
    while len(live) > 1:
        out = live[1::2]
        kept = live[0::2]
        solved = dict(zip(out, eliminate([system[i] for i in out], size)))
        fresh = {}
        for place, i in enumerate(kept):
            a = system[i]
            total = jnp.where(is_own | is_rhs, a, 0.0)
            if place > 0:
                t = product(a[:, size : 2 * size], solved[out[place - 1]])
                shifted = pltpu.roll(t, width - 2 * size, 1)
                total = total - jnp.where(is_own, shifted, jnp.where(is_low | is_rhs, t, 0.0))
            if place < len(out):
                t = product(a[:, 2 * size : 3 * size], solved[out[place]])
                shifted = pltpu.roll(t, width - size, 1)
                total = total - jnp.where(is_own, shifted, jnp.where(is_high | is_rhs, t, 0.0))
            fresh[i] = total
        levels.append((live, out, solved))
        system = fresh
        live = kept
    last = eliminate([system[live[0]]], size)[0]
    answer = {live[0]: last[:, 3 * size :]}
    for before, out, solved in reversed(levels):
        for i in out:
            a = solved[i]
            place = before.index(i)
            x = a[:, 3 * size :] - product(a[:, size : 2 * size], answer[before[place - 1]])
            if place + 1 < len(before):
                x = x - product(a[:, 2 * size : 3 * size], answer[before[place + 1]])
            answer[i] = x
    return [answer[i] for i in range(count)]


WEST, EAST, SOUTH, NORTH, LOW, HIGH_Z = range(1, 7)


def sweep_rates(sweeps, damping):
    powers = [0.0] * sweeps
    term = [1.0]
    for _ in range(sweeps):
        for i, value in enumerate(term):
            powers[i] += value
        longer = [0.0] * (len(term) + 1)
        for i, value in enumerate(term):
            longer[i] += (1.0 - damping) * value
            longer[i + 1] += damping * value
        term = longer
    return damping * powers[0], [powers[i] / powers[i - 1] for i in range(sweeps - 1, 0, -1)]


def packed(v):
    coarse = v.astype(jnp.bfloat16).astype(jnp.float32)
    return jnp.concatenate([coarse, v - coarse], axis=0).astype(jnp.bfloat16)


def kernel(
    count_x, count_y, scale_all, rates,
    stiffness, phases, vectors, res,
    mine, out,
    ext, vraw, rbuf, hx, hy, ybuf, obuf, mown, msend, mx, my,
    weights, hweights, own_p, side_y, side_x, phis, lhs,
    panel, gathered, coeffs, first, second, third,
    load_sem, res_sem, out_sem, panel_send, panel_recv, halo_send, halo_recv
):
    index_x = lax.axis_index("gx")
    index_y = lax.axis_index("yz")
    count = count_x * count_y
    me = index_x * count_y + index_y
    rhs, parts, depth, breadth, length = res.shape
    width = vectors.shape[0]
    levels = stiffness.shape[0]
    wide = breadth + 4
    cross = breadth + 2
    barrier = pltpu.get_barrier_semaphore()
    zero = jnp.zeros((width, length), jnp.float32)
    tall = jnp.zeros((rhs, length), jnp.float32)

    def rows_of(ref):
        return ref.reshape(ref.shape[0] * breadth, length)

    def load(i, carry):
        c = i // depth
        x = i - c * depth
        pltpu.make_async_copy(vectors.at[:, c, x], vraw.at[i], load_sem).start()
        return carry

    lax.fori_loop(0, parts * depth, load, 0)

    def load_res(i, carry):
        c = i // depth
        x = i - c * depth
        pltpu.make_async_copy(res.at[:, c, x], rbuf.at[i], res_sem).start()
        return carry

    lax.fori_loop(0, parts * depth, load_res, 0)

    def clear_y(y, carry):
        for f in range(parts + 1):
            for x in (0, 1, depth + 2, depth + 3):
                ext[f, x, y] = zero
        return carry

    def clear_x(x, carry):
        for f in range(parts + 1):
            for y in (0, 1, breadth + 2, breadth + 3):
                ext[f, x + 2, y] = zero
        return carry

    lax.fori_loop(0, wide, clear_y, 0)
    lax.fori_loop(0, depth, clear_x, 0)
    mx[...] = jnp.zeros(mx.shape, jnp.float32)
    my[...] = jnp.zeros(my.shape, jnp.float32)

    def each_other(act):
        def along(g, carry):
            for h in range(count_y):
                pl.when(jnp.logical_or(g != index_x, h != index_y))(functools.partial(act, g, h))
            return carry

        lax.fori_loop(0, count_x, along, 0)

    def greet(g, h):
        pl.semaphore_signal(barrier, inc=1, device_id=(g, h), device_id_type=MESH)

    each_other(greet)

    for x in range(depth):
        p = phases[x]
        m = jnp.zeros(p.shape, jnp.float32)
        for level in range(levels):
            m = jnp.where(p == level, stiffness[level], m)
        mown[pl.ds(x * breadth, breadth), :] = m
    for side in range(2):
        for layer in range(2):
            y = layer + side * (breadth - 2)
            msend[side, layer] = mown[pl.ds(y, depth, stride=breadth), :]

    def spread_own(x, carry):
        for y in range(breadth):
            row = mown[pl.ds(x * breadth + y, 1), :]
            ext[parts, x + 2, y + 2] = jnp.broadcast_to(row, (width, length))
        return carry

    lax.fori_loop(0, depth, spread_own, 0)
    pltpu.make_async_copy(vraw, vraw, load_sem).wait()

    def fill(i, carry):
        c = i // depth
        x = i - c * depth
        tiles = rows_of(vraw.at[i])
        for y in range(breadth):
            ext[c, x + 2, y + 2] = tiles[pl.ds(y, width, stride=breadth), :]
        return carry

    lax.fori_loop(0, parts * depth, fill, 0)
    pl.semaphore_wait(barrier, count - 1)

    def can(dx, dy):
        ok = index_x >= 0
        if dx:
            ok = index_x > 0 if dx < 0 else index_x < count_x - 1
        if dy:
            ok_y = index_y > 0 if dy < 0 else index_y < count_y - 1
            ok = jnp.logical_and(ok, ok_y) if dx else ok_y
        return ok

    def exchange(source, target, dx, dy, slot):
        return pltpu.make_async_remote_copy(
            src_ref=source,
            dst_ref=target,
            send_sem=halo_send.at[slot],
            recv_sem=halo_recv.at[slot],
            device_id=(index_x + dx, index_y + dy),
            device_id_type=MESH,
        )

    started = []

    def start(source, target, dx, dy):
        copy = exchange(source, target, dx, dy, len(started))
        pl.when(can(dx, dy))(copy.start)
        started.append((can(dx, dy), can(-dx, -dy), copy))

    def arrived(low, high):
        for _, receives, copy in started[low:high]:
            pl.when(receives)(copy.wait_recv)

    start(mown.at[pl.ds(0, 2 * breadth)], mx.at[1], -1, 0)
    start(mown.at[pl.ds((depth - 2) * breadth, 2 * breadth)], mx.at[0], 1, 0)
    start(msend.at[0], my.at[1], 0, -1)
    start(msend.at[1], my.at[0], 0, 1)

    field = pl.ds(0, parts)
    inner_x, inner_y = pl.ds(2, depth), pl.ds(2, breadth)

    def layer(step):
        start(ext.at[field, 2 + step, inner_y], ext.at[field, depth + 2 + step, inner_y], -1, 0)
        start(ext.at[field, depth + 1 - step, inner_y], ext.at[field, 1 - step, inner_y], 1, 0)
        start(ext.at[field, inner_x, 2 + step], ext.at[field, inner_x, breadth + 2 + step], 0, -1)
        start(ext.at[field, inner_x, breadth + 1 - step], ext.at[field, inner_x, 1 - step], 0, 1)

    for x, dx, to_x in ((2, -1, depth + 2), (depth + 1, 1, 1)):
        for y, dy, to_y in ((2, -1, breadth + 2), (breadth + 1, 1, 1)):
            start(ext.at[:, x, y], ext.at[:, to_x, to_y], dx, dy)
    layer(0)
    layer(1)

    base_slot = len(started)
    ways = ((-1, 0), (1, 0), (0, -1), (0, 1))

    def res_copy(way, part):
        dx, dy = ways[way]
        if dx:
            source, target = res.at[:, part, 0 if dx < 0 else depth - 1], hx.at[1 - way, part]
        else:
            source, target = ybuf.at[way - 2, part], hy.at[3 - way, part]
        return exchange(source, target, dx, dy, base_slot + part * 4 + way)

    pltpu.make_async_copy(rbuf, rbuf, res_sem).wait()

    def loads(i, sums):
        f = i // depth
        x = i - f * depth
        tiles = rows_of(rbuf.at[i])
        for side in range(2):
            ybuf[side, f, x] = tiles[pl.ds(side * (breadth - 1), rhs, stride=breadth), :]
        for y in range(breadth):
            v = ext[f, x + 2, y + 2]
            sums = tuple(
                total + v * tiles[pl.ds(r * breadth + y, 1), :] for r, total in enumerate(sums)
            )
        return sums

    sums = lax.fori_loop(0, parts * depth, loads, (zero,) * rhs)
    lane = lax.broadcasted_iota(jnp.int32, panel.shape, 1)

    def placed(total, at):
        return jnp.where(lane == at, jnp.sum(total, axis=1, keepdims=True), 0.0)

    size = count_y * width
    row = jnp.zeros(panel.shape, jnp.float32)
    for r in range(rhs):
        row = row + placed(sums[r], 3 * size + r)

    arrived(0, 4)

    def spread_x(y, carry):
        for side in range(2):
            for step in range(2):
                line = mx[side, pl.ds(step * breadth + y, 1), :]
                ext[parts, side * (depth + 2) + step, y + 2] = jnp.broadcast_to(line, (width, length))
        return carry

    def spread_y(x, carry):
        for side in range(2):
            for step in range(2):
                line = my[side, step, pl.ds(x, 1), :]
                ext[parts, x + 2, side * (breadth + 2) + step] = jnp.broadcast_to(line, (width, length))
        return carry

    lax.fori_loop(0, breadth, spread_x, 0)
    lax.fori_loop(0, depth, spread_y, 0)
    arrived(4, 8)
    z = lax.broadcasted_iota(jnp.int32, (width, length), 1)

    def weigh(i, carry):
        inside = jnp.where(jnp.logical_or(i == 0, i == depth + 1), 0.0, 1.0).astype(jnp.float32)
        for j in range(cross):
            x, y = i + 1, j + 1
            m = ext[parts, x, y]
            low = 0.5 * (m + jnp.where(z > 0, pltpu.roll(m, 1, 1), 0.0))
            high = 0.5 * (m + jnp.where(z < length - 1, pltpu.roll(m, length - 1, 1), 0.0))
            west = 0.5 * (m + ext[parts, x - 1, y])
            east = 0.5 * (m + ext[parts, x + 1, y])
            south = 0.5 * (m + ext[parts, x, y - 1])
            north = 0.5 * (m + ext[parts, x, y + 1])
            diagonal = 0.002 + west + east + south + north + low + high
            inverse = jnp.where(m > 0, 1.0, 0.0) / diagonal
            if j == 0 or j == cross - 1:
                inverse = inverse * inside
            at = i * cross + j
            weights[at, 0] = scale_all * inverse
            weights[at, WEST] = inverse * west
            weights[at, EAST] = inverse * east
            weights[at, SOUTH] = inverse * south
            weights[at, NORTH] = inverse * north
            weights[at, LOW] = jnp.where(z > 0, inverse * low, 0.0)
            weights[at, HIGH_Z] = jnp.where(z < length - 1, inverse * high, 0.0)
            weights[at, 7] = diagonal
        return carry

    lax.fori_loop(0, depth + 2, weigh, 0)

    def gram(sums, left, f, x, y):
        return tuple(
            total + left * ext[f, x, y, pl.ds(l, 1), :] for l, total in enumerate(sums)
        )

    def own_block(i, sums):
        inside_x = (
            jnp.where(i > 0, 1.0, 0.0).astype(jnp.float32),
            jnp.where(i < depth - 1, 1.0, 0.0).astype(jnp.float32),
        )
        x = i + 2
        x_low = jnp.maximum(i - 1, 0) + 2
        x_high = jnp.minimum(i + 1, depth - 1) + 2
        for y in range(2, breadth + 2):
            at = (i + 1) * cross + y - 1
            west = weights[at, WEST] * inside_x[0]
            east = weights[at, EAST] * inside_x[1]
            for f in range(parts):
                v = ext[f, x, y]
                near = west * ext[f, x_low, y] + east * ext[f, x_high, y]
                if y > 2:
                    near = near + weights[at, SOUTH] * ext[f, x, y - 1]
                if y < breadth + 1:
                    near = near + weights[at, NORTH] * ext[f, x, y + 1]
                near = near + weights[at, LOW] * pltpu.roll(v, 1, 1)
                near = near + weights[at, HIGH_Z] * pltpu.roll(v, length - 1, 1)
                own_p[f, i + 1, y - 1] = packed(near - v)
                phis[f, i, y - 2] = packed(v)
                sums = gram(sums, weights[at, 7] * (v - near), f, x, y)
        return sums

    def side_block(along, fixed_x, fixed_y, dx, dy):
        which = {(-1, 0): WEST, (1, 0): EAST, (0, -1): SOUTH, (0, 1): NORTH}[(dx, dy)]

        def one(i, sums):
            x = i + 2 if fixed_x is None else fixed_x
            y = i + 2 if fixed_y is None else fixed_y
            at = (x - 1) * cross + y - 1
            weight = weights[at, which] * weights[at, 7]
            for f in range(parts):
                sums = gram(sums, -weight * ext[f, x, y], f, x + dx, y + dy)
            return sums

        return lax.fori_loop(0, along, one, (zero,) * width)

    def put(row, totals, at):
        for l in range(width):
            row = row + placed(totals[l], at + l)
        return row

    row = put(row, lax.fori_loop(0, depth, own_block, (zero,) * width), index_y * width)
    arrived(8, 12)
    row = put(row, side_block(depth, None, 2, 0, -1), (index_y - 1) * width)
    row = put(row, side_block(depth, None, breadth + 1, 0, 1), (index_y + 1) * width)
    row = put(row, side_block(breadth, 2, None, -1, 0), size + index_y * width)
    row = put(row, side_block(breadth, depth + 1, None, 1, 0), 2 * size + index_y * width)
    panel[...] = row
    gathered[me] = row

    def send(g, h):
        pltpu.make_async_remote_copy(
            src_ref=panel,
            dst_ref=gathered.at[me],
            send_sem=panel_send,
            recv_sem=panel_recv,
            device_id=(g, h),
            device_id_type=MESH,
        ).start()

    each_other(send)
    for part in range(parts):
        for way in range(4):
            pl.when(can(*ways[way]))(res_copy(way, part).start)

    def no_halo(way):
        dx, dy = ways[way]

        def wipe_x():
            hx[way] = jnp.zeros(hx.shape[1:], jnp.float32)

        def wipe_y():
            hy[way - 2] = jnp.zeros(hy.shape[1:], jnp.float32)

        pl.when(jnp.logical_not(can(dx, dy)))(wipe_x if dx else wipe_y)

    for way in range(4):
        no_halo(way)

    def multiples(i, carry):
        for j in range(cross):
            at = i * cross + j
            for q in range(WEST, HIGH_Z + 1):
                w = weights[at, q]
                for n, rate in enumerate(rates):
                    hweights[n, at, q - 1] = rate * w
        return carry

    lax.fori_loop(0, depth + 2, multiples, 0)

    def reach(f, at, which, x, y):
        return packed(weights[at, which] * ext[f, x, y])

    def seams_x(i, carry):
        y = i + 2
        for f in range(parts):
            side_x[f, 1, i + 1] = reach(f, cross + i + 1, WEST, 1, y)
            side_x[f, 2, i + 1] = reach(f, depth * cross + i + 1, EAST, depth + 2, y)
            own_p[f, 0, i + 1] = reach(f, i + 1, EAST, 2, y)
            own_p[f, depth + 1, i + 1] = reach(f, (depth + 1) * cross + i + 1, WEST, depth + 1, y)
        return carry

    def seams_y(i, carry):
        x = i + 2
        at = (i + 1) * cross
        for f in range(parts):
            side_y[f, i, 1] = reach(f, at + 1, SOUTH, x, 1)
            side_y[f, i, 2] = reach(f, at + breadth, NORTH, x, breadth + 2)
            own_p[f, i + 1, 0] = reach(f, at, NORTH, x, 2)
            own_p[f, i + 1, breadth + 1] = reach(f, at + breadth + 1, SOUTH, x, breadth + 1)
        return carry

    lax.fori_loop(0, breadth, seams_x, 0)
    lax.fori_loop(0, depth, seams_y, 0)

    for buffer in (first, second, third):
        def clear_row(y, carry, buffer=buffer):
            buffer[y] = tall
            buffer[(depth + 3) * wide + y] = tall
            return carry

        def clear_column(x, carry, buffer=buffer):
            buffer[x * wide] = tall
            buffer[x * wide + wide - 1] = tall
            return carry

        lax.fori_loop(0, wide, clear_row, 0)
        lax.fori_loop(0, depth + 4, clear_column, 0)
    for x in (1, depth + 2):
        for y in (1, breadth + 2):
            first[x * wide + y] = tall

    arrived(12, 16)
    for f in range(parts):
        for slot, at_low, at_high, way, x in (
            (0, 1, breadth, None, 1), (1, cross, cross + breadth + 1, WEST, 1),
            (2, depth * cross, depth * cross + breadth + 1, EAST, depth + 2),
            (3, (depth + 1) * cross + 1, (depth + 1) * cross + breadth, None, depth + 2),
        ):
            side_x[f, slot, 0] = reach(f, at_low, way or SOUTH, x, 1)
            side_x[f, slot, breadth + 1] = reach(f, at_high, way or NORTH, x, breadth + 2)

    def bounds(i, last):
        return (
            jnp.where(i > 0, 1.0, 0.0).astype(jnp.float32),
            jnp.where(i < last, 1.0, 0.0).astype(jnp.float32),
        )

    def halo_term(f, at, x, y, terms):
        v = ext[f, x, y]
        near = weights[at, LOW] * pltpu.roll(v, 1, 1)
        near = near + weights[at, HIGH_Z] * pltpu.roll(v, length - 1, 1)
        for weight, px, py in terms:
            near = near + weight * ext[f, px, py]
        return packed(near - v)

    def rims_x(i, carry):
        y = i + 2
        low, high = bounds(i, breadth - 1)
        for slot, x, outward, px in ((0, 1, WEST, 0), (3, depth + 2, EAST, depth + 3)):
            at = (x - 1) * cross + i + 1
            terms = (
                (weights[at, outward], px, y),
                (weights[at, SOUTH] * low, x, y - 1),
                (weights[at, NORTH] * high, x, y + 1),
            )
            for f in range(parts):
                side_x[f, slot, i + 1] = halo_term(f, at, x, y, terms)
        return carry

    def rims_y(i, carry):
        x = i + 2
        low, high = bounds(i, depth - 1)
        for slot, y, outward, py in ((0, 1, SOUTH, 0), (3, breadth + 2, NORTH, breadth + 3)):
            at = (i + 1) * cross + y - 1
            terms = (
                (weights[at, outward], x, py),
                (weights[at, WEST] * low, x - 1, y),
                (weights[at, EAST] * high, x + 1, y),
            )
            for f in range(parts):
                side_y[f, i, slot] = halo_term(f, at, x, y, terms)
        return carry

    lax.fori_loop(0, breadth, rims_x, 0)
    lax.fori_loop(0, depth, rims_y, 0)

    everyone = gathered.at[pl.ds(0, count - 1)]
    panels_all = pltpu.make_async_remote_copy(
        src_ref=everyone,
        dst_ref=everyone,
        send_sem=panel_send,
        recv_sem=panel_recv,
        device_id=(lax.rem(index_x + 1, count_x), index_y),
        device_id_type=MESH,
    )
    panels_all.wait_recv()
    panels = [gathered[pl.ds(g * count_y, count_y)].reshape(size, panel.shape[1]) for g in range(count_x)]
    for g, x in enumerate(cyclic_solve(panels, size)):
        coeffs[pl.ds(g * size, size), :] = x
    mine[...] = coeffs[pl.ds(pl.multiple_of(me * width, width), width), :]

    for slot in range(10):
        step_x, step_y = (slot // 3 - 1, slot % 3 - 1) if slot < 9 else (0, 0)
        near_x = jnp.clip(index_x + step_x, 0, count_x - 1)
        near_y = jnp.clip(index_y + step_y, 0, count_y - 1)
        begin = pl.multiple_of((near_x * count_y + near_y) * width, width)
        c = coeffs[pl.ds(begin, width), :]
        if slot < 9:
            c = scale_all * c
        coarse = c.astype(jnp.bfloat16).astype(jnp.float32)
        fine = c - coarse
        lhs[slot] = jnp.concatenate([coarse, coarse, fine, fine], axis=0).T.astype(jnp.bfloat16)

    def combine(slot, cells):
        block = jnp.concatenate(cells, axis=1)
        return jnp.dot(
            lhs[slot], jnp.concatenate([block, block], axis=0), preferred_element_type=jnp.float32
        )

    def cut(block, i):
        return block[:, i * length : (i + 1) * length]

    def spread(w):
        return jnp.concatenate([w] * (rhs // width), axis=0)

    def beside(source, n, x, y):
        cell = x * wide + y
        at = (x - 1) * cross + y - 1
        centre = source[cell]
        total = spread(hweights[n, at, 4]) * pltpu.roll(centre, 1, 1)
        total = total + spread(hweights[n, at, 5]) * pltpu.roll(centre, length - 1, 1)
        total = total + spread(hweights[n, at, 0]) * source[cell - wide]
        total = total + spread(hweights[n, at, 1]) * source[cell + wide]
        total = total + spread(hweights[n, at, 2]) * source[cell - 1]
        total = total + spread(hweights[n, at, 3]) * source[cell + 1]
        return total

    def component(part, carry):
        for way in range(4):
            dx, dy = ways[way]
            pl.when(can(-dx, -dy))(res_copy(way, part).wait_recv)

        def force_row(i, carry):
            own = combine(4, [own_p[part, i + 1, j] for j in range(cross)])
            south = combine(3, [side_y[part, i, j] for j in (0, 1)])
            north = combine(5, [side_y[part, i, j] for j in (2, 3)])
            tiles = rows_of(rbuf.at[part * depth + i])
            for j in range(cross):
                value = cut(own, j)
                if j < 2:
                    value = value + cut(south, j)
                if j >= breadth:
                    value = value + cut(north, j - breadth)
                if j == 0 or j == cross - 1:
                    loaded = hy[j // breadth, part, i]
                else:
                    loaded = tiles[pl.ds(j - 1, rhs, stride=breadth), :]
                first[(i + 2) * wide + j + 1] = spread(weights[(i + 1) * cross + j, 0]) * loaded + value
            return carry

        lax.fori_loop(0, depth, force_row, 0)
        for side in range(2):
            x, block = side * (depth - 1) + 2, 6 * side
            edge = 1 + side
            corner = [combine(block + 2 * end, [side_x[part, edge, end * (breadth + 1)]]) for end in range(2)]
            middle = combine(block + 1, [side_x[part, edge, j + 1] for j in range(breadth)])
            for j in range(cross):
                if j == 0 or j == cross - 1:
                    value = corner[j // breadth]
                else:
                    value = cut(middle, j - 1)
                cell = x * wide + j + 1
                first[cell] = first[cell] + value
            x, edge = side * (depth + 1) + 1, 3 * side
            corner = [combine(block + 2 * end, [side_x[part, edge, end * (breadth + 1)]]) for end in range(2)]
            middle = combine(block + 1, [side_x[part, edge, j + 1] for j in range(breadth)])
            own = combine(4, [own_p[part, x - 1, j + 1] for j in range(breadth)])
            tiles = rows_of(hx.at[side, part])
            for j in range(breadth):
                value = cut(middle, j) + cut(own, j)
                if j == 0:
                    value = value + corner[0]
                if j == breadth - 1:
                    value = value + corner[1]
                loaded = tiles[pl.ds(j, rhs, stride=breadth), :]
                first[x * wide + j + 2] = spread(weights[(x - 1) * cross + j + 1, 0]) * loaded + value

        source, target, spare = first, second, third
        for n in range(len(rates) - 1):
            def relax(i, carry, source=source, target=target, n=n):
                for j in range(cross):
                    cell = (i + 1) * wide + j + 1
                    target[cell] = first[cell] + beside(source, n, i + 1, j + 1)
                return carry

            lax.fori_loop(0, depth + 2, relax, 0)
            source, target, spare = target, spare, target

        def finish(i, carry):
            fine = combine(9, [phis[part, i, j] for j in range(breadth)])
            tiles = rows_of(obuf.at[part * depth + i])
            for j in range(breadth):
                value = cut(fine, j) + first[(i + 2) * wide + j + 2]
                value = value + beside(source, len(rates) - 1, i + 2, j + 2)
                tiles[pl.ds(j, rhs, stride=breadth), :] = value
            pltpu.make_async_copy(obuf.at[part * depth + i], out.at[:, part, i], out_sem).start()
            return carry

        lax.fori_loop(0, depth, finish, 0)
        return carry

    lax.fori_loop(0, parts, component, 0)
    panels_all.wait_send()
    for sends, _, copy in started:
        pl.when(sends)(copy.wait_send)
    for part in range(parts):
        for way in range(4):
            pl.when(can(*ways[way]))(res_copy(way, part).wait_send)
    pltpu.make_async_copy(obuf, obuf, out_sem).wait()


def on_device(residuals, vectors, phases, stiffness):
    count_x = lax.axis_size("gx")
    count_y = lax.axis_size("yz")
    rhs, parts, depth, breadth, length = residuals.shape
    width = vectors.shape[0]
    count = count_x * count_y
    scale_all, rates = sweep_rates(SWEEPS, 0.8)
    vmem = pl.BlockSpec(memory_space=pltpu.VMEM)
    hbm = pl.BlockSpec(memory_space=pl.ANY)
    panel = (width, 3 * count_y * width + rhs)
    cells = (depth + 2) * (breadth + 2)
    field = pltpu.VMEM(((depth + 4) * (breadth + 4), rhs, length), jnp.float32)
    slots = 16 + 4 * parts
    f32, half = jnp.float32, jnp.bfloat16
    return pl.pallas_call(
        functools.partial(kernel, count_x, count_y, scale_all, rates),
        out_shape=(
            jax.ShapeDtypeStruct((width, rhs), f32),
            jax.ShapeDtypeStruct(residuals.shape, f32),
        ),
        in_specs=[pl.BlockSpec(memory_space=pltpu.SMEM), vmem, hbm, hbm],
        out_specs=(vmem, hbm),
        scratch_shapes=[
            pltpu.VMEM((parts + 1, depth + 4, breadth + 4, width, length), f32),
            pltpu.VMEM((parts * depth, width, breadth, length), f32),
            pltpu.VMEM((parts * depth, rhs, breadth, length), f32),
            pltpu.VMEM((2, parts, rhs, breadth, length), f32),
            pltpu.VMEM((2, parts, depth, rhs, length), f32),
            pltpu.VMEM((2, parts, depth, rhs, length), f32),
            pltpu.VMEM((parts * depth, rhs, breadth, length), f32),
            pltpu.VMEM((depth * breadth, length), f32),
            pltpu.VMEM((2, 2, depth, length), f32),
            pltpu.VMEM((2, 2 * breadth, length), f32),
            pltpu.VMEM((2, 2, depth, length), f32),
            pltpu.VMEM((cells, 8, width, length), f32),
            pltpu.VMEM((SWEEPS - 1, cells, 6, width, length), f32),
            pltpu.VMEM((parts, depth + 2, breadth + 2, 2 * width, length), half),
            pltpu.VMEM((parts, depth, 4, 2 * width, length), half),
            pltpu.VMEM((parts, 4, breadth + 2, 2 * width, length), half),
            pltpu.VMEM((parts, depth, breadth, 2 * width, length), half),
            pltpu.VMEM((10, rhs, 4 * width), half),
            pltpu.VMEM(panel, f32),
            pltpu.VMEM((count,) + panel, f32),
            pltpu.VMEM((count * width, rhs), f32),
            field, field, field,
            pltpu.SemaphoreType.DMA,
            pltpu.SemaphoreType.DMA,
            pltpu.SemaphoreType.DMA,
            pltpu.SemaphoreType.DMA,
            pltpu.SemaphoreType.DMA,
            pltpu.SemaphoreType.DMA((slots,)),
            pltpu.SemaphoreType.DMA((slots,)),
        ],
        compiler_params=pltpu.CompilerParams(
            collective_id=0, has_side_effects=True, vmem_limit_bytes=60 * 1024 * 1024
        ),
    )(stiffness, phases, vectors, residuals)


def solution(mesh):
    return jax.shard_map(
        on_device,
        mesh=mesh,
        in_specs=(
            P(None, None, "gx", "yz", None),
            P(None, None, "gx", "yz", None),
            P("gx", "yz", None),
            P(),
        ),
        out_specs=(P(("gx", "yz"), None), P(None, None, "gx", "yz", None)),
        check_vma=False,
    )
```

```python
import functools

import jax
import jax.numpy as jnp
from jax import lax
from jax.experimental import pallas as pl
from jax.experimental.pallas import tpu as pltpu
from jax.sharding import PartitionSpec as P

SWEEPS = 4


HIGH = lax.Precision.HIGHEST


MESH = pl.DeviceIdType.MESH


def eliminate(rows, size):
    sublane = lax.broadcasted_iota(jnp.int32, rows[0].shape, 0)
    for p in range(size):
        reduced = []
        for a in rows:
            column = jnp.broadcast_to(a[:, p : p + 1], a.shape)
            pivot = a[p : p + 1, :] / column[p : p + 1, :]
            reduced.append(jnp.where(sublane == p, pivot, a - column * pivot))
        rows = reduced
    return rows


def product(a, b):
    return jnp.dot(a, b, precision=HIGH, preferred_element_type=jnp.float32)


def cyclic_solve(rows, size):
    count = len(rows)
    width = rows[0].shape[1]
    lane = lax.broadcasted_iota(jnp.int32, rows[0].shape, 1)
    is_own = lane < size
    is_low = (lane >= size) & (lane < 2 * size)
    is_high = (lane >= 2 * size) & (lane < 3 * size)
    is_rhs = lane >= 3 * size
    live = list(range(count))
    system = dict(enumerate(rows))
    levels = []
    while len(live) > 1:
        out = live[1::2]
        kept = live[0::2]
        solved = dict(zip(out, eliminate([system[i] for i in out], size)))
        fresh = {}
        for place, i in enumerate(kept):
            a = system[i]
            total = jnp.where(is_own | is_rhs, a, 0.0)
            if place > 0:
                t = product(a[:, size : 2 * size], solved[out[place - 1]])
                shifted = pltpu.roll(t, width - 2 * size, 1)
                total = total - jnp.where(is_own, shifted, jnp.where(is_low | is_rhs, t, 0.0))
            if place < len(out):
                t = product(a[:, 2 * size : 3 * size], solved[out[place]])
                shifted = pltpu.roll(t, width - size, 1)
                total = total - jnp.where(is_own, shifted, jnp.where(is_high | is_rhs, t, 0.0))
            fresh[i] = total
        levels.append((live, out, solved))
        system = fresh
        live = kept
    last = eliminate([system[live[0]]], size)[0]
    answer = {live[0]: last[:, 3 * size :]}
    for before, out, solved in reversed(levels):
        for i in out:
            a = solved[i]
            place = before.index(i)
            x = a[:, 3 * size :] - product(a[:, size : 2 * size], answer[before[place - 1]])
            if place + 1 < len(before):
                x = x - product(a[:, 2 * size : 3 * size], answer[before[place + 1]])
            answer[i] = x
    return [answer[i] for i in range(count)]


WEST, EAST, SOUTH, NORTH, LOW, HIGH_Z = range(1, 7)


def sweep_rates(sweeps, damping):
    powers = [0.0] * sweeps
    term = [1.0]
    for _ in range(sweeps):
        for i, value in enumerate(term):
            powers[i] += value
        longer = [0.0] * (len(term) + 1)
        for i, value in enumerate(term):
            longer[i] += (1.0 - damping) * value
            longer[i + 1] += damping * value
        term = longer
    return damping * powers[0], [powers[i] / powers[i - 1] for i in range(sweeps - 1, 0, -1)]


def packed(v):
    coarse = v.astype(jnp.bfloat16).astype(jnp.float32)
    return jnp.concatenate([coarse, v - coarse], axis=0).astype(jnp.bfloat16)


def kernel(
    count_x, count_y, scale_all, rates,
    stiffness, phases, vectors, res,
    mine, out,
    ext, vraw, rbuf, hx, hy, ybuf, obuf, mown, msend, mx, my,
    weights, hweights, own_p, side_y, side_x, phis, lhs,
    panel, gathered, coeffs, first, second, third,
    load_sem, res_sem, out_sem, panel_send, panel_recv, halo_send, halo_recv
):
    index_x = lax.axis_index("gx")
    index_y = lax.axis_index("yz")
    count = count_x * count_y
    me = index_x * count_y + index_y
    rhs, parts, depth, breadth, length = res.shape
    width = vectors.shape[0]
    levels = stiffness.shape[0]
    wide = breadth + 4
    cross = breadth + 2
    barrier = pltpu.get_barrier_semaphore()
    zero = jnp.zeros((width, length), jnp.float32)
    tall = jnp.zeros((rhs, length), jnp.float32)

    def rows_of(ref):
        return ref.reshape(ref.shape[0] * breadth, length)

    def load(i, carry):
        c = i // depth
        x = i - c * depth
        pltpu.make_async_copy(vectors.at[:, c, x], vraw.at[i], load_sem).start()
        return carry

    lax.fori_loop(0, parts * depth, load, 0)

    def clear_y(y, carry):
        for f in range(parts + 1):
            for x in (0, 1, depth + 2, depth + 3):
                ext[f, x, y] = zero
        return carry

    def clear_x(x, carry):
        for f in range(parts + 1):
            for y in (0, 1, breadth + 2, breadth + 3):
                ext[f, x + 2, y] = zero
        return carry

    lax.fori_loop(0, wide, clear_y, 0)
    lax.fori_loop(0, depth, clear_x, 0)
    mx[...] = jnp.zeros(mx.shape, jnp.float32)
    my[...] = jnp.zeros(my.shape, jnp.float32)

    def each_other(act):
        def along(g, carry):
            for h in range(count_y):
                pl.when(jnp.logical_or(g != index_x, h != index_y))(functools.partial(act, g, h))
            return carry

        lax.fori_loop(0, count_x, along, 0)

    def greet(g, h):
        pl.semaphore_signal(barrier, inc=1, device_id=(g, h), device_id_type=MESH)

    each_other(greet)

    def load_res(i, carry):
        c = i // depth
        x = i - c * depth
        pltpu.make_async_copy(res.at[:, c, x], rbuf.at[i], res_sem).start()
        return carry

    lax.fori_loop(0, parts * depth, load_res, 0)

    for x in range(depth):
        p = phases[x]
        m = jnp.zeros(p.shape, jnp.float32)
        for level in range(levels):
            m = jnp.where(p == level, stiffness[level], m)
        mown[pl.ds(x * breadth, breadth), :] = m
    for side in range(2):
        for layer in range(2):
            y = layer + side * (breadth - 2)
            msend[side, layer] = mown[pl.ds(y, depth, stride=breadth), :]

    def spread_own(x, carry):
        for y in range(breadth):
            row = mown[pl.ds(x * breadth + y, 1), :]
            ext[parts, x + 2, y + 2] = jnp.broadcast_to(row, (width, length))
        return carry

    lax.fori_loop(0, depth, spread_own, 0)
    pltpu.make_async_copy(vraw, vraw, load_sem).wait()

    def fill(i, carry):
        c = i // depth
        x = i - c * depth
        tiles = rows_of(vraw.at[i])
        for y in range(breadth):
            ext[c, x + 2, y + 2] = tiles[pl.ds(y, width, stride=breadth), :]
        return carry

    lax.fori_loop(0, parts * depth, fill, 0)
    pl.semaphore_wait(barrier, count - 1)

    def can(dx, dy):
        ok = index_x >= 0
        if dx:
            ok = index_x > 0 if dx < 0 else index_x < count_x - 1
        if dy:
            ok_y = index_y > 0 if dy < 0 else index_y < count_y - 1
            ok = jnp.logical_and(ok, ok_y) if dx else ok_y
        return ok

    def exchange(source, target, dx, dy, slot):
        return pltpu.make_async_remote_copy(
            src_ref=source,
            dst_ref=target,
            send_sem=halo_send.at[slot],
            recv_sem=halo_recv.at[slot],
            device_id=(index_x + dx, index_y + dy),
            device_id_type=MESH,
        )

    started = []

    def start(source, target, dx, dy):
        copy = exchange(source, target, dx, dy, len(started))
        pl.when(can(dx, dy))(copy.start)
        started.append((can(dx, dy), can(-dx, -dy), copy))

    def arrived(low, high):
        for _, receives, copy in started[low:high]:
            pl.when(receives)(copy.wait_recv)

    start(mown.at[pl.ds(0, 2 * breadth)], mx.at[1], -1, 0)
    start(mown.at[pl.ds((depth - 2) * breadth, 2 * breadth)], mx.at[0], 1, 0)
    start(msend.at[0], my.at[1], 0, -1)
    start(msend.at[1], my.at[0], 0, 1)

    field = pl.ds(0, parts)
    inner_x, inner_y = pl.ds(2, depth), pl.ds(2, breadth)

    def layer(step):
        start(ext.at[field, 2 + step, inner_y], ext.at[field, depth + 2 + step, inner_y], -1, 0)
        start(ext.at[field, depth + 1 - step, inner_y], ext.at[field, 1 - step, inner_y], 1, 0)
        start(ext.at[field, inner_x, 2 + step], ext.at[field, inner_x, breadth + 2 + step], 0, -1)
        start(ext.at[field, inner_x, breadth + 1 - step], ext.at[field, inner_x, 1 - step], 0, 1)

    for x, dx, to_x in ((2, -1, depth + 2), (depth + 1, 1, 1)):
        for y, dy, to_y in ((2, -1, breadth + 2), (breadth + 1, 1, 1)):
            start(ext.at[:, x, y], ext.at[:, to_x, to_y], dx, dy)
    layer(0)

    base_slot = len(started) + 4
    ways = ((-1, 0), (1, 0), (0, -1), (0, 1))

    def res_copy(way, part):
        dx, dy = ways[way]
        if dx:
            source, target = res.at[:, part, 0 if dx < 0 else depth - 1], hx.at[1 - way, part]
        else:
            source, target = ybuf.at[way - 2, part], hy.at[3 - way, part]
        return exchange(source, target, dx, dy, base_slot + part * 4 + way)

    pltpu.make_async_copy(rbuf, rbuf, res_sem).wait()

    def loads(i, sums):
        f = i // depth
        x = i - f * depth
        tiles = rows_of(rbuf.at[i])
        for side in range(2):
            ybuf[side, f, x] = tiles[pl.ds(side * (breadth - 1), rhs, stride=breadth), :]
        for y in range(breadth):
            v = ext[f, x + 2, y + 2]
            sums = tuple(
                total + v * tiles[pl.ds(r * breadth + y, 1), :] for r, total in enumerate(sums)
            )
        return sums

    sums = lax.fori_loop(0, parts * depth, loads, (zero,) * rhs)
    lane = lax.broadcasted_iota(jnp.int32, panel.shape, 1)

    def placed(total, at):
        return jnp.where(lane == at, jnp.sum(total, axis=1, keepdims=True), 0.0)

    size = count_y * width
    row = jnp.zeros(panel.shape, jnp.float32)
    for r in range(rhs):
        row = row + placed(sums[r], 3 * size + r)

    arrived(0, 4)

    def spread_x(y, carry):
        for side in range(2):
            for step in range(2):
                line = mx[side, pl.ds(step * breadth + y, 1), :]
                ext[parts, side * (depth + 2) + step, y + 2] = jnp.broadcast_to(line, (width, length))
        return carry

    def spread_y(x, carry):
        for side in range(2):
            for step in range(2):
                line = my[side, step, pl.ds(x, 1), :]
                ext[parts, x + 2, side * (breadth + 2) + step] = jnp.broadcast_to(line, (width, length))
        return carry

    lax.fori_loop(0, breadth, spread_x, 0)
    lax.fori_loop(0, depth, spread_y, 0)
    arrived(4, 8)
    z = lax.broadcasted_iota(jnp.int32, (width, length), 1)

    def weigh(i, carry):
        inside = jnp.where(jnp.logical_or(i == 0, i == depth + 1), 0.0, 1.0).astype(jnp.float32)
        for j in range(cross):
            x, y = i + 1, j + 1
            m = ext[parts, x, y]
            low = 0.5 * (m + jnp.where(z > 0, pltpu.roll(m, 1, 1), 0.0))
            high = 0.5 * (m + jnp.where(z < length - 1, pltpu.roll(m, length - 1, 1), 0.0))
            west = 0.5 * (m + ext[parts, x - 1, y])
            east = 0.5 * (m + ext[parts, x + 1, y])
            south = 0.5 * (m + ext[parts, x, y - 1])
            north = 0.5 * (m + ext[parts, x, y + 1])
            diagonal = 0.002 + west + east + south + north + low + high
            inverse = jnp.where(m > 0, 1.0, 0.0) / diagonal
            if j == 0 or j == cross - 1:
                inverse = inverse * inside
            at = i * cross + j
            weights[at, 0] = scale_all * inverse
            weights[at, WEST] = inverse * west
            weights[at, EAST] = inverse * east
            weights[at, SOUTH] = inverse * south
            weights[at, NORTH] = inverse * north
            weights[at, LOW] = jnp.where(z > 0, inverse * low, 0.0)
            weights[at, HIGH_Z] = jnp.where(z < length - 1, inverse * high, 0.0)
            weights[at, 7] = diagonal
        return carry

    lax.fori_loop(0, depth + 2, weigh, 0)

    def gram(sums, left, f, x, y):
        return tuple(
            total + left * ext[f, x, y, pl.ds(l, 1), :] for l, total in enumerate(sums)
        )

    def own_block(i, sums):
        inside_x = (
            jnp.where(i > 0, 1.0, 0.0).astype(jnp.float32),
            jnp.where(i < depth - 1, 1.0, 0.0).astype(jnp.float32),
        )
        x = i + 2
        x_low = jnp.maximum(i - 1, 0) + 2
        x_high = jnp.minimum(i + 1, depth - 1) + 2
        for y in range(2, breadth + 2):
            at = (i + 1) * cross + y - 1
            west = weights[at, WEST] * inside_x[0]
            east = weights[at, EAST] * inside_x[1]
            for f in range(parts):
                v = ext[f, x, y]
                near = west * ext[f, x_low, y] + east * ext[f, x_high, y]
                if y > 2:
                    near = near + weights[at, SOUTH] * ext[f, x, y - 1]
                if y < breadth + 1:
                    near = near + weights[at, NORTH] * ext[f, x, y + 1]
                near = near + weights[at, LOW] * pltpu.roll(v, 1, 1)
                near = near + weights[at, HIGH_Z] * pltpu.roll(v, length - 1, 1)
                own_p[f, i + 1, y - 1] = packed(near - v)
                phis[f, i, y - 2] = packed(v)
                sums = gram(sums, weights[at, 7] * (v - near), f, x, y)
        return sums

    def side_block(along, fixed_x, fixed_y, dx, dy):
        which = {(-1, 0): WEST, (1, 0): EAST, (0, -1): SOUTH, (0, 1): NORTH}[(dx, dy)]

        def one(i, sums):
            x = i + 2 if fixed_x is None else fixed_x
            y = i + 2 if fixed_y is None else fixed_y
            at = (x - 1) * cross + y - 1
            weight = weights[at, which] * weights[at, 7]
            for f in range(parts):
                sums = gram(sums, -weight * ext[f, x, y], f, x + dx, y + dy)
            return sums

        return lax.fori_loop(0, along, one, (zero,) * width)

    def put(row, totals, at):
        for l in range(width):
            row = row + placed(totals[l], at + l)
        return row

    row = put(row, lax.fori_loop(0, depth, own_block, (zero,) * width), index_y * width)
    arrived(8, 12)
    row = put(row, side_block(depth, None, 2, 0, -1), (index_y - 1) * width)
    row = put(row, side_block(depth, None, breadth + 1, 0, 1), (index_y + 1) * width)
    row = put(row, side_block(breadth, 2, None, -1, 0), size + index_y * width)
    row = put(row, side_block(breadth, depth + 1, None, 1, 0), 2 * size + index_y * width)
    panel[...] = row
    gathered[me] = row

    def send(g, h):
        pltpu.make_async_remote_copy(
            src_ref=panel,
            dst_ref=gathered.at[me],
            send_sem=panel_send,
            recv_sem=panel_recv,
            device_id=(g, h),
            device_id_type=MESH,
        ).start()

    each_other(send)
    layer(1)
    for part in range(parts):
        for way in range(4):
            pl.when(can(*ways[way]))(res_copy(way, part).start)

    def no_halo(way):
        dx, dy = ways[way]

        def wipe_x():
            hx[way] = jnp.zeros(hx.shape[1:], jnp.float32)

        def wipe_y():
            hy[way - 2] = jnp.zeros(hy.shape[1:], jnp.float32)

        pl.when(jnp.logical_not(can(dx, dy)))(wipe_x if dx else wipe_y)

    for way in range(4):
        no_halo(way)

    def multiples(i, carry):
        for j in range(cross):
            at = i * cross + j
            for q in range(WEST, HIGH_Z + 1):
                w = weights[at, q]
                for n, rate in enumerate(rates):
                    hweights[n, at, q - 1] = rate * w
        return carry

    lax.fori_loop(0, depth + 2, multiples, 0)

    def reach(f, at, which, x, y):
        return packed(weights[at, which] * ext[f, x, y])

    def seams_x(i, carry):
        y = i + 2
        for f in range(parts):
            side_x[f, 1, i + 1] = reach(f, cross + i + 1, WEST, 1, y)
            side_x[f, 2, i + 1] = reach(f, depth * cross + i + 1, EAST, depth + 2, y)
            own_p[f, 0, i + 1] = reach(f, i + 1, EAST, 2, y)
            own_p[f, depth + 1, i + 1] = reach(f, (depth + 1) * cross + i + 1, WEST, depth + 1, y)
        return carry

    def seams_y(i, carry):
        x = i + 2
        at = (i + 1) * cross
        for f in range(parts):
            side_y[f, i, 1] = reach(f, at + 1, SOUTH, x, 1)
            side_y[f, i, 2] = reach(f, at + breadth, NORTH, x, breadth + 2)
            own_p[f, i + 1, 0] = reach(f, at, NORTH, x, 2)
            own_p[f, i + 1, breadth + 1] = reach(f, at + breadth + 1, SOUTH, x, breadth + 1)
        return carry

    lax.fori_loop(0, breadth, seams_x, 0)
    lax.fori_loop(0, depth, seams_y, 0)

    for buffer in (first, second, third):
        def clear_row(y, carry, buffer=buffer):
            buffer[y] = tall
            buffer[(depth + 3) * wide + y] = tall
            return carry

        def clear_column(x, carry, buffer=buffer):
            buffer[x * wide] = tall
            buffer[x * wide + wide - 1] = tall
            return carry

        lax.fori_loop(0, wide, clear_row, 0)
        lax.fori_loop(0, depth + 4, clear_column, 0)
    for x in (1, depth + 2):
        for y in (1, breadth + 2):
            first[x * wide + y] = tall

    arrived(12, 16)
    for f in range(parts):
        for slot, at_low, at_high, way, x in (
            (0, 1, breadth, None, 1), (1, cross, cross + breadth + 1, WEST, 1),
            (2, depth * cross, depth * cross + breadth + 1, EAST, depth + 2),
            (3, (depth + 1) * cross + 1, (depth + 1) * cross + breadth, None, depth + 2),
        ):
            side_x[f, slot, 0] = reach(f, at_low, way or SOUTH, x, 1)
            side_x[f, slot, breadth + 1] = reach(f, at_high, way or NORTH, x, breadth + 2)

    def bounds(i, last):
        return (
            jnp.where(i > 0, 1.0, 0.0).astype(jnp.float32),
            jnp.where(i < last, 1.0, 0.0).astype(jnp.float32),
        )

    def halo_term(f, at, x, y, terms):
        v = ext[f, x, y]
        near = weights[at, LOW] * pltpu.roll(v, 1, 1)
        near = near + weights[at, HIGH_Z] * pltpu.roll(v, length - 1, 1)
        for weight, px, py in terms:
            near = near + weight * ext[f, px, py]
        return packed(near - v)

    def rims_x(i, carry):
        y = i + 2
        low, high = bounds(i, breadth - 1)
        for slot, x, outward, px in ((0, 1, WEST, 0), (3, depth + 2, EAST, depth + 3)):
            at = (x - 1) * cross + i + 1
            terms = (
                (weights[at, outward], px, y),
                (weights[at, SOUTH] * low, x, y - 1),
                (weights[at, NORTH] * high, x, y + 1),
            )
            for f in range(parts):
                side_x[f, slot, i + 1] = halo_term(f, at, x, y, terms)
        return carry

    def rims_y(i, carry):
        x = i + 2
        low, high = bounds(i, depth - 1)
        for slot, y, outward, py in ((0, 1, SOUTH, 0), (3, breadth + 2, NORTH, breadth + 3)):
            at = (i + 1) * cross + y - 1
            terms = (
                (weights[at, outward], x, py),
                (weights[at, WEST] * low, x - 1, y),
                (weights[at, EAST] * high, x + 1, y),
            )
            for f in range(parts):
                side_y[f, i, slot] = halo_term(f, at, x, y, terms)
        return carry

    lax.fori_loop(0, breadth, rims_x, 0)
    lax.fori_loop(0, depth, rims_y, 0)

    everyone = gathered.at[pl.ds(0, count - 1)]
    panels_all = pltpu.make_async_remote_copy(
        src_ref=everyone,
        dst_ref=everyone,
        send_sem=panel_send,
        recv_sem=panel_recv,
        device_id=(lax.rem(index_x + 1, count_x), index_y),
        device_id_type=MESH,
    )
    panels_all.wait_recv()
    panels = [gathered[pl.ds(g * count_y, count_y)].reshape(size, panel.shape[1]) for g in range(count_x)]
    for g, x in enumerate(cyclic_solve(panels, size)):
        coeffs[pl.ds(g * size, size), :] = x
    mine[...] = coeffs[pl.ds(pl.multiple_of(me * width, width), width), :]

    for slot in range(10):
        step_x, step_y = (slot // 3 - 1, slot % 3 - 1) if slot < 9 else (0, 0)
        near_x = jnp.clip(index_x + step_x, 0, count_x - 1)
        near_y = jnp.clip(index_y + step_y, 0, count_y - 1)
        begin = pl.multiple_of((near_x * count_y + near_y) * width, width)
        c = coeffs[pl.ds(begin, width), :]
        if slot < 9:
            c = scale_all * c
        coarse = c.astype(jnp.bfloat16).astype(jnp.float32)
        fine = c - coarse
        lhs[slot] = jnp.concatenate([coarse, coarse, fine, fine], axis=0).T.astype(jnp.bfloat16)

    def combine(slot, cells):
        block = jnp.concatenate(cells, axis=1)
        return jnp.dot(
            lhs[slot], jnp.concatenate([block, block], axis=0), preferred_element_type=jnp.float32
        )

    def cut(block, i):
        return block[:, i * length : (i + 1) * length]

    def spread(w):
        return jnp.concatenate([w] * (rhs // width), axis=0)

    def beside(source, n, x, y):
        cell = x * wide + y
        at = (x - 1) * cross + y - 1
        centre = source[cell]
        total = spread(hweights[n, at, 0]) * source[cell - wide]
        total = total + spread(hweights[n, at, 1]) * source[cell + wide]
        total = total + spread(hweights[n, at, 2]) * source[cell - 1]
        total = total + spread(hweights[n, at, 3]) * source[cell + 1]
        total = total + spread(hweights[n, at, 4]) * pltpu.roll(centre, 1, 1)
        total = total + spread(hweights[n, at, 5]) * pltpu.roll(centre, length - 1, 1)
        return total

    def in_pairs(source, start, rows, act):
        def pair(i, carry):
            for k in range(2):
                act(start + 2 * i + k)
            return carry

        lax.fori_loop(0, rows // 2, pair, 0)

    def component(part, carry):
        for way in range(4):
            dx, dy = ways[way]
            pl.when(can(-dx, -dy))(res_copy(way, part).wait_recv)

        def force_row(i, side=None):
            own = combine(4, [own_p[part, i + 1, j] for j in range(cross)])
            south = combine(3, [side_y[part, i, j] for j in (0, 1)])
            north = combine(5, [side_y[part, i, j] for j in (2, 3)])
            tiles = rows_of(rbuf.at[part * depth + i])
            if side is not None:
                corner, middle = outer(side, 1 + side)
            for j in range(cross):
                value = cut(own, j)
                if j < 2:
                    value = value + cut(south, j)
                if j >= breadth:
                    value = value + cut(north, j - breadth)
                if j == 0 or j == cross - 1:
                    loaded = hy[j // breadth, part, i]
                else:
                    loaded = tiles[pl.ds(j - 1, rhs, stride=breadth), :]
                value = spread(weights[(i + 1) * cross + j, 0]) * loaded + value
                if side is not None:
                    value = value + (cut(middle, j - 1) if 0 < j < cross - 1 else corner[j // breadth])
                first[(i + 2) * wide + j + 1] = value

        def outer(side, edge):
            block = 6 * side
            corner = [combine(block + 2 * end, [side_x[part, edge, end * (breadth + 1)]]) for end in range(2)]
            return corner, combine(block + 1, [side_x[part, edge, j + 1] for j in range(breadth)])

        def force_inner(i, carry):
            force_row(i)
            return carry

        lax.fori_loop(1, depth - 1, force_inner, 0)
        for side in range(2):
            force_row(side * (depth - 1), side)
            x = side * (depth + 1) + 1
            corner, middle = outer(side, 3 * side)
            own = combine(4, [own_p[part, x - 1, j + 1] for j in range(breadth)])
            tiles = rows_of(hx.at[side, part])
            for j in range(breadth):
                value = cut(middle, j) + cut(own, j)
                if j == 0:
                    value = value + corner[0]
                if j == breadth - 1:
                    value = value + corner[1]
                loaded = tiles[pl.ds(j, rhs, stride=breadth), :]
                value = spread(weights[(x - 1) * cross + j + 1, 0]) * loaded + value
                first[x * wide + j + 2] = value

        source, target, spare = first, second, third
        for n in range(len(rates) - 1):
            def relax(x, source=source, target=target, n=n):
                for j in range(cross):
                    cell = x * wide + j + 1
                    target[cell] = first[cell] + beside(source, n, x, j + 1)

            in_pairs(source, 1, depth + 2, relax)
            source, target, spare = target, spare, target

        def finish(x):
            fine = combine(9, [phis[part, x - 2, j] for j in range(breadth)])
            row = part * depth + x - 2
            tiles = rows_of(obuf.at[row])
            for j in range(breadth):
                value = cut(fine, j) + first[x * wide + j + 2]
                value = value + beside(source, len(rates) - 1, x, j + 2)
                tiles[pl.ds(j, rhs, stride=breadth), :] = value
            pltpu.make_async_copy(obuf.at[row], out.at[:, part, x - 2], out_sem).start()

        in_pairs(source, 2, depth, finish)
        return carry

    lax.fori_loop(0, parts, component, 0)
    panels_all.wait_send()
    for sends, _, copy in started:
        pl.when(sends)(copy.wait_send)
    for part in range(parts):
        for way in range(4):
            pl.when(can(*ways[way]))(res_copy(way, part).wait_send)
    pltpu.make_async_copy(obuf, obuf, out_sem).wait()


def deliver_kernel(chunks, solved, field, mine, out, held, in_sem, out_sem):
    rows = held.shape[0] // chunks
    for i in range(chunks):
        part = pl.ds(i * rows, rows)
        pltpu.make_async_copy(field.at[part], held.at[part], in_sem.at[i]).start()
    mine[...] = solved[...]
    for i in range(chunks):
        part = pl.ds(i * rows, rows)
        pltpu.make_async_copy(field.at[part], held.at[part], in_sem.at[i]).wait()
        pltpu.make_async_copy(held.at[part], out.at[part], out_sem).start()
    pltpu.make_async_copy(held, out, out_sem).wait()


def deliver(solved, field):
    chunks = 8 if field.shape[0] % 8 == 0 else 1
    vmem = pl.BlockSpec(memory_space=pltpu.VMEM)
    hbm = pl.BlockSpec(memory_space=pl.ANY)
    return pl.pallas_call(
        functools.partial(deliver_kernel, chunks),
        out_shape=(
            jax.ShapeDtypeStruct(solved.shape, solved.dtype),
            jax.ShapeDtypeStruct(field.shape, field.dtype),
        ),
        in_specs=[vmem, hbm],
        out_specs=(vmem, hbm),
        scratch_shapes=[
            pltpu.VMEM(field.shape, field.dtype),
            pltpu.SemaphoreType.DMA((chunks,)),
            pltpu.SemaphoreType.DMA,
        ],
        compiler_params=pltpu.CompilerParams(vmem_limit_bytes=60 * 1024 * 1024),
    )(solved, field)


def on_device(residuals, vectors, phases, stiffness):
    count_x = lax.axis_size("gx")
    count_y = lax.axis_size("yz")
    rhs, parts, depth, breadth, length = residuals.shape
    width = vectors.shape[0]
    count = count_x * count_y
    scale_all, rates = sweep_rates(SWEEPS, 0.8)
    vmem = pl.BlockSpec(memory_space=pltpu.VMEM)
    hbm = pl.BlockSpec(memory_space=pl.ANY)
    panel = (width, 3 * count_y * width + rhs)
    cells = (depth + 2) * (breadth + 2)
    field = pltpu.VMEM(((depth + 4) * (breadth + 4), rhs, length), jnp.float32)
    slots = 16 + 4 * parts
    f32, half = jnp.float32, jnp.bfloat16
    solved, field_out = pl.pallas_call(
        functools.partial(kernel, count_x, count_y, scale_all, rates),
        out_shape=(
            jax.ShapeDtypeStruct((width, rhs), f32),
            jax.ShapeDtypeStruct(residuals.shape, f32),
        ),
        in_specs=[pl.BlockSpec(memory_space=pltpu.SMEM), vmem, hbm, hbm],
        out_specs=(vmem, hbm),
        scratch_shapes=[
            pltpu.VMEM((parts + 1, depth + 4, breadth + 4, width, length), f32),
            pltpu.VMEM((parts * depth, width, breadth, length), f32),
            pltpu.VMEM((parts * depth, rhs, breadth, length), f32),
            pltpu.VMEM((2, parts, rhs, breadth, length), f32),
            pltpu.VMEM((2, parts, depth, rhs, length), f32),
            pltpu.VMEM((2, parts, depth, rhs, length), f32),
            pltpu.VMEM((parts * depth, rhs, breadth, length), f32),
            pltpu.VMEM((depth * breadth, length), f32),
            pltpu.VMEM((2, 2, depth, length), f32),
            pltpu.VMEM((2, 2 * breadth, length), f32),
            pltpu.VMEM((2, 2, depth, length), f32),
            pltpu.VMEM((cells, 8, width, length), f32),
            pltpu.VMEM((SWEEPS - 1, cells, 6, width, length), f32),
            pltpu.VMEM((parts, depth + 2, breadth + 2, 2 * width, length), half),
            pltpu.VMEM((parts, depth, 4, 2 * width, length), half),
            pltpu.VMEM((parts, 4, breadth + 2, 2 * width, length), half),
            pltpu.VMEM((parts, depth, breadth, 2 * width, length), half),
            pltpu.VMEM((10, rhs, 4 * width), half),
            pltpu.VMEM(panel, f32),
            pltpu.VMEM((count,) + panel, f32),
            pltpu.VMEM((count * width, rhs), f32),
            field, field, field,
            pltpu.SemaphoreType.DMA,
            pltpu.SemaphoreType.DMA,
            pltpu.SemaphoreType.DMA,
            pltpu.SemaphoreType.DMA,
            pltpu.SemaphoreType.DMA,
            pltpu.SemaphoreType.DMA((slots,)),
            pltpu.SemaphoreType.DMA((slots,)),
        ],
        compiler_params=pltpu.CompilerParams(
            collective_id=0, has_side_effects=True, vmem_limit_bytes=60 * 1024 * 1024
        ),
    )(stiffness, phases, vectors, residuals)
    return deliver(solved, field_out)


def solution(mesh):
    return jax.shard_map(
        on_device,
        mesh=mesh,
        in_specs=(
            P(None, None, "gx", "yz", None),
            P(None, None, "gx", "yz", None),
            P("gx", "yz", None),
            P(),
        ),
        out_specs=(P(("gx", "yz"), None), P(None, None, "gx", "yz", None)),
        check_vma=False,
    )
```

```python
import functools

import jax
import jax.numpy as jnp
from jax import lax
from jax.experimental import pallas as pl
from jax.experimental.pallas import tpu as pltpu
from jax.sharding import PartitionSpec as P

SWEEPS = 4


HIGH = lax.Precision.HIGHEST


MESH = pl.DeviceIdType.MESH


def eliminate(rows, size, group):
    sublane = lax.broadcasted_iota(jnp.int32, rows[0].shape, 0)
    rows = list(rows)
    for base in range(0, size, group):
        columns = [
            [jnp.broadcast_to(a[:, base + j : base + j + 1], a.shape) for j in range(group)] for a in rows
        ]
        for j in range(group):
            p = base + j
            here = sublane == p
            for i, a in enumerate(rows):
                own = columns[i][j]
                inverse = 1.0 / own[p : p + 1, :]
                pivot = a[p : p + 1, :] * inverse
                for k in range(j + 1, group):
                    c = columns[i][k]
                    step = c[p : p + 1, :] * inverse
                    columns[i][k] = jnp.where(here, step, c - own * step)
                rows[i] = jnp.where(here, pivot, a - own * pivot)
    return rows


def product(a, b):
    return jnp.dot(a, b, precision=HIGH, preferred_element_type=jnp.float32)


def cyclic_solve(rows, size):
    count = len(rows)
    width = rows[0].shape[1]
    lane = lax.broadcasted_iota(jnp.int32, rows[0].shape, 1)
    is_own = lane < size
    is_low = (lane >= size) & (lane < 2 * size)
    is_high = (lane >= 2 * size) & (lane < 3 * size)
    is_rhs = lane >= 3 * size
    live = list(range(count))
    system = dict(enumerate(rows))
    levels = []
    while len(live) > 1:
        out = live[1::2]
        kept = live[0::2]
        solved = dict(zip(out, eliminate([system[i] for i in out], size, 4 if len(out) > 2 else 8)))
        fresh = {}
        for place, i in enumerate(kept):
            a = system[i]
            total = jnp.where(is_own | is_rhs, a, 0.0)
            if place > 0:
                t = product(a[:, size : 2 * size], solved[out[place - 1]])
                shifted = pltpu.roll(t, width - 2 * size, 1)
                total = total - jnp.where(is_own, shifted, jnp.where(is_low | is_rhs, t, 0.0))
            if place < len(out):
                t = product(a[:, 2 * size : 3 * size], solved[out[place]])
                shifted = pltpu.roll(t, width - size, 1)
                total = total - jnp.where(is_own, shifted, jnp.where(is_high | is_rhs, t, 0.0))
            fresh[i] = total
        levels.append((live, out, solved))
        system = fresh
        live = kept
    last = eliminate([system[live[0]]], size, 8)[0]
    answer = {live[0]: last[:, 3 * size :]}
    for before, out, solved in reversed(levels):
        for i in out:
            a = solved[i]
            place = before.index(i)
            x = a[:, 3 * size :] - product(a[:, size : 2 * size], answer[before[place - 1]])
            if place + 1 < len(before):
                x = x - product(a[:, 2 * size : 3 * size], answer[before[place + 1]])
            answer[i] = x
    return [answer[i] for i in range(count)]


WEST, EAST, SOUTH, NORTH, LOW, HIGH_Z = range(1, 7)


def sweep_rates(sweeps, damping):
    powers = [0.0] * sweeps
    term = [1.0]
    for _ in range(sweeps):
        for i, value in enumerate(term):
            powers[i] += value
        longer = [0.0] * (len(term) + 1)
        for i, value in enumerate(term):
            longer[i] += (1.0 - damping) * value
            longer[i + 1] += damping * value
        term = longer
    return damping * powers[0], [powers[i] / powers[i - 1] for i in range(sweeps - 1, 0, -1)]


def packed(v):
    coarse = v.astype(jnp.bfloat16).astype(jnp.float32)
    return jnp.concatenate([coarse, v - coarse], axis=0).astype(jnp.bfloat16)


def kernel(
    count_x, count_y, scale_all, rates,
    stiffness, phases, vectors, res,
    mine, out,
    ext, vraw, rbuf, hx, hy, ybuf, obuf, mown, msend, mx, my,
    weights, hweights, own_p, side_y, side_x, phis, lhs,
    panel, gathered, coeffs, first, second, third,
    load_sem, res_sem, out_sem, panel_send, panel_recv, halo_send, halo_recv
):
    index_x = lax.axis_index("gx")
    index_y = lax.axis_index("yz")
    count = count_x * count_y
    me = index_x * count_y + index_y
    rhs, parts, depth, breadth, length = res.shape
    width = vectors.shape[0]
    levels = stiffness.shape[0]
    wide = breadth + 4
    cross = breadth + 2
    barrier = pltpu.get_barrier_semaphore()
    zero = jnp.zeros((width, length), jnp.float32)
    tall = jnp.zeros((rhs, length), jnp.float32)

    def rows_of(ref):
        return ref.reshape(ref.shape[0] * breadth, length)

    def load(i, carry):
        c = i // depth
        x = i - c * depth
        pltpu.make_async_copy(vectors.at[:, c, x], vraw.at[i], load_sem).start()
        return carry

    lax.fori_loop(0, parts * depth, load, 0)

    def clear_y(y, carry):
        for f in range(parts + 1):
            for x in (0, 1, depth + 2, depth + 3):
                ext[f, x, y] = zero
        return carry

    def clear_x(x, carry):
        for f in range(parts + 1):
            for y in (0, 1, breadth + 2, breadth + 3):
                ext[f, x + 2, y] = zero
        return carry

    lax.fori_loop(0, wide, clear_y, 0)
    lax.fori_loop(0, depth, clear_x, 0)
    mx[...] = jnp.zeros(mx.shape, jnp.float32)
    my[...] = jnp.zeros(my.shape, jnp.float32)

    def each_other(act):
        def along(g, carry):
            for h in range(count_y):
                pl.when(jnp.logical_or(g != index_x, h != index_y))(functools.partial(act, g, h))
            return carry

        lax.fori_loop(0, count_x, along, 0)

    def greet(g, h):
        pl.semaphore_signal(barrier, inc=1, device_id=(g, h), device_id_type=MESH)

    each_other(greet)

    def load_res(i, carry):
        c = i // depth
        x = i - c * depth
        pltpu.make_async_copy(res.at[:, c, x], rbuf.at[i], res_sem).start()
        return carry

    lax.fori_loop(0, parts * depth, load_res, 0)

    for x in range(depth):
        p = phases[x]
        m = jnp.zeros(p.shape, jnp.float32)
        for level in range(levels):
            m = jnp.where(p == level, stiffness[level], m)
        mown[pl.ds(x * breadth, breadth), :] = m
    for side in range(2):
        for layer in range(2):
            y = layer + side * (breadth - 2)
            msend[side, layer] = mown[pl.ds(y, depth, stride=breadth), :]

    def spread_own(x, carry):
        for y in range(breadth):
            row = mown[pl.ds(x * breadth + y, 1), :]
            ext[parts, x + 2, y + 2] = jnp.broadcast_to(row, (width, length))
        return carry

    lax.fori_loop(0, depth, spread_own, 0)
    pltpu.make_async_copy(vraw, vraw, load_sem).wait()

    def fill(i, carry):
        c = i // depth
        x = i - c * depth
        tiles = rows_of(vraw.at[i])
        for y in range(breadth):
            ext[c, x + 2, y + 2] = tiles[pl.ds(y, width, stride=breadth), :]
        return carry

    lax.fori_loop(0, parts * depth, fill, 0)
    pl.semaphore_wait(barrier, count - 1)

    def can(dx, dy):
        ok = index_x >= 0
        if dx:
            ok = index_x > 0 if dx < 0 else index_x < count_x - 1
        if dy:
            ok_y = index_y > 0 if dy < 0 else index_y < count_y - 1
            ok = jnp.logical_and(ok, ok_y) if dx else ok_y
        return ok

    def exchange(source, target, dx, dy, slot):
        return pltpu.make_async_remote_copy(
            src_ref=source,
            dst_ref=target,
            send_sem=halo_send.at[slot],
            recv_sem=halo_recv.at[slot],
            device_id=(index_x + dx, index_y + dy),
            device_id_type=MESH,
        )

    started = []

    def start(source, target, dx, dy):
        copy = exchange(source, target, dx, dy, len(started))
        pl.when(can(dx, dy))(copy.start)
        started.append((can(dx, dy), can(-dx, -dy), copy))

    def arrived(low, high):
        for _, receives, copy in started[low:high]:
            pl.when(receives)(copy.wait_recv)

    start(mown.at[pl.ds(0, 2 * breadth)], mx.at[1], -1, 0)
    start(mown.at[pl.ds((depth - 2) * breadth, 2 * breadth)], mx.at[0], 1, 0)
    start(msend.at[0], my.at[1], 0, -1)
    start(msend.at[1], my.at[0], 0, 1)

    field = pl.ds(0, parts)
    inner_x, inner_y = pl.ds(2, depth), pl.ds(2, breadth)

    def layer(step):
        start(ext.at[field, 2 + step, inner_y], ext.at[field, depth + 2 + step, inner_y], -1, 0)
        start(ext.at[field, depth + 1 - step, inner_y], ext.at[field, 1 - step, inner_y], 1, 0)
        start(ext.at[field, inner_x, 2 + step], ext.at[field, inner_x, breadth + 2 + step], 0, -1)
        start(ext.at[field, inner_x, breadth + 1 - step], ext.at[field, inner_x, 1 - step], 0, 1)

    for x, dx, to_x in ((2, -1, depth + 2), (depth + 1, 1, 1)):
        for y, dy, to_y in ((2, -1, breadth + 2), (breadth + 1, 1, 1)):
            start(ext.at[:, x, y], ext.at[:, to_x, to_y], dx, dy)
    layer(0)

    base_slot = len(started) + 4
    ways = ((-1, 0), (1, 0), (0, -1), (0, 1))

    def res_copy(way, part):
        dx, dy = ways[way]
        if dx:
            source, target = res.at[:, part, 0 if dx < 0 else depth - 1], hx.at[1 - way, part]
        else:
            source, target = ybuf.at[way - 2, part], hy.at[3 - way, part]
        return exchange(source, target, dx, dy, base_slot + part * 4 + way)

    def send_res(begin, end, which):
        for part in range(begin, end):
            for way in which:
                pl.when(can(*ways[way]))(res_copy(way, part).start)

    layer(1)
    pltpu.make_async_copy(rbuf, rbuf, res_sem).wait()

    def loads(i, sums):
        f = i // depth
        x = i - f * depth
        tiles = rows_of(rbuf.at[i])
        for side in range(2):
            ybuf[side, f, x] = tiles[pl.ds(side * (breadth - 1), rhs, stride=breadth), :]
        for y in range(breadth):
            v = ext[f, x + 2, y + 2]
            sums = tuple(
                total + v * tiles[pl.ds(r * breadth + y, 1), :] for r, total in enumerate(sums)
            )
        return sums

    sums = lax.fori_loop(0, parts * depth, loads, (zero,) * rhs)
    send_res(0, parts, (2, 3))
    lane = lax.broadcasted_iota(jnp.int32, panel.shape, 1)

    def placed(total, at):
        return jnp.where(lane == at, jnp.sum(total, axis=1, keepdims=True), 0.0)

    size = count_y * width
    row = jnp.zeros(panel.shape, jnp.float32)
    for r in range(rhs):
        row = row + placed(sums[r], 3 * size + r)

    arrived(0, 4)

    def spread_x(y, carry):
        for side in range(2):
            for step in range(2):
                line = mx[side, pl.ds(step * breadth + y, 1), :]
                ext[parts, side * (depth + 2) + step, y + 2] = jnp.broadcast_to(line, (width, length))
        return carry

    def spread_y(x, carry):
        for side in range(2):
            for step in range(2):
                line = my[side, step, pl.ds(x, 1), :]
                ext[parts, x + 2, side * (breadth + 2) + step] = jnp.broadcast_to(line, (width, length))
        return carry

    lax.fori_loop(0, breadth, spread_x, 0)
    lax.fori_loop(0, depth, spread_y, 0)
    arrived(4, 8)
    z = lax.broadcasted_iota(jnp.int32, (width, length), 1)

    def weigh(i, carry):
        inside = jnp.where(jnp.logical_or(i == 0, i == depth + 1), 0.0, 1.0).astype(jnp.float32)
        for j in range(cross):
            x, y = i + 1, j + 1
            m = ext[parts, x, y]
            low = 0.5 * (m + jnp.where(z > 0, pltpu.roll(m, 1, 1), 0.0))
            high = 0.5 * (m + jnp.where(z < length - 1, pltpu.roll(m, length - 1, 1), 0.0))
            west = 0.5 * (m + ext[parts, x - 1, y])
            east = 0.5 * (m + ext[parts, x + 1, y])
            south = 0.5 * (m + ext[parts, x, y - 1])
            north = 0.5 * (m + ext[parts, x, y + 1])
            diagonal = 0.002 + west + east + south + north + low + high
            inverse = jnp.where(m > 0, 1.0, 0.0) / diagonal
            if j == 0 or j == cross - 1:
                inverse = inverse * inside
            at = i * cross + j
            weights[at, 0] = scale_all * inverse
            weights[at, WEST] = inverse * west
            weights[at, EAST] = inverse * east
            weights[at, SOUTH] = inverse * south
            weights[at, NORTH] = inverse * north
            weights[at, LOW] = jnp.where(z > 0, inverse * low, 0.0)
            weights[at, HIGH_Z] = jnp.where(z < length - 1, inverse * high, 0.0)
            weights[at, 7] = diagonal
        return carry

    lax.fori_loop(0, depth + 2, weigh, 0)

    def gram(sums, left, f, x, y):
        return tuple(
            total + left * ext[f, x, y, pl.ds(l, 1), :] for l, total in enumerate(sums)
        )

    def own_block(i, sums):
        inside_x = (
            jnp.where(i > 0, 1.0, 0.0).astype(jnp.float32),
            jnp.where(i < depth - 1, 1.0, 0.0).astype(jnp.float32),
        )
        x = i + 2
        x_low = jnp.maximum(i - 1, 0) + 2
        x_high = jnp.minimum(i + 1, depth - 1) + 2
        for y in range(2, breadth + 2):
            at = (i + 1) * cross + y - 1
            west = weights[at, WEST] * inside_x[0]
            east = weights[at, EAST] * inside_x[1]
            for f in range(parts):
                v = ext[f, x, y]
                near = west * ext[f, x_low, y] + east * ext[f, x_high, y]
                if y > 2:
                    near = near + weights[at, SOUTH] * ext[f, x, y - 1]
                if y < breadth + 1:
                    near = near + weights[at, NORTH] * ext[f, x, y + 1]
                near = near + weights[at, LOW] * pltpu.roll(v, 1, 1)
                near = near + weights[at, HIGH_Z] * pltpu.roll(v, length - 1, 1)
                own_p[f, i + 1, y - 1] = packed(near - v)
                phis[f, i, y - 2] = packed(v)
                sums = gram(sums, weights[at, 7] * (v - near), f, x, y)
        return sums

    def side_block(along, fixed_x, fixed_y, dx, dy):
        which = {(-1, 0): WEST, (1, 0): EAST, (0, -1): SOUTH, (0, 1): NORTH}[(dx, dy)]

        def one(i, sums):
            x = i + 2 if fixed_x is None else fixed_x
            y = i + 2 if fixed_y is None else fixed_y
            at = (x - 1) * cross + y - 1
            weight = weights[at, which] * weights[at, 7]
            for f in range(parts):
                sums = gram(sums, -weight * ext[f, x, y], f, x + dx, y + dy)
            return sums

        return lax.fori_loop(0, along, one, (zero,) * width)

    def put(row, totals, at):
        for l in range(width):
            row = row + placed(totals[l], at + l)
        return row

    row = put(row, lax.fori_loop(0, depth, own_block, (zero,) * width), index_y * width)
    arrived(8, 12)
    row = put(row, side_block(depth, None, 2, 0, -1), (index_y - 1) * width)
    row = put(row, side_block(depth, None, breadth + 1, 0, 1), (index_y + 1) * width)
    row = put(row, side_block(breadth, 2, None, -1, 0), size + index_y * width)
    row = put(row, side_block(breadth, depth + 1, None, 1, 0), 2 * size + index_y * width)
    panel[...] = row
    gathered[me] = row

    def send(g, h):
        pltpu.make_async_remote_copy(
            src_ref=panel,
            dst_ref=gathered.at[me],
            send_sem=panel_send,
            recv_sem=panel_recv,
            device_id=(g, h),
            device_id_type=MESH,
        ).start()

    each_other(send)
    send_res(0, parts, (0, 1))

    def no_halo(way):
        dx, dy = ways[way]

        def wipe_x():
            hx[way] = jnp.zeros(hx.shape[1:], jnp.float32)

        def wipe_y():
            hy[way - 2] = jnp.zeros(hy.shape[1:], jnp.float32)

        pl.when(jnp.logical_not(can(dx, dy)))(wipe_x if dx else wipe_y)

    for way in range(4):
        no_halo(way)

    def multiples(i, carry):
        for j in range(cross):
            at = i * cross + j
            for q in range(WEST, HIGH_Z + 1):
                w = weights[at, q]
                for n, rate in enumerate(rates):
                    hweights[n, at, q - 1] = rate * w
        return carry

    lax.fori_loop(0, depth + 2, multiples, 0)

    def reach(f, at, which, x, y):
        return packed(weights[at, which] * ext[f, x, y])

    def seams_x(i, carry):
        y = i + 2
        for f in range(parts):
            side_x[f, 1, i + 1] = reach(f, cross + i + 1, WEST, 1, y)
            side_x[f, 2, i + 1] = reach(f, depth * cross + i + 1, EAST, depth + 2, y)
            own_p[f, 0, i + 1] = reach(f, i + 1, EAST, 2, y)
            own_p[f, depth + 1, i + 1] = reach(f, (depth + 1) * cross + i + 1, WEST, depth + 1, y)
        return carry

    def seams_y(i, carry):
        x = i + 2
        at = (i + 1) * cross
        for f in range(parts):
            side_y[f, i, 1] = reach(f, at + 1, SOUTH, x, 1)
            side_y[f, i, 2] = reach(f, at + breadth, NORTH, x, breadth + 2)
            own_p[f, i + 1, 0] = reach(f, at, NORTH, x, 2)
            own_p[f, i + 1, breadth + 1] = reach(f, at + breadth + 1, SOUTH, x, breadth + 1)
        return carry

    lax.fori_loop(0, breadth, seams_x, 0)
    lax.fori_loop(0, depth, seams_y, 0)

    for buffer in (first, second, third):
        def clear_row(y, carry, buffer=buffer):
            buffer[y] = tall
            buffer[(depth + 3) * wide + y] = tall
            return carry

        def clear_column(x, carry, buffer=buffer):
            buffer[x * wide] = tall
            buffer[x * wide + wide - 1] = tall
            return carry

        lax.fori_loop(0, wide, clear_row, 0)
        lax.fori_loop(0, depth + 4, clear_column, 0)
    for x in (1, depth + 2):
        for y in (1, breadth + 2):
            first[x * wide + y] = tall

    everyone = gathered.at[pl.ds(0, count - 1)]
    panels_all = pltpu.make_async_remote_copy(
        src_ref=everyone,
        dst_ref=everyone,
        send_sem=panel_send,
        recv_sem=panel_recv,
        device_id=(lax.rem(index_x + 1, count_x), index_y),
        device_id_type=MESH,
    )
    panels_all.wait_recv()
    panels = [gathered[pl.ds(g * count_y, count_y)].reshape(size, panel.shape[1]) for g in range(count_x)]
    for g, x in enumerate(cyclic_solve(panels, size)):
        coeffs[pl.ds(g * size, size), :] = x
    mine[...] = coeffs[pl.ds(pl.multiple_of(me * width, width), width), :]

    for slot in range(10):
        step_x, step_y = (slot // 3 - 1, slot % 3 - 1) if slot < 9 else (0, 0)
        near_x = jnp.clip(index_x + step_x, 0, count_x - 1)
        near_y = jnp.clip(index_y + step_y, 0, count_y - 1)
        begin = pl.multiple_of((near_x * count_y + near_y) * width, width)
        c = coeffs[pl.ds(begin, width), :]
        if slot < 9:
            c = scale_all * c
        coarse = c.astype(jnp.bfloat16).astype(jnp.float32)
        fine = c - coarse
        lhs[slot] = jnp.concatenate([coarse, coarse, fine, fine], axis=0).T.astype(jnp.bfloat16)

    arrived(12, 16)
    for f in range(parts):
        for slot, at_low, at_high, way, x in (
            (0, 1, breadth, None, 1), (1, cross, cross + breadth + 1, WEST, 1),
            (2, depth * cross, depth * cross + breadth + 1, EAST, depth + 2),
            (3, (depth + 1) * cross + 1, (depth + 1) * cross + breadth, None, depth + 2),
        ):
            side_x[f, slot, 0] = reach(f, at_low, way or SOUTH, x, 1)
            side_x[f, slot, breadth + 1] = reach(f, at_high, way or NORTH, x, breadth + 2)

    def bounds(i, last):
        return (
            jnp.where(i > 0, 1.0, 0.0).astype(jnp.float32),
            jnp.where(i < last, 1.0, 0.0).astype(jnp.float32),
        )

    def halo_term(f, at, x, y, terms):
        v = ext[f, x, y]
        near = weights[at, LOW] * pltpu.roll(v, 1, 1)
        near = near + weights[at, HIGH_Z] * pltpu.roll(v, length - 1, 1)
        for weight, px, py in terms:
            near = near + weight * ext[f, px, py]
        return packed(near - v)

    def rims_x(i, carry):
        y = i + 2
        low, high = bounds(i, breadth - 1)
        for slot, x, outward, px in ((0, 1, WEST, 0), (3, depth + 2, EAST, depth + 3)):
            at = (x - 1) * cross + i + 1
            terms = (
                (weights[at, outward], px, y),
                (weights[at, SOUTH] * low, x, y - 1),
                (weights[at, NORTH] * high, x, y + 1),
            )
            for f in range(parts):
                side_x[f, slot, i + 1] = halo_term(f, at, x, y, terms)
        return carry

    def rims_y(i, carry):
        x = i + 2
        low, high = bounds(i, depth - 1)
        for slot, y, outward, py in ((0, 1, SOUTH, 0), (3, breadth + 2, NORTH, breadth + 3)):
            at = (i + 1) * cross + y - 1
            terms = (
                (weights[at, outward], x, py),
                (weights[at, WEST] * low, x - 1, y),
                (weights[at, EAST] * high, x + 1, y),
            )
            for f in range(parts):
                side_y[f, i, slot] = halo_term(f, at, x, y, terms)
        return carry

    lax.fori_loop(0, breadth, rims_x, 0)
    lax.fori_loop(0, depth, rims_y, 0)

    def combine(slot, cells):
        block = jnp.concatenate(cells, axis=1)
        return jnp.dot(
            lhs[slot], jnp.concatenate([block, block], axis=0), preferred_element_type=jnp.float32
        )

    def cut(block, i):
        return block[:, i * length : (i + 1) * length]

    def spread(w):
        return jnp.concatenate([w] * (rhs // width), axis=0)

    def beside(source, n, x, y):
        cell = x * wide + y
        at = (x - 1) * cross + y - 1
        centre = source[cell]
        total = spread(hweights[n, at, 0]) * source[cell - wide]
        total = total + spread(hweights[n, at, 1]) * source[cell + wide]
        total = total + spread(hweights[n, at, 2]) * source[cell - 1]
        total = total + spread(hweights[n, at, 3]) * source[cell + 1]
        total = total + spread(hweights[n, at, 4]) * pltpu.roll(centre, 1, 1)
        total = total + spread(hweights[n, at, 5]) * pltpu.roll(centre, length - 1, 1)
        return total

    def in_pairs(source, start, rows, act):
        def pair(i, carry):
            for k in range(2):
                act(start + 2 * i + k)
            return carry

        lax.fori_loop(0, rows // 2, pair, 0)

    def component(part, carry):
        def halos(which):
            for way in which:
                dx, dy = ways[way]
                pl.when(can(-dx, -dy))(res_copy(way, part).wait_recv)

        def force_row(i, side=None):
            own = combine(4, [own_p[part, i + 1, j] for j in range(cross)])
            south = combine(3, [side_y[part, i, j] for j in (0, 1)])
            north = combine(5, [side_y[part, i, j] for j in (2, 3)])
            tiles = rows_of(rbuf.at[part * depth + i])
            if side is not None:
                corner, middle = outer(side, 1 + side)
            for j in range(cross):
                value = cut(own, j)
                if j < 2:
                    value = value + cut(south, j)
                if j >= breadth:
                    value = value + cut(north, j - breadth)
                if j == 0 or j == cross - 1:
                    loaded = hy[j // breadth, part, i]
                else:
                    loaded = tiles[pl.ds(j - 1, rhs, stride=breadth), :]
                value = spread(weights[(i + 1) * cross + j, 0]) * loaded + value
                if side is not None:
                    value = value + (cut(middle, j - 1) if 0 < j < cross - 1 else corner[j // breadth])
                first[(i + 2) * wide + j + 1] = value

        def outer(side, edge):
            block = 6 * side
            corner = [combine(block + 2 * end, [side_x[part, edge, end * (breadth + 1)]]) for end in range(2)]
            return corner, combine(block + 1, [side_x[part, edge, j + 1] for j in range(breadth)])

        def force_inner(i, carry):
            force_row(i)
            return carry

        halos((2, 3))
        lax.fori_loop(1, depth - 1, force_inner, 0)
        for side in range(2):
            force_row(side * (depth - 1), side)
        halos((0, 1))
        for side in range(2):
            x = side * (depth + 1) + 1
            corner, middle = outer(side, 3 * side)
            own = combine(4, [own_p[part, x - 1, j + 1] for j in range(breadth)])
            tiles = rows_of(hx.at[side, part])
            for j in range(breadth):
                value = cut(middle, j) + cut(own, j)
                if j == 0:
                    value = value + corner[0]
                if j == breadth - 1:
                    value = value + corner[1]
                loaded = tiles[pl.ds(j, rhs, stride=breadth), :]
                value = spread(weights[(x - 1) * cross + j + 1, 0]) * loaded + value
                first[x * wide + j + 2] = value

        source, target, spare = first, second, third
        for n in range(len(rates) - 1):
            def relax(x, source=source, target=target, n=n):
                for j in range(cross):
                    cell = x * wide + j + 1
                    target[cell] = first[cell] + beside(source, n, x, j + 1)

            in_pairs(source, 1, depth + 2, relax)
            source, target, spare = target, spare, target

        def finish(x):
            fine = combine(9, [phis[part, x - 2, j] for j in range(breadth)])
            row = part * depth + x - 2
            tiles = rows_of(obuf.at[row])
            for j in range(breadth):
                value = cut(fine, j) + first[x * wide + j + 2]
                value = value + beside(source, len(rates) - 1, x, j + 2)
                tiles[pl.ds(j, rhs, stride=breadth), :] = value
            pltpu.make_async_copy(obuf.at[row], out.at[:, part, x - 2], out_sem).start()

        in_pairs(source, 2, depth, finish)
        return carry

    lax.fori_loop(0, parts, component, 0)
    panels_all.wait_send()
    for sends, _, copy in started:
        pl.when(sends)(copy.wait_send)
    for part in range(parts):
        for way in range(4):
            pl.when(can(*ways[way]))(res_copy(way, part).wait_send)
    pltpu.make_async_copy(obuf, obuf, out_sem).wait()


def deliver_kernel(chunks, solved, field, mine, out, held, in_sem, out_sem):
    rows = held.shape[0] // chunks
    for i in range(chunks):
        part = pl.ds(i * rows, rows)
        pltpu.make_async_copy(field.at[part], held.at[part], in_sem.at[i]).start()
    mine[...] = solved[...]
    for i in range(chunks):
        part = pl.ds(i * rows, rows)
        pltpu.make_async_copy(field.at[part], held.at[part], in_sem.at[i]).wait()
        pltpu.make_async_copy(held.at[part], out.at[part], out_sem).start()
    pltpu.make_async_copy(held, out, out_sem).wait()


def deliver(solved, field):
    chunks = 8 if field.shape[0] % 8 == 0 else 1
    vmem = pl.BlockSpec(memory_space=pltpu.VMEM)
    hbm = pl.BlockSpec(memory_space=pl.ANY)
    return pl.pallas_call(
        functools.partial(deliver_kernel, chunks),
        out_shape=(
            jax.ShapeDtypeStruct(solved.shape, solved.dtype),
            jax.ShapeDtypeStruct(field.shape, field.dtype),
        ),
        in_specs=[vmem, hbm],
        out_specs=(vmem, hbm),
        scratch_shapes=[
            pltpu.VMEM(field.shape, field.dtype),
            pltpu.SemaphoreType.DMA((chunks,)),
            pltpu.SemaphoreType.DMA,
        ],
        compiler_params=pltpu.CompilerParams(vmem_limit_bytes=60 * 1024 * 1024),
    )(solved, field)


def on_device(residuals, vectors, phases, stiffness):
    count_x = lax.axis_size("gx")
    count_y = lax.axis_size("yz")
    rhs, parts, depth, breadth, length = residuals.shape
    width = vectors.shape[0]
    count = count_x * count_y
    scale_all, rates = sweep_rates(SWEEPS, 0.8)
    vmem = pl.BlockSpec(memory_space=pltpu.VMEM)
    hbm = pl.BlockSpec(memory_space=pl.ANY)
    panel = (width, 3 * count_y * width + rhs)
    cells = (depth + 2) * (breadth + 2)
    field = pltpu.VMEM(((depth + 4) * (breadth + 4), rhs, length), jnp.float32)
    slots = 16 + 4 * parts
    f32, half = jnp.float32, jnp.bfloat16
    solved, field_out = pl.pallas_call(
        functools.partial(kernel, count_x, count_y, scale_all, rates),
        out_shape=(
            jax.ShapeDtypeStruct((width, rhs), f32),
            jax.ShapeDtypeStruct(residuals.shape, f32),
        ),
        in_specs=[pl.BlockSpec(memory_space=pltpu.SMEM), vmem, hbm, hbm],
        out_specs=(vmem, hbm),
        scratch_shapes=[
            pltpu.VMEM((parts + 1, depth + 4, breadth + 4, width, length), f32),
            pltpu.VMEM((parts * depth, width, breadth, length), f32),
            pltpu.VMEM((parts * depth, rhs, breadth, length), f32),
            pltpu.VMEM((2, parts, rhs, breadth, length), f32),
            pltpu.VMEM((2, parts, depth, rhs, length), f32),
            pltpu.VMEM((2, parts, depth, rhs, length), f32),
            pltpu.VMEM((parts * depth, rhs, breadth, length), f32),
            pltpu.VMEM((depth * breadth, length), f32),
            pltpu.VMEM((2, 2, depth, length), f32),
            pltpu.VMEM((2, 2 * breadth, length), f32),
            pltpu.VMEM((2, 2, depth, length), f32),
            pltpu.VMEM((cells, 8, width, length), f32),
            pltpu.VMEM((SWEEPS - 1, cells, 6, width, length), f32),
            pltpu.VMEM((parts, depth + 2, breadth + 2, 2 * width, length), half),
            pltpu.VMEM((parts, depth, 4, 2 * width, length), half),
            pltpu.VMEM((parts, 4, breadth + 2, 2 * width, length), half),
            pltpu.VMEM((parts, depth, breadth, 2 * width, length), half),
            pltpu.VMEM((10, rhs, 4 * width), half),
            pltpu.VMEM(panel, f32),
            pltpu.VMEM((count,) + panel, f32),
            pltpu.VMEM((count * width, rhs), f32),
            field, field, field,
            pltpu.SemaphoreType.DMA,
            pltpu.SemaphoreType.DMA,
            pltpu.SemaphoreType.DMA,
            pltpu.SemaphoreType.DMA,
            pltpu.SemaphoreType.DMA,
            pltpu.SemaphoreType.DMA((slots,)),
            pltpu.SemaphoreType.DMA((slots,)),
        ],
        compiler_params=pltpu.CompilerParams(
            collective_id=0, has_side_effects=True, vmem_limit_bytes=60 * 1024 * 1024
        ),
    )(stiffness, phases, vectors, residuals)
    return deliver(solved, field_out)


def solution(mesh):
    return jax.shard_map(
        on_device,
        mesh=mesh,
        in_specs=(
            P(None, None, "gx", "yz", None),
            P(None, None, "gx", "yz", None),
            P("gx", "yz", None),
            P(),
        ),
        out_specs=(P(("gx", "yz"), None), P(None, None, "gx", "yz", None)),
        check_vma=False,
    )
```

```python
import functools

import jax
import jax.numpy as jnp
from jax import lax
from jax.experimental import pallas as pl
from jax.experimental.pallas import tpu as pltpu
from jax.sharding import PartitionSpec as P

SWEEPS = 4


HIGH = lax.Precision.HIGHEST


MESH = pl.DeviceIdType.MESH


def eliminate(rows, size, group):
    sublane = lax.broadcasted_iota(jnp.int32, rows[0].shape, 0)
    rows = list(rows)
    for base in range(0, size, group):
        columns = [
            [jnp.broadcast_to(a[:, base + j : base + j + 1], a.shape) for j in range(group)] for a in rows
        ]
        for j in range(group):
            p = base + j
            here = sublane == p
            for i, a in enumerate(rows):
                own = columns[i][j]
                inverse = 1.0 / own[p : p + 1, :]
                pivot = a[p : p + 1, :] * inverse
                for k in range(j + 1, group):
                    c = columns[i][k]
                    step = c[p : p + 1, :] * inverse
                    columns[i][k] = jnp.where(here, step, c - own * step)
                rows[i] = jnp.where(here, pivot, a - own * pivot)
    return rows


def product(a, b):
    return jnp.dot(a, b, precision=HIGH, preferred_element_type=jnp.float32)


def cyclic_solve(rows, size):
    count = len(rows)
    width = rows[0].shape[1]
    lane = lax.broadcasted_iota(jnp.int32, rows[0].shape, 1)
    is_own = lane < size
    is_low = (lane >= size) & (lane < 2 * size)
    is_high = (lane >= 2 * size) & (lane < 3 * size)
    is_rhs = lane >= 3 * size
    live = list(range(count))
    system = dict(enumerate(rows))
    levels = []
    while len(live) > 1:
        out = live[1::2]
        kept = live[0::2]
        solved = dict(zip(out, eliminate([system[i] for i in out], size, 4 if len(out) > 2 else 8)))
        fresh = {}
        for place, i in enumerate(kept):
            a = system[i]
            total = jnp.where(is_own | is_rhs, a, 0.0)
            if place > 0:
                t = product(a[:, size : 2 * size], solved[out[place - 1]])
                shifted = pltpu.roll(t, width - 2 * size, 1)
                total = total - jnp.where(is_own, shifted, jnp.where(is_low | is_rhs, t, 0.0))
            if place < len(out):
                t = product(a[:, 2 * size : 3 * size], solved[out[place]])
                shifted = pltpu.roll(t, width - size, 1)
                total = total - jnp.where(is_own, shifted, jnp.where(is_high | is_rhs, t, 0.0))
            fresh[i] = total
        levels.append((live, out, solved))
        system = fresh
        live = kept
    last = eliminate([system[live[0]]], size, 8)[0]
    answer = {live[0]: last[:, 3 * size :]}
    for before, out, solved in reversed(levels):
        for i in out:
            a = solved[i]
            place = before.index(i)
            x = a[:, 3 * size :] - product(a[:, size : 2 * size], answer[before[place - 1]])
            if place + 1 < len(before):
                x = x - product(a[:, 2 * size : 3 * size], answer[before[place + 1]])
            answer[i] = x
    return [answer[i] for i in range(count)]


WEST, EAST, SOUTH, NORTH, LOW, HIGH_Z = range(1, 7)


def sweep_rates(sweeps, damping):
    powers = [0.0] * sweeps
    term = [1.0]
    for _ in range(sweeps):
        for i, value in enumerate(term):
            powers[i] += value
        longer = [0.0] * (len(term) + 1)
        for i, value in enumerate(term):
            longer[i] += (1.0 - damping) * value
            longer[i + 1] += damping * value
        term = longer
    return damping * powers[0], [powers[i] / powers[i - 1] for i in range(sweeps - 1, 0, -1)]


def packed(v):
    coarse = v.astype(jnp.bfloat16).astype(jnp.float32)
    return jnp.concatenate([coarse, v - coarse], axis=0).astype(jnp.bfloat16)


def kernel(
    count_x, count_y, scale_all, rates,
    stiffness, phases, vectors, res,
    mine, out,
    ext, vraw, rbuf, hx, hy, ybuf, obuf, mown, msend, mx, my,
    weights, hweights, own_p, side_y, side_x, phis, lhs,
    panel, gathered, coeffs, first, second, third,
    load_sem, res_sem, out_sem, panel_send, panel_recv, halo_send, halo_recv
):
    index_x = lax.axis_index("gx")
    index_y = lax.axis_index("yz")
    count = count_x * count_y
    me = index_x * count_y + index_y
    rhs, parts, depth, breadth, length = res.shape
    width = vectors.shape[0]
    levels = stiffness.shape[0]
    wide = breadth + 4
    cross = breadth + 2
    barrier = pltpu.get_barrier_semaphore()
    zero = jnp.zeros((width, length), jnp.float32)
    tall = jnp.zeros((rhs, length), jnp.float32)

    def rows_of(ref):
        return ref.reshape(ref.shape[0] * breadth, length)

    def load(i, carry):
        c = i // depth
        x = i - c * depth
        pltpu.make_async_copy(vectors.at[:, c, x], vraw.at[i], load_sem).start()
        return carry

    lax.fori_loop(0, parts * depth, load, 0)

    def clear_y(y, carry):
        for f in range(parts + 1):
            for x in (0, 1, depth + 2, depth + 3):
                ext[f, x, y] = zero
        return carry

    def clear_x(x, carry):
        for f in range(parts + 1):
            for y in (0, 1, breadth + 2, breadth + 3):
                ext[f, x + 2, y] = zero
        return carry

    lax.fori_loop(0, wide, clear_y, 0)
    lax.fori_loop(0, depth, clear_x, 0)
    mx[...] = jnp.zeros(mx.shape, jnp.float32)
    my[...] = jnp.zeros(my.shape, jnp.float32)

    def each_other(act):
        def along(g, carry):
            for h in range(count_y):
                pl.when(jnp.logical_or(g != index_x, h != index_y))(functools.partial(act, g, h))
            return carry

        lax.fori_loop(0, count_x, along, 0)

    def greet(g, h):
        pl.semaphore_signal(barrier, inc=1, device_id=(g, h), device_id_type=MESH)

    each_other(greet)

    def load_res(i, carry):
        c = i // depth
        x = i - c * depth
        pltpu.make_async_copy(res.at[:, c, x], rbuf.at[i], res_sem).start()
        return carry

    lax.fori_loop(0, parts * depth, load_res, 0)

    for x in range(depth):
        p = phases[x]
        m = jnp.zeros(p.shape, jnp.float32)
        for level in range(levels):
            m = jnp.where(p == level, stiffness[level], m)
        mown[pl.ds(x * breadth, breadth), :] = m
    for side in range(2):
        for layer in range(2):
            y = layer + side * (breadth - 2)
            msend[side, layer] = mown[pl.ds(y, depth, stride=breadth), :]

    def spread_own(x, carry):
        for y in range(breadth):
            row = mown[pl.ds(x * breadth + y, 1), :]
            ext[parts, x + 2, y + 2] = jnp.broadcast_to(row, (width, length))
        return carry

    lax.fori_loop(0, depth, spread_own, 0)
    pltpu.make_async_copy(vraw, vraw, load_sem).wait()

    def fill(i, carry):
        c = i // depth
        x = i - c * depth
        tiles = rows_of(vraw.at[i])
        for y in range(breadth):
            ext[c, x + 2, y + 2] = tiles[pl.ds(y, width, stride=breadth), :]
        return carry

    lax.fori_loop(0, parts * depth, fill, 0)
    pl.semaphore_wait(barrier, count - 1)

    def can(dx, dy):
        ok = index_x >= 0
        if dx:
            ok = index_x > 0 if dx < 0 else index_x < count_x - 1
        if dy:
            ok_y = index_y > 0 if dy < 0 else index_y < count_y - 1
            ok = jnp.logical_and(ok, ok_y) if dx else ok_y
        return ok

    def exchange(source, target, dx, dy, slot):
        return pltpu.make_async_remote_copy(
            src_ref=source,
            dst_ref=target,
            send_sem=halo_send.at[slot],
            recv_sem=halo_recv.at[slot],
            device_id=(index_x + dx, index_y + dy),
            device_id_type=MESH,
        )

    started = []

    def start(source, target, dx, dy):
        copy = exchange(source, target, dx, dy, len(started))
        pl.when(can(dx, dy))(copy.start)
        started.append((can(dx, dy), can(-dx, -dy), copy))

    def arrived(low, high):
        for _, receives, copy in started[low:high]:
            pl.when(receives)(copy.wait_recv)

    start(mown.at[pl.ds(0, 2 * breadth)], mx.at[1], -1, 0)
    start(mown.at[pl.ds((depth - 2) * breadth, 2 * breadth)], mx.at[0], 1, 0)
    start(msend.at[0], my.at[1], 0, -1)
    start(msend.at[1], my.at[0], 0, 1)

    field = pl.ds(0, parts)
    inner_x, inner_y = pl.ds(2, depth), pl.ds(2, breadth)

    def layer(step):
        start(ext.at[field, 2 + step, inner_y], ext.at[field, depth + 2 + step, inner_y], -1, 0)
        start(ext.at[field, depth + 1 - step, inner_y], ext.at[field, 1 - step, inner_y], 1, 0)
        start(ext.at[field, inner_x, 2 + step], ext.at[field, inner_x, breadth + 2 + step], 0, -1)
        start(ext.at[field, inner_x, breadth + 1 - step], ext.at[field, inner_x, 1 - step], 0, 1)

    for x, dx, to_x in ((2, -1, depth + 2), (depth + 1, 1, 1)):
        for y, dy, to_y in ((2, -1, breadth + 2), (breadth + 1, 1, 1)):
            start(ext.at[:, x, y], ext.at[:, to_x, to_y], dx, dy)
    layer(0)

    base_slot = len(started) + 4
    ways = ((-1, 0), (1, 0), (0, -1), (0, 1))

    def res_copy(way, part):
        dx, dy = ways[way]
        if dx:
            source, target = res.at[:, part, 0 if dx < 0 else depth - 1], hx.at[1 - way, part]
        else:
            source, target = ybuf.at[way - 2, part], hy.at[3 - way, part]
        return exchange(source, target, dx, dy, base_slot + part * 4 + way)

    def send_res(begin, end, which):
        for part in range(begin, end):
            for way in which:
                pl.when(can(*ways[way]))(res_copy(way, part).start)

    layer(1)
    pltpu.make_async_copy(rbuf, rbuf, res_sem).wait()

    def loads(i, sums):
        f = i // depth
        x = i - f * depth
        tiles = rows_of(rbuf.at[i])
        for side in range(2):
            ybuf[side, f, x] = tiles[pl.ds(side * (breadth - 1), rhs, stride=breadth), :]
        for y in range(breadth):
            v = ext[f, x + 2, y + 2]
            sums = tuple(
                total + v * tiles[pl.ds(r * breadth + y, 1), :] for r, total in enumerate(sums)
            )
        return sums

    sums = lax.fori_loop(0, parts * depth, loads, (zero,) * rhs)
    send_res(0, parts, (2, 3))
    lane = lax.broadcasted_iota(jnp.int32, panel.shape, 1)

    def placed(total, at):
        return jnp.where(lane == at, jnp.sum(total, axis=1, keepdims=True), 0.0)

    size = count_y * width
    row = jnp.zeros(panel.shape, jnp.float32)
    for r in range(rhs):
        row = row + placed(sums[r], 3 * size + r)

    arrived(0, 4)

    def spread_x(y, carry):
        for side in range(2):
            for step in range(2):
                line = mx[side, pl.ds(step * breadth + y, 1), :]
                ext[parts, side * (depth + 2) + step, y + 2] = jnp.broadcast_to(line, (width, length))
        return carry

    def spread_y(x, carry):
        for side in range(2):
            for step in range(2):
                line = my[side, step, pl.ds(x, 1), :]
                ext[parts, x + 2, side * (breadth + 2) + step] = jnp.broadcast_to(line, (width, length))
        return carry

    lax.fori_loop(0, breadth, spread_x, 0)
    lax.fori_loop(0, depth, spread_y, 0)
    arrived(4, 8)
    z = lax.broadcasted_iota(jnp.int32, (width, length), 1)

    def weigh(i, carry):
        inside = jnp.where(jnp.logical_or(i == 0, i == depth + 1), 0.0, 1.0).astype(jnp.float32)
        for j in range(cross):
            x, y = i + 1, j + 1
            m = ext[parts, x, y]
            low = 0.5 * (m + jnp.where(z > 0, pltpu.roll(m, 1, 1), 0.0))
            high = 0.5 * (m + jnp.where(z < length - 1, pltpu.roll(m, length - 1, 1), 0.0))
            west = 0.5 * (m + ext[parts, x - 1, y])
            east = 0.5 * (m + ext[parts, x + 1, y])
            south = 0.5 * (m + ext[parts, x, y - 1])
            north = 0.5 * (m + ext[parts, x, y + 1])
            diagonal = 0.002 + west + east + south + north + low + high
            inverse = jnp.where(m > 0, 1.0, 0.0) / diagonal
            if j == 0 or j == cross - 1:
                inverse = inverse * inside
            at = i * cross + j
            weights[at, 0] = scale_all * inverse
            weights[at, WEST] = inverse * west
            weights[at, EAST] = inverse * east
            weights[at, SOUTH] = inverse * south
            weights[at, NORTH] = inverse * north
            weights[at, LOW] = jnp.where(z > 0, inverse * low, 0.0)
            weights[at, HIGH_Z] = jnp.where(z < length - 1, inverse * high, 0.0)
            weights[at, 7] = diagonal
        return carry

    lax.fori_loop(0, depth + 2, weigh, 0)

    def gram(sums, left, f, x, y):
        return tuple(
            total + left * ext[f, x, y, pl.ds(l, 1), :] for l, total in enumerate(sums)
        )

    def own_block(i, sums):
        inside_x = (
            jnp.where(i > 0, 1.0, 0.0).astype(jnp.float32),
            jnp.where(i < depth - 1, 1.0, 0.0).astype(jnp.float32),
        )
        x = i + 2
        x_low = jnp.maximum(i - 1, 0) + 2
        x_high = jnp.minimum(i + 1, depth - 1) + 2
        for y in range(2, breadth + 2):
            at = (i + 1) * cross + y - 1
            west = weights[at, WEST] * inside_x[0]
            east = weights[at, EAST] * inside_x[1]
            for f in range(parts):
                v = ext[f, x, y]
                near = west * ext[f, x_low, y] + east * ext[f, x_high, y]
                if y > 2:
                    near = near + weights[at, SOUTH] * ext[f, x, y - 1]
                if y < breadth + 1:
                    near = near + weights[at, NORTH] * ext[f, x, y + 1]
                near = near + weights[at, LOW] * pltpu.roll(v, 1, 1)
                near = near + weights[at, HIGH_Z] * pltpu.roll(v, length - 1, 1)
                own_p[f, i + 1, y - 1] = packed(near - v)
                phis[f, i, y - 2] = packed(v)
                sums = gram(sums, weights[at, 7] * (v - near), f, x, y)
        return sums

    def side_block(along, fixed_x, fixed_y, dx, dy):
        which = {(-1, 0): WEST, (1, 0): EAST, (0, -1): SOUTH, (0, 1): NORTH}[(dx, dy)]

        def one(i, sums):
            x = i + 2 if fixed_x is None else fixed_x
            y = i + 2 if fixed_y is None else fixed_y
            at = (x - 1) * cross + y - 1
            weight = weights[at, which] * weights[at, 7]
            for f in range(parts):
                sums = gram(sums, -weight * ext[f, x, y], f, x + dx, y + dy)
            return sums

        return lax.fori_loop(0, along, one, (zero,) * width)

    def put(row, totals, at):
        for l in range(width):
            row = row + placed(totals[l], at + l)
        return row

    row = put(row, lax.fori_loop(0, depth, own_block, (zero,) * width), index_y * width)
    arrived(8, 12)
    row = put(row, side_block(depth, None, 2, 0, -1), (index_y - 1) * width)
    row = put(row, side_block(depth, None, breadth + 1, 0, 1), (index_y + 1) * width)
    row = put(row, side_block(breadth, 2, None, -1, 0), size + index_y * width)
    row = put(row, side_block(breadth, depth + 1, None, 1, 0), 2 * size + index_y * width)
    panel[...] = row
    gathered[me] = row

    def send(g, h):
        pltpu.make_async_remote_copy(
            src_ref=panel,
            dst_ref=gathered.at[me],
            send_sem=panel_send,
            recv_sem=panel_recv,
            device_id=(g, h),
            device_id_type=MESH,
        ).start()

    each_other(send)
    send_res(0, parts, (0, 1))

    def no_halo(way):
        dx, dy = ways[way]

        def wipe_x():
            hx[way] = jnp.zeros(hx.shape[1:], jnp.float32)

        def wipe_y():
            hy[way - 2] = jnp.zeros(hy.shape[1:], jnp.float32)

        pl.when(jnp.logical_not(can(dx, dy)))(wipe_x if dx else wipe_y)

    for way in range(4):
        no_halo(way)

    def multiples(i, carry):
        for j in range(cross):
            at = i * cross + j
            for q in range(WEST, HIGH_Z + 1):
                w = weights[at, q]
                for n, rate in enumerate(rates):
                    hweights[n, at, q - 1] = rate * w
        return carry

    lax.fori_loop(0, depth + 2, multiples, 0)

    def reach(f, at, which, x, y):
        return packed(weights[at, which] * ext[f, x, y])

    def seams_x(i, carry):
        y = i + 2
        for f in range(parts):
            side_x[f, 1, i + 1] = reach(f, cross + i + 1, WEST, 1, y)
            side_x[f, 2, i + 1] = reach(f, depth * cross + i + 1, EAST, depth + 2, y)
            own_p[f, 0, i + 1] = reach(f, i + 1, EAST, 2, y)
            own_p[f, depth + 1, i + 1] = reach(f, (depth + 1) * cross + i + 1, WEST, depth + 1, y)
        return carry

    def seams_y(i, carry):
        x = i + 2
        at = (i + 1) * cross
        for f in range(parts):
            side_y[f, i, 1] = reach(f, at + 1, SOUTH, x, 1)
            side_y[f, i, 2] = reach(f, at + breadth, NORTH, x, breadth + 2)
            own_p[f, i + 1, 0] = reach(f, at, NORTH, x, 2)
            own_p[f, i + 1, breadth + 1] = reach(f, at + breadth + 1, SOUTH, x, breadth + 1)
        return carry

    lax.fori_loop(0, breadth, seams_x, 0)
    lax.fori_loop(0, depth, seams_y, 0)

    for buffer in (first, second, third):
        def clear_row(y, carry, buffer=buffer):
            buffer[y] = tall
            buffer[(depth + 3) * wide + y] = tall
            return carry

        def clear_column(x, carry, buffer=buffer):
            buffer[x * wide] = tall
            buffer[x * wide + wide - 1] = tall
            return carry

        lax.fori_loop(0, wide, clear_row, 0)
        lax.fori_loop(0, depth + 4, clear_column, 0)
    for x in (1, depth + 2):
        for y in (1, breadth + 2):
            first[x * wide + y] = tall

    arrived(12, 16)
    for f in range(parts):
        for slot, at_low, at_high, way, x in (
            (0, 1, breadth, None, 1), (1, cross, cross + breadth + 1, WEST, 1),
            (2, depth * cross, depth * cross + breadth + 1, EAST, depth + 2),
            (3, (depth + 1) * cross + 1, (depth + 1) * cross + breadth, None, depth + 2),
        ):
            side_x[f, slot, 0] = reach(f, at_low, way or SOUTH, x, 1)
            side_x[f, slot, breadth + 1] = reach(f, at_high, way or NORTH, x, breadth + 2)

    def bounds(i, last):
        return (
            jnp.where(i > 0, 1.0, 0.0).astype(jnp.float32),
            jnp.where(i < last, 1.0, 0.0).astype(jnp.float32),
        )

    def halo_term(f, at, x, y, terms):
        v = ext[f, x, y]
        near = weights[at, LOW] * pltpu.roll(v, 1, 1)
        near = near + weights[at, HIGH_Z] * pltpu.roll(v, length - 1, 1)
        for weight, px, py in terms:
            near = near + weight * ext[f, px, py]
        return packed(near - v)

    def rims_x(i, carry):
        y = i + 2
        low, high = bounds(i, breadth - 1)
        for slot, x, outward, px in ((0, 1, WEST, 0), (3, depth + 2, EAST, depth + 3)):
            at = (x - 1) * cross + i + 1
            terms = (
                (weights[at, outward], px, y),
                (weights[at, SOUTH] * low, x, y - 1),
                (weights[at, NORTH] * high, x, y + 1),
            )
            for f in range(parts):
                side_x[f, slot, i + 1] = halo_term(f, at, x, y, terms)
        return carry

    def rims_y(i, carry):
        x = i + 2
        low, high = bounds(i, depth - 1)
        for slot, y, outward, py in ((0, 1, SOUTH, 0), (3, breadth + 2, NORTH, breadth + 3)):
            at = (i + 1) * cross + y - 1
            terms = (
                (weights[at, outward], x, py),
                (weights[at, WEST] * low, x - 1, y),
                (weights[at, EAST] * high, x + 1, y),
            )
            for f in range(parts):
                side_y[f, i, slot] = halo_term(f, at, x, y, terms)
        return carry

    lax.fori_loop(0, breadth, rims_x, 0)
    lax.fori_loop(0, depth, rims_y, 0)

    everyone = gathered.at[pl.ds(0, count - 1)]
    panels_all = pltpu.make_async_remote_copy(
        src_ref=everyone,
        dst_ref=everyone,
        send_sem=panel_send,
        recv_sem=panel_recv,
        device_id=(lax.rem(index_x + 1, count_x), index_y),
        device_id_type=MESH,
    )
    panels_all.wait_recv()
    panels = [gathered[pl.ds(g * count_y, count_y)].reshape(size, panel.shape[1]) for g in range(count_x)]
    for g, x in enumerate(cyclic_solve(panels, size)):
        coeffs[pl.ds(g * size, size), :] = x
    mine[...] = coeffs[pl.ds(pl.multiple_of(me * width, width), width), :]

    for slot in range(10):
        step_x, step_y = (slot // 3 - 1, slot % 3 - 1) if slot < 9 else (0, 0)
        near_x = jnp.clip(index_x + step_x, 0, count_x - 1)
        near_y = jnp.clip(index_y + step_y, 0, count_y - 1)
        begin = pl.multiple_of((near_x * count_y + near_y) * width, width)
        c = coeffs[pl.ds(begin, width), :]
        if slot < 9:
            c = scale_all * c
        coarse = c.astype(jnp.bfloat16).astype(jnp.float32)
        fine = c - coarse
        lhs[slot] = jnp.concatenate([coarse, coarse, fine, fine], axis=0).T.astype(jnp.bfloat16)

    def combine(slot, cells):
        block = jnp.concatenate(cells, axis=1)
        return jnp.dot(
            lhs[slot], jnp.concatenate([block, block], axis=0), preferred_element_type=jnp.float32
        )

    def cut(block, i):
        return block[:, i * length : (i + 1) * length]

    def spread(w):
        return jnp.concatenate([w] * (rhs // width), axis=0)

    def beside(source, n, x, y):
        cell = x * wide + y
        at = (x - 1) * cross + y - 1
        centre = source[cell]
        total = spread(hweights[n, at, 0]) * source[cell - wide]
        total = total + spread(hweights[n, at, 1]) * source[cell + wide]
        total = total + spread(hweights[n, at, 2]) * source[cell - 1]
        total = total + spread(hweights[n, at, 3]) * source[cell + 1]
        total = total + spread(hweights[n, at, 4]) * pltpu.roll(centre, 1, 1)
        total = total + spread(hweights[n, at, 5]) * pltpu.roll(centre, length - 1, 1)
        return total

    def in_groups(start, rows, act):
        step = next(k for k in (5, 4, 3, 2, 1) if rows % k == 0)

        def some(i, carry):
            for k in range(step):
                act(start + step * i + k)
            return carry

        lax.fori_loop(0, rows // step, some, 0)

    def component(part, carry):
        def halos(which):
            for way in which:
                dx, dy = ways[way]
                pl.when(can(-dx, -dy))(res_copy(way, part).wait_recv)

        def force_row(i, side=None):
            own = combine(4, [own_p[part, i + 1, j] for j in range(cross)])
            south = combine(3, [side_y[part, i, j] for j in (0, 1)])
            north = combine(5, [side_y[part, i, j] for j in (2, 3)])
            tiles = rows_of(rbuf.at[part * depth + i])
            if side is not None:
                corner, middle = outer(side, 1 + side)
            for j in range(cross):
                value = cut(own, j)
                if j < 2:
                    value = value + cut(south, j)
                if j >= breadth:
                    value = value + cut(north, j - breadth)
                if j == 0 or j == cross - 1:
                    loaded = hy[j // breadth, part, i]
                else:
                    loaded = tiles[pl.ds(j - 1, rhs, stride=breadth), :]
                value = spread(weights[(i + 1) * cross + j, 0]) * loaded + value
                if side is not None:
                    value = value + (cut(middle, j - 1) if 0 < j < cross - 1 else corner[j // breadth])
                first[(i + 2) * wide + j + 1] = value

        def outer(side, edge):
            block = 6 * side
            corner = [combine(block + 2 * end, [side_x[part, edge, end * (breadth + 1)]]) for end in range(2)]
            return corner, combine(block + 1, [side_x[part, edge, j + 1] for j in range(breadth)])

        def force_inner(i, carry):
            force_row(i)
            return carry

        halos((2, 3))
        lax.fori_loop(1, depth - 1, force_inner, 0)
        for side in range(2):
            force_row(side * (depth - 1), side)
        halos((0, 1))
        for side in range(2):
            x = side * (depth + 1) + 1
            corner, middle = outer(side, 3 * side)
            own = combine(4, [own_p[part, x - 1, j + 1] for j in range(breadth)])
            tiles = rows_of(hx.at[side, part])
            for j in range(breadth):
                value = cut(middle, j) + cut(own, j)
                if j == 0:
                    value = value + corner[0]
                if j == breadth - 1:
                    value = value + corner[1]
                loaded = tiles[pl.ds(j, rhs, stride=breadth), :]
                value = spread(weights[(x - 1) * cross + j + 1, 0]) * loaded + value
                first[x * wide + j + 2] = value

        source, target, spare = first, second, third
        for n in range(len(rates) - 1):
            def relax(x, source=source, target=target, n=n):
                for j in range(cross):
                    cell = x * wide + j + 1
                    target[cell] = first[cell] + beside(source, n, x, j + 1)

            in_groups(1, depth + 2, relax)
            source, target, spare = target, spare, target

        def finish(x):
            fine = combine(9, [phis[part, x - 2, j] for j in range(breadth)])
            row = part * depth + x - 2
            tiles = rows_of(obuf.at[row])
            for j in range(breadth):
                value = cut(fine, j) + first[x * wide + j + 2]
                value = value + beside(source, len(rates) - 1, x, j + 2)
                tiles[pl.ds(j, rhs, stride=breadth), :] = value
            pltpu.make_async_copy(obuf.at[row], out.at[:, part, x - 2], out_sem).start()

        in_groups(2, depth, finish)
        return carry

    lax.fori_loop(0, parts, component, 0)
    panels_all.wait_send()
    for sends, _, copy in started:
        pl.when(sends)(copy.wait_send)
    for part in range(parts):
        for way in range(4):
            pl.when(can(*ways[way]))(res_copy(way, part).wait_send)
    pltpu.make_async_copy(obuf, obuf, out_sem).wait()


def deliver_kernel(chunks, solved, field, mine, out, held, in_sem, out_sem):
    rows = held.shape[0] // chunks
    for i in range(chunks):
        part = pl.ds(i * rows, rows)
        pltpu.make_async_copy(field.at[part], held.at[part], in_sem.at[i]).start()
    mine[...] = solved[...]
    for i in range(chunks):
        part = pl.ds(i * rows, rows)
        pltpu.make_async_copy(field.at[part], held.at[part], in_sem.at[i]).wait()
        pltpu.make_async_copy(held.at[part], out.at[part], out_sem).start()
    pltpu.make_async_copy(held, out, out_sem).wait()


def deliver(solved, field):
    chunks = 8 if field.shape[0] % 8 == 0 else 1
    vmem = pl.BlockSpec(memory_space=pltpu.VMEM)
    hbm = pl.BlockSpec(memory_space=pl.ANY)
    return pl.pallas_call(
        functools.partial(deliver_kernel, chunks),
        out_shape=(
            jax.ShapeDtypeStruct(solved.shape, solved.dtype),
            jax.ShapeDtypeStruct(field.shape, field.dtype),
        ),
        in_specs=[vmem, hbm],
        out_specs=(vmem, hbm),
        scratch_shapes=[
            pltpu.VMEM(field.shape, field.dtype),
            pltpu.SemaphoreType.DMA((chunks,)),
            pltpu.SemaphoreType.DMA,
        ],
        compiler_params=pltpu.CompilerParams(vmem_limit_bytes=60 * 1024 * 1024),
    )(solved, field)


def on_device(residuals, vectors, phases, stiffness):
    count_x = lax.axis_size("gx")
    count_y = lax.axis_size("yz")
    rhs, parts, depth, breadth, length = residuals.shape
    width = vectors.shape[0]
    count = count_x * count_y
    scale_all, rates = sweep_rates(SWEEPS, 0.8)
    vmem = pl.BlockSpec(memory_space=pltpu.VMEM)
    hbm = pl.BlockSpec(memory_space=pl.ANY)
    panel = (width, 3 * count_y * width + rhs)
    cells = (depth + 2) * (breadth + 2)
    field = pltpu.VMEM(((depth + 4) * (breadth + 4), rhs, length), jnp.float32)
    slots = 16 + 4 * parts
    f32, half = jnp.float32, jnp.bfloat16
    solved, field_out = pl.pallas_call(
        functools.partial(kernel, count_x, count_y, scale_all, rates),
        out_shape=(
            jax.ShapeDtypeStruct((width, rhs), f32),
            jax.ShapeDtypeStruct(residuals.shape, f32),
        ),
        in_specs=[pl.BlockSpec(memory_space=pltpu.SMEM), vmem, hbm, hbm],
        out_specs=(vmem, hbm),
        scratch_shapes=[
            pltpu.VMEM((parts + 1, depth + 4, breadth + 4, width, length), f32),
            pltpu.VMEM((parts * depth, width, breadth, length), f32),
            pltpu.VMEM((parts * depth, rhs, breadth, length), f32),
            pltpu.VMEM((2, parts, rhs, breadth, length), f32),
            pltpu.VMEM((2, parts, depth, rhs, length), f32),
            pltpu.VMEM((2, parts, depth, rhs, length), f32),
            pltpu.VMEM((parts * depth, rhs, breadth, length), f32),
            pltpu.VMEM((depth * breadth, length), f32),
            pltpu.VMEM((2, 2, depth, length), f32),
            pltpu.VMEM((2, 2 * breadth, length), f32),
            pltpu.VMEM((2, 2, depth, length), f32),
            pltpu.VMEM((cells, 8, width, length), f32),
            pltpu.VMEM((SWEEPS - 1, cells, 6, width, length), f32),
            pltpu.VMEM((parts, depth + 2, breadth + 2, 2 * width, length), half),
            pltpu.VMEM((parts, depth, 4, 2 * width, length), half),
            pltpu.VMEM((parts, 4, breadth + 2, 2 * width, length), half),
            pltpu.VMEM((parts, depth, breadth, 2 * width, length), half),
            pltpu.VMEM((10, rhs, 4 * width), half),
            pltpu.VMEM(panel, f32),
            pltpu.VMEM((count,) + panel, f32),
            pltpu.VMEM((count * width, rhs), f32),
            field, field, field,
            pltpu.SemaphoreType.DMA,
            pltpu.SemaphoreType.DMA,
            pltpu.SemaphoreType.DMA,
            pltpu.SemaphoreType.DMA,
            pltpu.SemaphoreType.DMA,
            pltpu.SemaphoreType.DMA((slots,)),
            pltpu.SemaphoreType.DMA((slots,)),
        ],
        compiler_params=pltpu.CompilerParams(
            collective_id=0, has_side_effects=True, vmem_limit_bytes=60 * 1024 * 1024
        ),
    )(stiffness, phases, vectors, residuals)
    return deliver(solved, field_out)


def solution(mesh):
    return jax.shard_map(
        on_device,
        mesh=mesh,
        in_specs=(
            P(None, None, "gx", "yz", None),
            P(None, None, "gx", "yz", None),
            P("gx", "yz", None),
            P(),
        ),
        out_specs=(P(("gx", "yz"), None), P(None, None, "gx", "yz", None)),
        check_vma=False,
    )
```

```python
import functools

import jax
import jax.numpy as jnp
from jax import lax
from jax.experimental import pallas as pl
from jax.experimental.pallas import tpu as pltpu
from jax.sharding import PartitionSpec as P

SWEEPS = 4


HIGH = lax.Precision.HIGHEST


MESH = pl.DeviceIdType.MESH


def eliminate(rows, size, group):
    sublane = lax.broadcasted_iota(jnp.int32, rows[0].shape, 0)
    rows = list(rows)
    for base in range(0, size, group):
        columns = [
            [jnp.broadcast_to(a[:, base + j : base + j + 1], a.shape) for j in range(group)] for a in rows
        ]
        for j in range(group):
            p = base + j
            here = sublane == p
            for i, a in enumerate(rows):
                own = columns[i][j]
                inverse = 1.0 / own[p : p + 1, :]
                pivot = a[p : p + 1, :] * inverse
                for k in range(j + 1, group):
                    c = columns[i][k]
                    step = c[p : p + 1, :] * inverse
                    columns[i][k] = jnp.where(here, step, c - own * step)
                rows[i] = jnp.where(here, pivot, a - own * pivot)
    return rows


def product(a, b):
    return jnp.dot(a, b, precision=HIGH, preferred_element_type=jnp.float32)


def cyclic_solve(rows, size):
    count = len(rows)
    width = rows[0].shape[1]
    lane = lax.broadcasted_iota(jnp.int32, rows[0].shape, 1)
    is_own = lane < size
    is_low = (lane >= size) & (lane < 2 * size)
    is_high = (lane >= 2 * size) & (lane < 3 * size)
    is_rhs = lane >= 3 * size
    live = list(range(count))
    system = dict(enumerate(rows))
    levels = []
    while len(live) > 1:
        out = live[1::2]
        kept = live[0::2]
        solved = dict(zip(out, eliminate([system[i] for i in out], size, 4 if len(out) > 2 else 8)))
        fresh = {}
        for place, i in enumerate(kept):
            a = system[i]
            total = jnp.where(is_own | is_rhs, a, 0.0)
            if place > 0:
                t = product(a[:, size : 2 * size], solved[out[place - 1]])
                shifted = pltpu.roll(t, width - 2 * size, 1)
                total = total - jnp.where(is_own, shifted, jnp.where(is_low | is_rhs, t, 0.0))
            if place < len(out):
                t = product(a[:, 2 * size : 3 * size], solved[out[place]])
                shifted = pltpu.roll(t, width - size, 1)
                total = total - jnp.where(is_own, shifted, jnp.where(is_high | is_rhs, t, 0.0))
            fresh[i] = total
        levels.append((live, out, solved))
        system = fresh
        live = kept
    last = eliminate([system[live[0]]], size, 8)[0]
    answer = {live[0]: last[:, 3 * size :]}
    for before, out, solved in reversed(levels):
        for i in out:
            a = solved[i]
            place = before.index(i)
            x = a[:, 3 * size :] - product(a[:, size : 2 * size], answer[before[place - 1]])
            if place + 1 < len(before):
                x = x - product(a[:, 2 * size : 3 * size], answer[before[place + 1]])
            answer[i] = x
    return [answer[i] for i in range(count)]


WEST, EAST, SOUTH, NORTH, LOW, HIGH_Z = range(1, 7)


def sweep_rates(sweeps, damping):
    powers = [0.0] * sweeps
    term = [1.0]
    for _ in range(sweeps):
        for i, value in enumerate(term):
            powers[i] += value
        longer = [0.0] * (len(term) + 1)
        for i, value in enumerate(term):
            longer[i] += (1.0 - damping) * value
            longer[i + 1] += damping * value
        term = longer
    return damping * powers[0], [powers[i] / powers[i - 1] for i in range(sweeps - 1, 0, -1)]


def packed(v):
    coarse = v.astype(jnp.bfloat16).astype(jnp.float32)
    return jnp.concatenate([coarse, v - coarse], axis=0).astype(jnp.bfloat16)


def kernel(
    count_x, count_y, scale_all, rates,
    stiffness, phases, vectors, res,
    mine, out,
    ext, vraw, rbuf, hx, hy, ybuf, obuf, mown, msend, mx, my,
    weights, hweights, own_p, side_y, side_x, phis, lhs,
    panel, gathered, coeffs, first, second, third,
    load_sem, res_sem, out_sem, panel_send, panel_recv, halo_send, halo_recv
):
    index_x = lax.axis_index("gx")
    index_y = lax.axis_index("yz")
    count = count_x * count_y
    me = index_x * count_y + index_y
    rhs, parts, depth, breadth, length = res.shape
    width = vectors.shape[0]
    levels = stiffness.shape[0]
    wide = breadth + 4
    cross = breadth + 2
    barrier = pltpu.get_barrier_semaphore()
    zero = jnp.zeros((width, length), jnp.float32)
    tall = jnp.zeros((rhs, length), jnp.float32)

    def rows_of(ref):
        return ref.reshape(ref.shape[0] * breadth, length)

    def load(i, carry):
        c = i // depth
        x = i - c * depth
        pltpu.make_async_copy(vectors.at[:, c, x], vraw.at[i], load_sem).start()
        return carry


    def clear_y(y, carry):
        for f in range(parts + 1):
            for x in (0, 1, depth + 2, depth + 3):
                ext[f, x, y] = zero
        return carry

    def clear_x(x, carry):
        for f in range(parts + 1):
            for y in (0, 1, breadth + 2, breadth + 3):
                ext[f, x + 2, y] = zero
        return carry

    lax.fori_loop(0, wide, clear_y, 0)
    lax.fori_loop(0, depth, clear_x, 0)
    mx[...] = jnp.zeros(mx.shape, jnp.float32)
    my[...] = jnp.zeros(my.shape, jnp.float32)

    def each_other(act):
        def along(g, carry):
            for h in range(count_y):
                pl.when(jnp.logical_or(g != index_x, h != index_y))(functools.partial(act, g, h))
            return carry

        lax.fori_loop(0, count_x, along, 0)

    def greet(g, h):
        pl.semaphore_signal(barrier, inc=1, device_id=(g, h), device_id_type=MESH)

    each_other(greet)
    lax.fori_loop(0, parts * depth, load, 0)

    def load_res(i, carry):
        c = i // depth
        x = i - c * depth
        pltpu.make_async_copy(res.at[:, c, x], rbuf.at[i], res_sem).start()
        return carry

    lax.fori_loop(0, parts * depth, load_res, 0)

    for x in range(depth):
        p = phases[x]
        m = jnp.zeros(p.shape, jnp.float32)
        for level in range(levels):
            m = jnp.where(p == level, stiffness[level], m)
        mown[pl.ds(x * breadth, breadth), :] = m
    for side in range(2):
        for layer in range(2):
            y = layer + side * (breadth - 2)
            msend[side, layer] = mown[pl.ds(y, depth, stride=breadth), :]

    def spread_own(x, carry):
        for y in range(breadth):
            row = mown[pl.ds(x * breadth + y, 1), :]
            ext[parts, x + 2, y + 2] = jnp.broadcast_to(row, (width, length))
        return carry

    lax.fori_loop(0, depth, spread_own, 0)
    pltpu.make_async_copy(vraw, vraw, load_sem).wait()

    def fill(i, carry):
        c = i // depth
        x = i - c * depth
        tiles = rows_of(vraw.at[i])
        for y in range(breadth):
            ext[c, x + 2, y + 2] = tiles[pl.ds(y, width, stride=breadth), :]
        return carry

    lax.fori_loop(0, parts * depth, fill, 0)
    pl.semaphore_wait(barrier, count - 1)

    def can(dx, dy):
        ok = index_x >= 0
        if dx:
            ok = index_x > 0 if dx < 0 else index_x < count_x - 1
        if dy:
            ok_y = index_y > 0 if dy < 0 else index_y < count_y - 1
            ok = jnp.logical_and(ok, ok_y) if dx else ok_y
        return ok

    def exchange(source, target, dx, dy, slot):
        return pltpu.make_async_remote_copy(
            src_ref=source,
            dst_ref=target,
            send_sem=halo_send.at[slot],
            recv_sem=halo_recv.at[slot],
            device_id=(index_x + dx, index_y + dy),
            device_id_type=MESH,
        )

    started = []

    def start(source, target, dx, dy):
        copy = exchange(source, target, dx, dy, len(started))
        pl.when(can(dx, dy))(copy.start)
        started.append((can(dx, dy), can(-dx, -dy), copy))

    def arrived(low, high):
        for _, receives, copy in started[low:high]:
            pl.when(receives)(copy.wait_recv)

    start(mown.at[pl.ds(0, 2 * breadth)], mx.at[1], -1, 0)
    start(mown.at[pl.ds((depth - 2) * breadth, 2 * breadth)], mx.at[0], 1, 0)
    start(msend.at[0], my.at[1], 0, -1)
    start(msend.at[1], my.at[0], 0, 1)

    field = pl.ds(0, parts)
    inner_x, inner_y = pl.ds(2, depth), pl.ds(2, breadth)

    def layer_down(step):
        start(ext.at[field, 2 + step, inner_y], ext.at[field, depth + 2 + step, inner_y], -1, 0)

    def layer_sides(step):
        start(ext.at[field, inner_x, 2 + step], ext.at[field, inner_x, breadth + 2 + step], 0, -1)
        start(ext.at[field, inner_x, breadth + 1 - step], ext.at[field, inner_x, 1 - step], 0, 1)

    def layer_up(step):
        start(ext.at[field, depth + 1 - step, inner_y], ext.at[field, 1 - step, inner_y], 1, 0)

    for x, dx, to_x in ((2, -1, depth + 2), (depth + 1, 1, 1)):
        for y, dy, to_y in ((2, -1, breadth + 2), (breadth + 1, 1, 1)):
            start(ext.at[:, x, y], ext.at[:, to_x, to_y], dx, dy)
    layer_down(0)
    layer_sides(0)

    base_slot = len(started) + 5
    ways = ((-1, 0), (1, 0), (0, -1), (0, 1))

    def res_copy(way, part):
        dx, dy = ways[way]
        if dx:
            source, target = res.at[:, part, 0 if dx < 0 else depth - 1], hx.at[1 - way, part]
        else:
            source, target = ybuf.at[way - 2, part], hy.at[3 - way, part]
        return exchange(source, target, dx, dy, base_slot + part * 4 + way)

    def send_res(begin, end, which):
        for part in range(begin, end):
            for way in which:
                pl.when(can(*ways[way]))(res_copy(way, part).start)

    layer_up(0)
    layer_down(1)
    layer_sides(1)
    layer_up(1)
    pltpu.make_async_copy(rbuf, rbuf, res_sem).wait()

    def loads(i, sums):
        f = i // depth
        x = i - f * depth
        tiles = rows_of(rbuf.at[i])
        for side in range(2):
            ybuf[side, f, x] = tiles[pl.ds(side * (breadth - 1), rhs, stride=breadth), :]
        for y in range(breadth):
            v = ext[f, x + 2, y + 2]
            sums = tuple(
                total + v * tiles[pl.ds(r * breadth + y, 1), :] for r, total in enumerate(sums)
            )
        return sums

    sums = lax.fori_loop(0, parts * depth, loads, (zero,) * rhs)
    send_res(0, parts, (2, 3))
    lane = lax.broadcasted_iota(jnp.int32, panel.shape, 1)

    def placed(total, at):
        return jnp.where(lane == at, jnp.sum(total, axis=1, keepdims=True), 0.0)

    size = count_y * width
    row = jnp.zeros(panel.shape, jnp.float32)
    for r in range(rhs):
        row = row + placed(sums[r], 3 * size + r)

    arrived(0, 4)

    def spread_x(y, carry):
        for side in range(2):
            for step in range(2):
                line = mx[side, pl.ds(step * breadth + y, 1), :]
                ext[parts, side * (depth + 2) + step, y + 2] = jnp.broadcast_to(line, (width, length))
        return carry

    def spread_y(x, carry):
        for side in range(2):
            for step in range(2):
                line = my[side, step, pl.ds(x, 1), :]
                ext[parts, x + 2, side * (breadth + 2) + step] = jnp.broadcast_to(line, (width, length))
        return carry

    lax.fori_loop(0, breadth, spread_x, 0)
    lax.fori_loop(0, depth, spread_y, 0)
    arrived(4, 8)
    z = lax.broadcasted_iota(jnp.int32, (width, length), 1)

    def weigh(i, carry):
        inside = jnp.where(jnp.logical_or(i == 0, i == depth + 1), 0.0, 1.0).astype(jnp.float32)
        for j in range(cross):
            x, y = i + 1, j + 1
            m = ext[parts, x, y]
            low = 0.5 * (m + jnp.where(z > 0, pltpu.roll(m, 1, 1), 0.0))
            high = 0.5 * (m + jnp.where(z < length - 1, pltpu.roll(m, length - 1, 1), 0.0))
            west = 0.5 * (m + ext[parts, x - 1, y])
            east = 0.5 * (m + ext[parts, x + 1, y])
            south = 0.5 * (m + ext[parts, x, y - 1])
            north = 0.5 * (m + ext[parts, x, y + 1])
            diagonal = 0.002 + west + east + south + north + low + high
            inverse = jnp.where(m > 0, 1.0, 0.0) / diagonal
            if j == 0 or j == cross - 1:
                inverse = inverse * inside
            at = i * cross + j
            weights[at, 0] = scale_all * inverse
            weights[at, WEST] = inverse * west
            weights[at, EAST] = inverse * east
            weights[at, SOUTH] = inverse * south
            weights[at, NORTH] = inverse * north
            weights[at, LOW] = jnp.where(z > 0, inverse * low, 0.0)
            weights[at, HIGH_Z] = jnp.where(z < length - 1, inverse * high, 0.0)
            weights[at, 7] = diagonal
        return carry

    lax.fori_loop(0, depth + 2, weigh, 0)

    def gram(sums, left, f, x, y):
        return tuple(
            total + left * ext[f, x, y, pl.ds(l, 1), :] for l, total in enumerate(sums)
        )

    def own_block(i, sums):
        inside_x = (
            jnp.where(i > 0, 1.0, 0.0).astype(jnp.float32),
            jnp.where(i < depth - 1, 1.0, 0.0).astype(jnp.float32),
        )
        x = i + 2
        x_low = jnp.maximum(i - 1, 0) + 2
        x_high = jnp.minimum(i + 1, depth - 1) + 2
        for y in range(2, breadth + 2):
            at = (i + 1) * cross + y - 1
            west = weights[at, WEST] * inside_x[0]
            east = weights[at, EAST] * inside_x[1]
            for f in range(parts):
                v = ext[f, x, y]
                near = west * ext[f, x_low, y] + east * ext[f, x_high, y]
                if y > 2:
                    near = near + weights[at, SOUTH] * ext[f, x, y - 1]
                if y < breadth + 1:
                    near = near + weights[at, NORTH] * ext[f, x, y + 1]
                near = near + weights[at, LOW] * pltpu.roll(v, 1, 1)
                near = near + weights[at, HIGH_Z] * pltpu.roll(v, length - 1, 1)
                own_p[f, i + 1, y - 1] = packed(near - v)
                phis[f, i, y - 2] = packed(v)
                sums = gram(sums, weights[at, 7] * (v - near), f, x, y)
        return sums

    def side_block(along, fixed_x, fixed_y, dx, dy, turned=False):
        which = {(-1, 0): WEST, (1, 0): EAST, (0, -1): SOUTH, (0, 1): NORTH}[(dx, dy)]

        def one(i, sums):
            x = i + 2 if fixed_x is None else fixed_x
            y = i + 2 if fixed_y is None else fixed_y
            at = (x - 1) * cross + y - 1
            weight = weights[at, which] * weights[at, 7]
            for f in range(parts):
                if turned:
                    sums = gram(sums, -weight * ext[f, x + dx, y + dy], f, x, y)
                else:
                    sums = gram(sums, -weight * ext[f, x, y], f, x + dx, y + dy)
            return sums

        return lax.fori_loop(0, along, one, (zero,) * width)

    def put(row, totals, at):
        for l in range(width):
            row = row + placed(totals[l], at + l)
        return row

    row = put(row, lax.fori_loop(0, depth, own_block, (zero,) * width), index_y * width)
    arrived(8, 11)
    row = put(row, side_block(depth, None, 2, 0, -1), (index_y - 1) * width)
    row = put(row, side_block(depth, None, breadth + 1, 0, 1), (index_y + 1) * width)
    row = put(row, side_block(breadth, depth + 1, None, 1, 0, True), size + index_y * width)
    row = put(row, side_block(breadth, depth + 1, None, 1, 0), 2 * size + index_y * width)
    panel[...] = row
    gathered[me] = row

    def send(g, h):
        pltpu.make_async_remote_copy(
            src_ref=panel,
            dst_ref=gathered.at[me],
            send_sem=panel_send,
            recv_sem=panel_recv,
            device_id=(g, h),
            device_id_type=MESH,
        ).start()

    each_other(send)
    send_res(0, parts, (0, 1))

    def no_halo(way):
        dx, dy = ways[way]

        def wipe_x():
            hx[way] = jnp.zeros(hx.shape[1:], jnp.float32)

        def wipe_y():
            hy[way - 2] = jnp.zeros(hy.shape[1:], jnp.float32)

        pl.when(jnp.logical_not(can(dx, dy)))(wipe_x if dx else wipe_y)

    for way in range(4):
        no_halo(way)

    def multiples(i, carry):
        for j in range(cross):
            at = i * cross + j
            for q in range(WEST, HIGH_Z + 1):
                w = weights[at, q]
                for n, rate in enumerate(rates):
                    hweights[n, at, q - 1] = rate * w
        return carry

    lax.fori_loop(0, depth + 2, multiples, 0)

    def reach(f, at, which, x, y):
        return packed(weights[at, which] * ext[f, x, y])

    arrived(11, 12)

    def seams_x(i, carry):
        y = i + 2
        for f in range(parts):
            side_x[f, 1, i + 1] = reach(f, cross + i + 1, WEST, 1, y)
            side_x[f, 2, i + 1] = reach(f, depth * cross + i + 1, EAST, depth + 2, y)
            own_p[f, 0, i + 1] = reach(f, i + 1, EAST, 2, y)
            own_p[f, depth + 1, i + 1] = reach(f, (depth + 1) * cross + i + 1, WEST, depth + 1, y)
        return carry

    def seams_y(i, carry):
        x = i + 2
        at = (i + 1) * cross
        for f in range(parts):
            side_y[f, i, 1] = reach(f, at + 1, SOUTH, x, 1)
            side_y[f, i, 2] = reach(f, at + breadth, NORTH, x, breadth + 2)
            own_p[f, i + 1, 0] = reach(f, at, NORTH, x, 2)
            own_p[f, i + 1, breadth + 1] = reach(f, at + breadth + 1, SOUTH, x, breadth + 1)
        return carry

    lax.fori_loop(0, breadth, seams_x, 0)
    lax.fori_loop(0, depth, seams_y, 0)

    for buffer in (first, second, third):
        def clear_row(y, carry, buffer=buffer):
            buffer[y] = tall
            buffer[(depth + 3) * wide + y] = tall
            return carry

        def clear_column(x, carry, buffer=buffer):
            buffer[x * wide] = tall
            buffer[x * wide + wide - 1] = tall
            return carry

        lax.fori_loop(0, wide, clear_row, 0)
        lax.fori_loop(0, depth + 4, clear_column, 0)
    for x in (1, depth + 2):
        for y in (1, breadth + 2):
            first[x * wide + y] = tall

    arrived(12, 16)
    for f in range(parts):
        for slot, at_low, at_high, way, x in (
            (0, 1, breadth, None, 1), (1, cross, cross + breadth + 1, WEST, 1),
            (2, depth * cross, depth * cross + breadth + 1, EAST, depth + 2),
            (3, (depth + 1) * cross + 1, (depth + 1) * cross + breadth, None, depth + 2),
        ):
            side_x[f, slot, 0] = reach(f, at_low, way or SOUTH, x, 1)
            side_x[f, slot, breadth + 1] = reach(f, at_high, way or NORTH, x, breadth + 2)

    def bounds(i, last):
        return (
            jnp.where(i > 0, 1.0, 0.0).astype(jnp.float32),
            jnp.where(i < last, 1.0, 0.0).astype(jnp.float32),
        )

    def halo_term(f, at, x, y, terms):
        v = ext[f, x, y]
        near = weights[at, LOW] * pltpu.roll(v, 1, 1)
        near = near + weights[at, HIGH_Z] * pltpu.roll(v, length - 1, 1)
        for weight, px, py in terms:
            near = near + weight * ext[f, px, py]
        return packed(near - v)

    def rims_x(i, carry):
        y = i + 2
        low, high = bounds(i, breadth - 1)
        for slot, x, outward, px in ((0, 1, WEST, 0), (3, depth + 2, EAST, depth + 3)):
            at = (x - 1) * cross + i + 1
            terms = (
                (weights[at, outward], px, y),
                (weights[at, SOUTH] * low, x, y - 1),
                (weights[at, NORTH] * high, x, y + 1),
            )
            for f in range(parts):
                side_x[f, slot, i + 1] = halo_term(f, at, x, y, terms)
        return carry

    def rims_y(i, carry):
        x = i + 2
        low, high = bounds(i, depth - 1)
        for slot, y, outward, py in ((0, 1, SOUTH, 0), (3, breadth + 2, NORTH, breadth + 3)):
            at = (i + 1) * cross + y - 1
            terms = (
                (weights[at, outward], x, py),
                (weights[at, WEST] * low, x - 1, y),
                (weights[at, EAST] * high, x + 1, y),
            )
            for f in range(parts):
                side_y[f, i, slot] = halo_term(f, at, x, y, terms)
        return carry

    lax.fori_loop(0, breadth, rims_x, 0)
    lax.fori_loop(0, depth, rims_y, 0)

    everyone = gathered.at[pl.ds(0, count - 1)]
    panels_all = pltpu.make_async_remote_copy(
        src_ref=everyone,
        dst_ref=everyone,
        send_sem=panel_send,
        recv_sem=panel_recv,
        device_id=(lax.rem(index_x + 1, count_x), index_y),
        device_id_type=MESH,
    )
    panels_all.wait_recv()
    panels = [gathered[pl.ds(g * count_y, count_y)].reshape(size, panel.shape[1]) for g in range(count_x)]
    spot = lax.broadcasted_iota(jnp.int32, panels[0].shape, 1)
    is_low = (spot >= size) & (spot < 2 * size)
    below = [jnp.zeros(panels[0].shape, jnp.float32)] + panels[:-1]
    panels = [jnp.where(is_low, b, p) for b, p in zip(below, panels)]
    for g, x in enumerate(cyclic_solve(panels, size)):
        coeffs[pl.ds(g * size, size), :] = x
    mine[...] = coeffs[pl.ds(pl.multiple_of(me * width, width), width), :]

    for slot in range(10):
        step_x, step_y = (slot // 3 - 1, slot % 3 - 1) if slot < 9 else (0, 0)
        near_x = jnp.clip(index_x + step_x, 0, count_x - 1)
        near_y = jnp.clip(index_y + step_y, 0, count_y - 1)
        begin = pl.multiple_of((near_x * count_y + near_y) * width, width)
        c = coeffs[pl.ds(begin, width), :]
        if slot < 9:
            c = scale_all * c
        coarse = c.astype(jnp.bfloat16).astype(jnp.float32)
        fine = c - coarse
        lhs[slot] = jnp.concatenate([coarse, coarse, fine, fine], axis=0).T.astype(jnp.bfloat16)

    def combine(slot, cells):
        block = jnp.concatenate(cells, axis=1)
        return jnp.dot(
            lhs[slot], jnp.concatenate([block, block], axis=0), preferred_element_type=jnp.float32
        )

    def cut(block, i):
        return block[:, i * length : (i + 1) * length]

    def spread(w):
        return jnp.concatenate([w] * (rhs // width), axis=0)

    def beside(source, n, x, y):
        cell = x * wide + y
        at = (x - 1) * cross + y - 1
        centre = source[cell]
        total = spread(hweights[n, at, 0]) * source[cell - wide]
        total = total + spread(hweights[n, at, 1]) * source[cell + wide]
        total = total + spread(hweights[n, at, 2]) * source[cell - 1]
        total = total + spread(hweights[n, at, 3]) * source[cell + 1]
        total = total + spread(hweights[n, at, 4]) * pltpu.roll(centre, 1, 1)
        total = total + spread(hweights[n, at, 5]) * pltpu.roll(centre, length - 1, 1)
        return total

    def in_groups(start, rows, act):
        step = next(k for k in (5, 4, 3, 2, 1) if rows % k == 0)

        def some(i, carry):
            for k in range(step):
                act(start + step * i + k)
            return carry

        lax.fori_loop(0, rows // step, some, 0)

    def component(part, carry):
        def halos(which):
            for way in which:
                dx, dy = ways[way]
                pl.when(can(-dx, -dy))(res_copy(way, part).wait_recv)

        def force_row(i, side=None):
            own = combine(4, [own_p[part, i + 1, j] for j in range(cross)])
            south = combine(3, [side_y[part, i, j] for j in (0, 1)])
            north = combine(5, [side_y[part, i, j] for j in (2, 3)])
            tiles = rows_of(rbuf.at[part * depth + i])
            if side is not None:
                corner, middle = outer(side, 1 + side)
            for j in range(cross):
                value = cut(own, j)
                if j < 2:
                    value = value + cut(south, j)
                if j >= breadth:
                    value = value + cut(north, j - breadth)
                if j == 0 or j == cross - 1:
                    loaded = hy[j // breadth, part, i]
                else:
                    loaded = tiles[pl.ds(j - 1, rhs, stride=breadth), :]
                value = spread(weights[(i + 1) * cross + j, 0]) * loaded + value
                if side is not None:
                    value = value + (cut(middle, j - 1) if 0 < j < cross - 1 else corner[j // breadth])
                first[(i + 2) * wide + j + 1] = value

        def outer(side, edge):
            block = 6 * side
            corner = [combine(block + 2 * end, [side_x[part, edge, end * (breadth + 1)]]) for end in range(2)]
            return corner, combine(block + 1, [side_x[part, edge, j + 1] for j in range(breadth)])

        def force_inner(i, carry):
            force_row(i)
            return carry

        halos((2, 3))
        lax.fori_loop(1, depth - 1, force_inner, 0)
        for side in range(2):
            force_row(side * (depth - 1), side)
        halos((0, 1))
        for side in range(2):
            x = side * (depth + 1) + 1
            corner, middle = outer(side, 3 * side)
            own = combine(4, [own_p[part, x - 1, j + 1] for j in range(breadth)])
            tiles = rows_of(hx.at[side, part])
            for j in range(breadth):
                value = cut(middle, j) + cut(own, j)
                if j == 0:
                    value = value + corner[0]
                if j == breadth - 1:
                    value = value + corner[1]
                loaded = tiles[pl.ds(j, rhs, stride=breadth), :]
                value = spread(weights[(x - 1) * cross + j + 1, 0]) * loaded + value
                first[x * wide + j + 2] = value

        source, target, spare = first, second, third
        for n in range(len(rates) - 1):
            def relax(x, source=source, target=target, n=n):
                for j in range(cross):
                    cell = x * wide + j + 1
                    target[cell] = first[cell] + beside(source, n, x, j + 1)

            in_groups(1, depth + 2, relax)
            source, target, spare = target, spare, target

        def finish(x):
            fine = combine(9, [phis[part, x - 2, j] for j in range(breadth)])
            row = part * depth + x - 2
            tiles = rows_of(obuf.at[row])
            for j in range(breadth):
                value = cut(fine, j) + first[x * wide + j + 2]
                value = value + beside(source, len(rates) - 1, x, j + 2)
                tiles[pl.ds(j, rhs, stride=breadth), :] = value
            pltpu.make_async_copy(obuf.at[row], out.at[:, part, x - 2], out_sem).start()

        in_groups(2, depth, finish)
        return carry

    lax.fori_loop(0, parts, component, 0)
    panels_all.wait_send()
    for sends, _, copy in started:
        pl.when(sends)(copy.wait_send)
    for part in range(parts):
        for way in range(4):
            pl.when(can(*ways[way]))(res_copy(way, part).wait_send)
    pltpu.make_async_copy(obuf, obuf, out_sem).wait()


def deliver_kernel(chunks, solved, field, mine, out, held, in_sem, out_sem):
    rows = held.shape[0] // chunks
    for i in range(chunks):
        part = pl.ds(i * rows, rows)
        pltpu.make_async_copy(field.at[part], held.at[part], in_sem.at[i]).start()
    mine[...] = solved[...]
    for i in range(chunks):
        part = pl.ds(i * rows, rows)
        pltpu.make_async_copy(field.at[part], held.at[part], in_sem.at[i]).wait()
        pltpu.make_async_copy(held.at[part], out.at[part], out_sem).start()
    pltpu.make_async_copy(held, out, out_sem).wait()


def deliver(solved, field):
    chunks = 8 if field.shape[0] % 8 == 0 else 1
    vmem = pl.BlockSpec(memory_space=pltpu.VMEM)
    hbm = pl.BlockSpec(memory_space=pl.ANY)
    return pl.pallas_call(
        functools.partial(deliver_kernel, chunks),
        out_shape=(
            jax.ShapeDtypeStruct(solved.shape, solved.dtype),
            jax.ShapeDtypeStruct(field.shape, field.dtype),
        ),
        in_specs=[vmem, hbm],
        out_specs=(vmem, hbm),
        scratch_shapes=[
            pltpu.VMEM(field.shape, field.dtype),
            pltpu.SemaphoreType.DMA((chunks,)),
            pltpu.SemaphoreType.DMA,
        ],
        compiler_params=pltpu.CompilerParams(vmem_limit_bytes=60 * 1024 * 1024),
    )(solved, field)


def on_device(residuals, vectors, phases, stiffness):
    count_x = lax.axis_size("gx")
    count_y = lax.axis_size("yz")
    rhs, parts, depth, breadth, length = residuals.shape
    width = vectors.shape[0]
    count = count_x * count_y
    scale_all, rates = sweep_rates(SWEEPS, 0.8)
    vmem = pl.BlockSpec(memory_space=pltpu.VMEM)
    hbm = pl.BlockSpec(memory_space=pl.ANY)
    panel = (width, 3 * count_y * width + rhs)
    cells = (depth + 2) * (breadth + 2)
    field = pltpu.VMEM(((depth + 4) * (breadth + 4), rhs, length), jnp.float32)
    slots = 16 + 4 * parts
    f32, half = jnp.float32, jnp.bfloat16
    solved, field_out = pl.pallas_call(
        functools.partial(kernel, count_x, count_y, scale_all, rates),
        out_shape=(
            jax.ShapeDtypeStruct((width, rhs), f32),
            jax.ShapeDtypeStruct(residuals.shape, f32),
        ),
        in_specs=[pl.BlockSpec(memory_space=pltpu.SMEM), vmem, hbm, hbm],
        out_specs=(vmem, hbm),
        scratch_shapes=[
            pltpu.VMEM((parts + 1, depth + 4, breadth + 4, width, length), f32),
            pltpu.VMEM((parts * depth, width, breadth, length), f32),
            pltpu.VMEM((parts * depth, rhs, breadth, length), f32),
            pltpu.VMEM((2, parts, rhs, breadth, length), f32),
            pltpu.VMEM((2, parts, depth, rhs, length), f32),
            pltpu.VMEM((2, parts, depth, rhs, length), f32),
            pltpu.VMEM((parts * depth, rhs, breadth, length), f32),
            pltpu.VMEM((depth * breadth, length), f32),
            pltpu.VMEM((2, 2, depth, length), f32),
            pltpu.VMEM((2, 2 * breadth, length), f32),
            pltpu.VMEM((2, 2, depth, length), f32),
            pltpu.VMEM((cells, 8, width, length), f32),
            pltpu.VMEM((SWEEPS - 1, cells, 6, width, length), f32),
            pltpu.VMEM((parts, depth + 2, breadth + 2, 2 * width, length), half),
            pltpu.VMEM((parts, depth, 4, 2 * width, length), half),
            pltpu.VMEM((parts, 4, breadth + 2, 2 * width, length), half),
            pltpu.VMEM((parts, depth, breadth, 2 * width, length), half),
            pltpu.VMEM((10, rhs, 4 * width), half),
            pltpu.VMEM(panel, f32),
            pltpu.VMEM((count,) + panel, f32),
            pltpu.VMEM((count * width, rhs), f32),
            field, field, field,
            pltpu.SemaphoreType.DMA,
            pltpu.SemaphoreType.DMA,
            pltpu.SemaphoreType.DMA,
            pltpu.SemaphoreType.DMA,
            pltpu.SemaphoreType.DMA,
            pltpu.SemaphoreType.DMA((slots,)),
            pltpu.SemaphoreType.DMA((slots,)),
        ],
        compiler_params=pltpu.CompilerParams(
            collective_id=0, has_side_effects=True, vmem_limit_bytes=60 * 1024 * 1024
        ),
    )(stiffness, phases, vectors, residuals)
    return deliver(solved, field_out)


def solution(mesh):
    return jax.shard_map(
        on_device,
        mesh=mesh,
        in_specs=(
            P(None, None, "gx", "yz", None),
            P(None, None, "gx", "yz", None),
            P("gx", "yz", None),
            P(),
        ),
        out_specs=(P(("gx", "yz"), None), P(None, None, "gx", "yz", None)),
        check_vma=False,
    )
```

```python
import functools

import jax
import jax.numpy as jnp
from jax import lax
from jax.experimental import pallas as pl
from jax.experimental.pallas import tpu as pltpu
from jax.sharding import PartitionSpec as P

SWEEPS = 4


HIGH = lax.Precision.HIGHEST


MESH = pl.DeviceIdType.MESH


def eliminate(rows, size, group):
    sublane = lax.broadcasted_iota(jnp.int32, rows[0].shape, 0)
    rows = list(rows)
    for base in range(0, size, group):
        columns = [
            [jnp.broadcast_to(a[:, base + j : base + j + 1], a.shape) for j in range(group)] for a in rows
        ]
        for j in range(group):
            p = base + j
            here = sublane == p
            for i, a in enumerate(rows):
                own = columns[i][j]
                inverse = 1.0 / own[p : p + 1, :]
                pivot = a[p : p + 1, :] * inverse
                for k in range(j + 1, group):
                    c = columns[i][k]
                    step = c[p : p + 1, :] * inverse
                    columns[i][k] = jnp.where(here, step, c - own * step)
                rows[i] = jnp.where(here, pivot, a - own * pivot)
    return rows


def product(a, b):
    return jnp.dot(a, b, precision=HIGH, preferred_element_type=jnp.float32)


def cyclic_solve(rows, size):
    count = len(rows)
    width = rows[0].shape[1]
    lane = lax.broadcasted_iota(jnp.int32, rows[0].shape, 1)
    is_own = lane < size
    is_low = (lane >= size) & (lane < 2 * size)
    is_high = (lane >= 2 * size) & (lane < 3 * size)
    is_rhs = lane >= 3 * size
    live = list(range(count))
    system = dict(enumerate(rows))
    levels = []
    while len(live) > 1:
        out = live[1::2]
        kept = live[0::2]
        solved = dict(zip(out, eliminate([system[i] for i in out], size, 4 if len(out) > 2 else 8)))
        fresh = {}
        for place, i in enumerate(kept):
            a = system[i]
            total = jnp.where(is_own | is_rhs, a, 0.0)
            if place > 0:
                t = product(a[:, size : 2 * size], solved[out[place - 1]])
                shifted = pltpu.roll(t, width - 2 * size, 1)
                total = total - jnp.where(is_own, shifted, jnp.where(is_low | is_rhs, t, 0.0))
            if place < len(out):
                t = product(a[:, 2 * size : 3 * size], solved[out[place]])
                shifted = pltpu.roll(t, width - size, 1)
                total = total - jnp.where(is_own, shifted, jnp.where(is_high | is_rhs, t, 0.0))
            fresh[i] = total
        levels.append((live, out, solved))
        system = fresh
        live = kept
    last = eliminate([system[live[0]]], size, 8)[0]
    answer = {live[0]: last[:, 3 * size :]}
    for before, out, solved in reversed(levels):
        for i in out:
            a = solved[i]
            place = before.index(i)
            x = a[:, 3 * size :] - product(a[:, size : 2 * size], answer[before[place - 1]])
            if place + 1 < len(before):
                x = x - product(a[:, 2 * size : 3 * size], answer[before[place + 1]])
            answer[i] = x
    return [answer[i] for i in range(count)]


WEST, EAST, SOUTH, NORTH, LOW, HIGH_Z = range(1, 7)


def sweep_rates(sweeps, damping):
    powers = [0.0] * sweeps
    term = [1.0]
    for _ in range(sweeps):
        for i, value in enumerate(term):
            powers[i] += value
        longer = [0.0] * (len(term) + 1)
        for i, value in enumerate(term):
            longer[i] += (1.0 - damping) * value
            longer[i + 1] += damping * value
        term = longer
    return damping * powers[0], [powers[i] / powers[i - 1] for i in range(sweeps - 1, 0, -1)]


def packed(v):
    coarse = v.astype(jnp.bfloat16).astype(jnp.float32)
    return jnp.concatenate([coarse, v - coarse], axis=0).astype(jnp.bfloat16)


def kernel(
    count_x, count_y, scale_all, rates,
    stiffness, phases, vectors, res,
    mine, out,
    ext, vraw, rbuf, hx, hy, ybuf, obuf, mown, msend, mx, my,
    weights, hweights, own_p, side_y, side_x, phis, lhs,
    panel, gathered, coeffs, first, second, third,
    load_sem, res_sem, out_sem, panel_send, panel_recv, halo_send, halo_recv
):
    index_x = lax.axis_index("gx")
    index_y = lax.axis_index("yz")
    count = count_x * count_y
    me = index_x * count_y + index_y
    rhs, parts, depth, breadth, length = res.shape
    width = vectors.shape[0]
    levels = stiffness.shape[0]
    wide = breadth + 4
    cross = breadth + 2
    barrier = pltpu.get_barrier_semaphore()
    zero = jnp.zeros((width, length), jnp.float32)
    tall = jnp.zeros((rhs, length), jnp.float32)

    def rows_of(ref):
        return ref.reshape(ref.shape[0] * breadth, length)

    def load(i, carry):
        c = i // depth
        x = i - c * depth
        pltpu.make_async_copy(vectors.at[:, c, x], vraw.at[i], load_sem).start()
        return carry


    def clear_y(y, carry):
        for f in range(parts + 1):
            for x in (0, 1, depth + 2, depth + 3):
                ext[f, x, y] = zero
        return carry

    def clear_x(x, carry):
        for f in range(parts + 1):
            for y in (0, 1, breadth + 2, breadth + 3):
                ext[f, x + 2, y] = zero
        return carry

    lax.fori_loop(0, wide, clear_y, 0)
    lax.fori_loop(0, depth, clear_x, 0)
    mx[...] = jnp.zeros(mx.shape, jnp.float32)
    my[...] = jnp.zeros(my.shape, jnp.float32)

    def each_other(act):
        def along(g, carry):
            for h in range(count_y):
                pl.when(jnp.logical_or(g != index_x, h != index_y))(functools.partial(act, g, h))
            return carry

        lax.fori_loop(0, count_x, along, 0)

    def greet(g, h):
        pl.semaphore_signal(barrier, inc=1, device_id=(g, h), device_id_type=MESH)

    each_other(greet)
    lax.fori_loop(0, parts * depth, load, 0)

    def load_res(i, carry):
        c = i // depth
        x = i - c * depth
        pltpu.make_async_copy(res.at[:, c, x], rbuf.at[i], res_sem).start()
        return carry

    lax.fori_loop(0, parts * depth, load_res, 0)

    for x in range(depth):
        p = phases[x]
        m = jnp.zeros(p.shape, jnp.float32)
        for level in range(levels):
            m = jnp.where(p == level, stiffness[level], m)
        mown[pl.ds(x * breadth, breadth), :] = m
    for side in range(2):
        for layer in range(2):
            y = layer + side * (breadth - 2)
            msend[side, layer] = mown[pl.ds(y, depth, stride=breadth), :]

    def spread_own(x, carry):
        for y in range(breadth):
            row = mown[pl.ds(x * breadth + y, 1), :]
            ext[parts, x + 2, y + 2] = jnp.broadcast_to(row, (width, length))
        return carry

    lax.fori_loop(0, depth, spread_own, 0)
    pltpu.make_async_copy(vraw, vraw, load_sem).wait()

    def fill(i, carry):
        c = i // depth
        x = i - c * depth
        tiles = rows_of(vraw.at[i])
        for y in range(breadth):
            ext[c, x + 2, y + 2] = tiles[pl.ds(y, width, stride=breadth), :]
        return carry

    lax.fori_loop(0, parts * depth, fill, 0)
    pl.semaphore_wait(barrier, count - 1)

    def can(dx, dy):
        ok = index_x >= 0
        if dx:
            ok = index_x > 0 if dx < 0 else index_x < count_x - 1
        if dy:
            ok_y = index_y > 0 if dy < 0 else index_y < count_y - 1
            ok = jnp.logical_and(ok, ok_y) if dx else ok_y
        return ok

    def exchange(source, target, dx, dy, slot):
        return pltpu.make_async_remote_copy(
            src_ref=source,
            dst_ref=target,
            send_sem=halo_send.at[slot],
            recv_sem=halo_recv.at[slot],
            device_id=(index_x + dx, index_y + dy),
            device_id_type=MESH,
        )

    started = []

    def start(source, target, dx, dy):
        copy = exchange(source, target, dx, dy, len(started))
        pl.when(can(dx, dy))(copy.start)
        started.append((can(dx, dy), can(-dx, -dy), copy))

    def arrived(low, high):
        for _, receives, copy in started[low:high]:
            pl.when(receives)(copy.wait_recv)

    start(mown.at[pl.ds(0, 2 * breadth)], mx.at[1], -1, 0)
    start(mown.at[pl.ds((depth - 2) * breadth, 2 * breadth)], mx.at[0], 1, 0)
    start(msend.at[0], my.at[1], 0, -1)
    start(msend.at[1], my.at[0], 0, 1)

    field = pl.ds(0, parts)
    inner_x, inner_y = pl.ds(2, depth), pl.ds(2, breadth)

    def layer_down(step):
        start(ext.at[field, 2 + step, inner_y], ext.at[field, depth + 2 + step, inner_y], -1, 0)

    def layer_sides(step):
        start(ext.at[field, inner_x, 2 + step], ext.at[field, inner_x, breadth + 2 + step], 0, -1)
        start(ext.at[field, inner_x, breadth + 1 - step], ext.at[field, inner_x, 1 - step], 0, 1)

    def layer_up(step):
        start(ext.at[field, depth + 1 - step, inner_y], ext.at[field, 1 - step, inner_y], 1, 0)

    for x, dx, to_x in ((2, -1, depth + 2), (depth + 1, 1, 1)):
        for y, dy, to_y in ((2, -1, breadth + 2), (breadth + 1, 1, 1)):
            start(ext.at[:, x, y], ext.at[:, to_x, to_y], dx, dy)
    layer_down(0)
    layer_sides(0)

    base_slot = len(started) + 5
    ways = ((-1, 0), (1, 0), (0, -1), (0, 1))

    def res_copy(way, part):
        dx, dy = ways[way]
        if dx:
            source, target = res.at[:, part, 0 if dx < 0 else depth - 1], hx.at[1 - way, part]
        else:
            source, target = ybuf.at[way - 2, part], hy.at[3 - way, part]
        return exchange(source, target, dx, dy, base_slot + part * 4 + way)

    def send_res(begin, end, which):
        for part in range(begin, end):
            for way in which:
                pl.when(can(*ways[way]))(res_copy(way, part).start)

    layer_up(0)
    layer_down(1)
    layer_sides(1)
    layer_up(1)
    pltpu.make_async_copy(rbuf, rbuf, res_sem).wait()

    def loads(i, sums):
        f = i // depth
        x = i - f * depth
        tiles = rows_of(rbuf.at[i])
        for side in range(2):
            ybuf[side, f, x] = tiles[pl.ds(side * (breadth - 1), rhs, stride=breadth), :]
        for y in range(breadth):
            v = ext[f, x + 2, y + 2]
            sums = tuple(
                total + v * tiles[pl.ds(r * breadth + y, 1), :] for r, total in enumerate(sums)
            )
        return sums

    sums = lax.fori_loop(0, parts * depth, loads, (zero,) * rhs)
    send_res(0, parts, (2, 3))
    lane = lax.broadcasted_iota(jnp.int32, panel.shape, 1)

    def placed(total, at):
        return jnp.where(lane == at, jnp.sum(total, axis=1, keepdims=True), 0.0)

    size = count_y * width
    row = jnp.zeros(panel.shape, jnp.float32)
    for r in range(rhs):
        row = row + placed(sums[r], 3 * size + r)

    arrived(0, 4)

    def spread_x(y, carry):
        for side in range(2):
            for step in range(2):
                line = mx[side, pl.ds(step * breadth + y, 1), :]
                ext[parts, side * (depth + 2) + step, y + 2] = jnp.broadcast_to(line, (width, length))
        return carry

    def spread_y(x, carry):
        for side in range(2):
            for step in range(2):
                line = my[side, step, pl.ds(x, 1), :]
                ext[parts, x + 2, side * (breadth + 2) + step] = jnp.broadcast_to(line, (width, length))
        return carry

    lax.fori_loop(0, breadth, spread_x, 0)
    lax.fori_loop(0, depth, spread_y, 0)
    arrived(4, 8)
    z = lax.broadcasted_iota(jnp.int32, (width, length), 1)

    def weigh(i, carry):
        inside = jnp.where(jnp.logical_or(i == 0, i == depth + 1), 0.0, 1.0).astype(jnp.float32)
        for j in range(cross):
            x, y = i + 1, j + 1
            m = ext[parts, x, y]
            low = 0.5 * (m + jnp.where(z > 0, pltpu.roll(m, 1, 1), 0.0))
            high = 0.5 * (m + jnp.where(z < length - 1, pltpu.roll(m, length - 1, 1), 0.0))
            west = 0.5 * (m + ext[parts, x - 1, y])
            east = 0.5 * (m + ext[parts, x + 1, y])
            south = 0.5 * (m + ext[parts, x, y - 1])
            north = 0.5 * (m + ext[parts, x, y + 1])
            diagonal = 0.002 + west + east + south + north + low + high
            inverse = jnp.where(m > 0, 1.0, 0.0) / diagonal
            if j == 0 or j == cross - 1:
                inverse = inverse * inside
            at = i * cross + j
            weights[at, 0] = scale_all * inverse
            weights[at, WEST] = inverse * west
            weights[at, EAST] = inverse * east
            weights[at, SOUTH] = inverse * south
            weights[at, NORTH] = inverse * north
            weights[at, LOW] = jnp.where(z > 0, inverse * low, 0.0)
            weights[at, HIGH_Z] = jnp.where(z < length - 1, inverse * high, 0.0)
            weights[at, 7] = diagonal
        return carry

    lax.fori_loop(0, depth + 2, weigh, 0)

    def gram(sums, left, f, x, y):
        return tuple(
            total + left * ext[f, x, y, pl.ds(l, 1), :] for l, total in enumerate(sums)
        )

    def own_block(i, sums):
        inside_x = (
            jnp.where(i > 0, 1.0, 0.0).astype(jnp.float32),
            jnp.where(i < depth - 1, 1.0, 0.0).astype(jnp.float32),
        )
        x = i + 2
        x_low = jnp.maximum(i - 1, 0) + 2
        x_high = jnp.minimum(i + 1, depth - 1) + 2
        for y in range(2, breadth + 2):
            at = (i + 1) * cross + y - 1
            west = weights[at, WEST] * inside_x[0]
            east = weights[at, EAST] * inside_x[1]
            for f in range(parts):
                v = ext[f, x, y]
                near = west * ext[f, x_low, y] + east * ext[f, x_high, y]
                if y > 2:
                    near = near + weights[at, SOUTH] * ext[f, x, y - 1]
                if y < breadth + 1:
                    near = near + weights[at, NORTH] * ext[f, x, y + 1]
                near = near + weights[at, LOW] * pltpu.roll(v, 1, 1)
                near = near + weights[at, HIGH_Z] * pltpu.roll(v, length - 1, 1)
                own_p[f, i + 1, y - 1] = packed(near - v)
                phis[f, i, y - 2] = packed(v)
                sums = gram(sums, weights[at, 7] * (v - near), f, x, y)
        return sums

    def side_block(along, fixed_x, fixed_y, dx, dy, turned=False):
        which = {(-1, 0): WEST, (1, 0): EAST, (0, -1): SOUTH, (0, 1): NORTH}[(dx, dy)]

        def one(i, sums):
            x = i + 2 if fixed_x is None else fixed_x
            y = i + 2 if fixed_y is None else fixed_y
            at = (x - 1) * cross + y - 1
            weight = weights[at, which] * weights[at, 7]
            for f in range(parts):
                if turned:
                    sums = gram(sums, -weight * ext[f, x + dx, y + dy], f, x, y)
                else:
                    sums = gram(sums, -weight * ext[f, x, y], f, x + dx, y + dy)
            return sums

        return lax.fori_loop(0, along, one, (zero,) * width)

    def put(row, totals, at):
        for l in range(width):
            row = row + placed(totals[l], at + l)
        return row

    row = put(row, lax.fori_loop(0, depth, own_block, (zero,) * width), index_y * width)
    arrived(9, 11)
    row = put(row, side_block(depth, None, 2, 0, -1), (index_y - 1) * width)
    row = put(row, side_block(depth, None, breadth + 1, 0, 1), (index_y + 1) * width)
    arrived(8, 9)
    row = put(row, side_block(breadth, depth + 1, None, 1, 0, True), size + index_y * width)
    row = put(row, side_block(breadth, depth + 1, None, 1, 0), 2 * size + index_y * width)
    panel[...] = row
    gathered[me] = row

    def send(g, h):
        pltpu.make_async_remote_copy(
            src_ref=panel,
            dst_ref=gathered.at[me],
            send_sem=panel_send,
            recv_sem=panel_recv,
            device_id=(g, h),
            device_id_type=MESH,
        ).start()

    each_other(send)
    send_res(0, parts, (0, 1))

    def no_halo(way):
        dx, dy = ways[way]

        def wipe_x():
            hx[way] = jnp.zeros(hx.shape[1:], jnp.float32)

        def wipe_y():
            hy[way - 2] = jnp.zeros(hy.shape[1:], jnp.float32)

        pl.when(jnp.logical_not(can(dx, dy)))(wipe_x if dx else wipe_y)

    for way in range(4):
        no_halo(way)

    def multiples(i, carry):
        for j in range(cross):
            at = i * cross + j
            for q in range(WEST, HIGH_Z + 1):
                w = weights[at, q]
                for n, rate in enumerate(rates):
                    hweights[n, at, q - 1] = rate * w
        return carry

    lax.fori_loop(0, depth + 2, multiples, 0)

    def reach(f, at, which, x, y):
        return packed(weights[at, which] * ext[f, x, y])

    arrived(11, 12)

    def seams_x(i, carry):
        y = i + 2
        for f in range(parts):
            side_x[f, 1, i + 1] = reach(f, cross + i + 1, WEST, 1, y)
            side_x[f, 2, i + 1] = reach(f, depth * cross + i + 1, EAST, depth + 2, y)
            own_p[f, 0, i + 1] = reach(f, i + 1, EAST, 2, y)
            own_p[f, depth + 1, i + 1] = reach(f, (depth + 1) * cross + i + 1, WEST, depth + 1, y)
        return carry

    def seams_y(i, carry):
        x = i + 2
        at = (i + 1) * cross
        for f in range(parts):
            side_y[f, i, 1] = reach(f, at + 1, SOUTH, x, 1)
            side_y[f, i, 2] = reach(f, at + breadth, NORTH, x, breadth + 2)
            own_p[f, i + 1, 0] = reach(f, at, NORTH, x, 2)
            own_p[f, i + 1, breadth + 1] = reach(f, at + breadth + 1, SOUTH, x, breadth + 1)
        return carry

    lax.fori_loop(0, breadth, seams_x, 0)
    lax.fori_loop(0, depth, seams_y, 0)

    for buffer in (first, second, third):
        def clear_row(y, carry, buffer=buffer):
            buffer[y] = tall
            buffer[(depth + 3) * wide + y] = tall
            return carry

        def clear_column(x, carry, buffer=buffer):
            buffer[x * wide] = tall
            buffer[x * wide + wide - 1] = tall
            return carry

        lax.fori_loop(0, wide, clear_row, 0)
        lax.fori_loop(0, depth + 4, clear_column, 0)
    for x in (1, depth + 2):
        for y in (1, breadth + 2):
            first[x * wide + y] = tall

    arrived(12, 16)
    for f in range(parts):
        for slot, at_low, at_high, way, x in (
            (0, 1, breadth, None, 1), (1, cross, cross + breadth + 1, WEST, 1),
            (2, depth * cross, depth * cross + breadth + 1, EAST, depth + 2),
            (3, (depth + 1) * cross + 1, (depth + 1) * cross + breadth, None, depth + 2),
        ):
            side_x[f, slot, 0] = reach(f, at_low, way or SOUTH, x, 1)
            side_x[f, slot, breadth + 1] = reach(f, at_high, way or NORTH, x, breadth + 2)

    def bounds(i, last):
        return (
            jnp.where(i > 0, 1.0, 0.0).astype(jnp.float32),
            jnp.where(i < last, 1.0, 0.0).astype(jnp.float32),
        )

    def halo_term(f, at, x, y, terms):
        v = ext[f, x, y]
        near = weights[at, LOW] * pltpu.roll(v, 1, 1)
        near = near + weights[at, HIGH_Z] * pltpu.roll(v, length - 1, 1)
        for weight, px, py in terms:
            near = near + weight * ext[f, px, py]
        return packed(near - v)

    def rims_x(i, carry):
        y = i + 2
        low, high = bounds(i, breadth - 1)
        for slot, x, outward, px in ((0, 1, WEST, 0), (3, depth + 2, EAST, depth + 3)):
            at = (x - 1) * cross + i + 1
            terms = (
                (weights[at, outward], px, y),
                (weights[at, SOUTH] * low, x, y - 1),
                (weights[at, NORTH] * high, x, y + 1),
            )
            for f in range(parts):
                side_x[f, slot, i + 1] = halo_term(f, at, x, y, terms)
        return carry

    def rims_y(i, carry):
        x = i + 2
        low, high = bounds(i, depth - 1)
        for slot, y, outward, py in ((0, 1, SOUTH, 0), (3, breadth + 2, NORTH, breadth + 3)):
            at = (i + 1) * cross + y - 1
            terms = (
                (weights[at, outward], x, py),
                (weights[at, WEST] * low, x - 1, y),
                (weights[at, EAST] * high, x + 1, y),
            )
            for f in range(parts):
                side_y[f, i, slot] = halo_term(f, at, x, y, terms)
        return carry

    lax.fori_loop(0, breadth, rims_x, 0)
    lax.fori_loop(0, depth, rims_y, 0)

    everyone = gathered.at[pl.ds(0, count - 1)]
    panels_all = pltpu.make_async_remote_copy(
        src_ref=everyone,
        dst_ref=everyone,
        send_sem=panel_send,
        recv_sem=panel_recv,
        device_id=(lax.rem(index_x + 1, count_x), index_y),
        device_id_type=MESH,
    )
    panels_all.wait_recv()
    panels = [gathered[pl.ds(g * count_y, count_y)].reshape(size, panel.shape[1]) for g in range(count_x)]
    spot = lax.broadcasted_iota(jnp.int32, panels[0].shape, 1)
    is_low = (spot >= size) & (spot < 2 * size)
    below = [jnp.zeros(panels[0].shape, jnp.float32)] + panels[:-1]
    panels = [jnp.where(is_low, b, p) for b, p in zip(below, panels)]
    for g, x in enumerate(cyclic_solve(panels, size)):
        coeffs[pl.ds(g * size, size), :] = x
    mine[...] = coeffs[pl.ds(pl.multiple_of(me * width, width), width), :]

    for slot in range(10):
        step_x, step_y = (slot // 3 - 1, slot % 3 - 1) if slot < 9 else (0, 0)
        near_x = jnp.clip(index_x + step_x, 0, count_x - 1)
        near_y = jnp.clip(index_y + step_y, 0, count_y - 1)
        begin = pl.multiple_of((near_x * count_y + near_y) * width, width)
        c = coeffs[pl.ds(begin, width), :]
        if slot < 9:
            c = scale_all * c
        coarse = c.astype(jnp.bfloat16).astype(jnp.float32)
        fine = c - coarse
        lhs[slot] = jnp.concatenate([coarse, coarse, fine, fine], axis=0).T.astype(jnp.bfloat16)

    def combine(slot, cells):
        block = jnp.concatenate(cells, axis=1)
        return jnp.dot(
            lhs[slot], jnp.concatenate([block, block], axis=0), preferred_element_type=jnp.float32
        )

    def cut(block, i):
        return block[:, i * length : (i + 1) * length]

    def spread(w):
        return jnp.concatenate([w] * (rhs // width), axis=0)

    def beside(source, n, x, y):
        cell = x * wide + y
        at = (x - 1) * cross + y - 1
        centre = source[cell]
        total = spread(hweights[n, at, 0]) * source[cell - wide]
        total = total + spread(hweights[n, at, 1]) * source[cell + wide]
        total = total + spread(hweights[n, at, 2]) * source[cell - 1]
        total = total + spread(hweights[n, at, 3]) * source[cell + 1]
        total = total + spread(hweights[n, at, 4]) * pltpu.roll(centre, 1, 1)
        total = total + spread(hweights[n, at, 5]) * pltpu.roll(centre, length - 1, 1)
        return total

    def in_groups(start, rows, act):
        step = next(k for k in (5, 4, 3, 2, 1) if rows % k == 0)

        def some(i, carry):
            for k in range(step):
                act(start + step * i + k)
            return carry

        lax.fori_loop(0, rows // step, some, 0)

    def component(part, carry):
        def halos(which):
            for way in which:
                dx, dy = ways[way]
                pl.when(can(-dx, -dy))(res_copy(way, part).wait_recv)

        def force_row(i, side=None):
            own = combine(4, [own_p[part, i + 1, j] for j in range(cross)])
            south = combine(3, [side_y[part, i, j] for j in (0, 1)])
            north = combine(5, [side_y[part, i, j] for j in (2, 3)])
            tiles = rows_of(rbuf.at[part * depth + i])
            if side is not None:
                corner, middle = outer(side, 1 + side)
            for j in range(cross):
                value = cut(own, j)
                if j < 2:
                    value = value + cut(south, j)
                if j >= breadth:
                    value = value + cut(north, j - breadth)
                if j == 0 or j == cross - 1:
                    loaded = hy[j // breadth, part, i]
                else:
                    loaded = tiles[pl.ds(j - 1, rhs, stride=breadth), :]
                value = spread(weights[(i + 1) * cross + j, 0]) * loaded + value
                if side is not None:
                    value = value + (cut(middle, j - 1) if 0 < j < cross - 1 else corner[j // breadth])
                first[(i + 2) * wide + j + 1] = value

        def outer(side, edge):
            block = 6 * side
            corner = [combine(block + 2 * end, [side_x[part, edge, end * (breadth + 1)]]) for end in range(2)]
            return corner, combine(block + 1, [side_x[part, edge, j + 1] for j in range(breadth)])

        def force_inner(i, carry):
            force_row(i)
            return carry

        halos((2, 3))
        lax.fori_loop(1, depth - 1, force_inner, 0)
        for side in range(2):
            force_row(side * (depth - 1), side)
        halos((0, 1))
        for side in range(2):
            x = side * (depth + 1) + 1
            corner, middle = outer(side, 3 * side)
            own = combine(4, [own_p[part, x - 1, j + 1] for j in range(breadth)])
            tiles = rows_of(hx.at[side, part])
            for j in range(breadth):
                value = cut(middle, j) + cut(own, j)
                if j == 0:
                    value = value + corner[0]
                if j == breadth - 1:
                    value = value + corner[1]
                loaded = tiles[pl.ds(j, rhs, stride=breadth), :]
                value = spread(weights[(x - 1) * cross + j + 1, 0]) * loaded + value
                first[x * wide + j + 2] = value

        source, target, spare = first, second, third
        for n in range(len(rates) - 1):
            def relax(x, source=source, target=target, n=n):
                for j in range(cross):
                    cell = x * wide + j + 1
                    target[cell] = first[cell] + beside(source, n, x, j + 1)

            in_groups(1, depth + 2, relax)
            source, target, spare = target, spare, target

        def finish(x):
            fine = combine(9, [phis[part, x - 2, j] for j in range(breadth)])
            row = part * depth + x - 2
            tiles = rows_of(obuf.at[row])
            for j in range(breadth):
                value = cut(fine, j) + first[x * wide + j + 2]
                value = value + beside(source, len(rates) - 1, x, j + 2)
                tiles[pl.ds(j, rhs, stride=breadth), :] = value
            pltpu.make_async_copy(obuf.at[row], out.at[:, part, x - 2], out_sem).start()

        in_groups(2, depth, finish)
        return carry

    lax.fori_loop(0, parts, component, 0)
    panels_all.wait_send()
    for sends, _, copy in started:
        pl.when(sends)(copy.wait_send)
    for part in range(parts):
        for way in range(4):
            pl.when(can(*ways[way]))(res_copy(way, part).wait_send)
    pltpu.make_async_copy(obuf, obuf, out_sem).wait()


def deliver_kernel(chunks, solved, field, mine, out, held, in_sem, out_sem):
    rows = held.shape[0] // chunks
    for i in range(chunks):
        part = pl.ds(i * rows, rows)
        pltpu.make_async_copy(field.at[part], held.at[part], in_sem.at[i]).start()
    mine[...] = solved[...]
    for i in range(chunks):
        part = pl.ds(i * rows, rows)
        pltpu.make_async_copy(field.at[part], held.at[part], in_sem.at[i]).wait()
        pltpu.make_async_copy(held.at[part], out.at[part], out_sem).start()
    pltpu.make_async_copy(held, out, out_sem).wait()


def deliver(solved, field):
    chunks = 8 if field.shape[0] % 8 == 0 else 1
    vmem = pl.BlockSpec(memory_space=pltpu.VMEM)
    hbm = pl.BlockSpec(memory_space=pl.ANY)
    return pl.pallas_call(
        functools.partial(deliver_kernel, chunks),
        out_shape=(
            jax.ShapeDtypeStruct(solved.shape, solved.dtype),
            jax.ShapeDtypeStruct(field.shape, field.dtype),
        ),
        in_specs=[vmem, hbm],
        out_specs=(vmem, hbm),
        scratch_shapes=[
            pltpu.VMEM(field.shape, field.dtype),
            pltpu.SemaphoreType.DMA((chunks,)),
            pltpu.SemaphoreType.DMA,
        ],
        compiler_params=pltpu.CompilerParams(vmem_limit_bytes=60 * 1024 * 1024),
    )(solved, field)


def on_device(residuals, vectors, phases, stiffness):
    count_x = lax.axis_size("gx")
    count_y = lax.axis_size("yz")
    rhs, parts, depth, breadth, length = residuals.shape
    width = vectors.shape[0]
    count = count_x * count_y
    scale_all, rates = sweep_rates(SWEEPS, 0.8)
    vmem = pl.BlockSpec(memory_space=pltpu.VMEM)
    hbm = pl.BlockSpec(memory_space=pl.ANY)
    panel = (width, 3 * count_y * width + rhs)
    cells = (depth + 2) * (breadth + 2)
    field = pltpu.VMEM(((depth + 4) * (breadth + 4), rhs, length), jnp.float32)
    slots = 16 + 4 * parts
    f32, half = jnp.float32, jnp.bfloat16
    solved, field_out = pl.pallas_call(
        functools.partial(kernel, count_x, count_y, scale_all, rates),
        out_shape=(
            jax.ShapeDtypeStruct((width, rhs), f32),
            jax.ShapeDtypeStruct(residuals.shape, f32),
        ),
        in_specs=[pl.BlockSpec(memory_space=pltpu.SMEM), vmem, hbm, hbm],
        out_specs=(vmem, hbm),
        scratch_shapes=[
            pltpu.VMEM((parts + 1, depth + 4, breadth + 4, width, length), f32),
            pltpu.VMEM((parts * depth, width, breadth, length), f32),
            pltpu.VMEM((parts * depth, rhs, breadth, length), f32),
            pltpu.VMEM((2, parts, rhs, breadth, length), f32),
            pltpu.VMEM((2, parts, depth, rhs, length), f32),
            pltpu.VMEM((2, parts, depth, rhs, length), f32),
            pltpu.VMEM((parts * depth, rhs, breadth, length), f32),
            pltpu.VMEM((depth * breadth, length), f32),
            pltpu.VMEM((2, 2, depth, length), f32),
            pltpu.VMEM((2, 2 * breadth, length), f32),
            pltpu.VMEM((2, 2, depth, length), f32),
            pltpu.VMEM((cells, 8, width, length), f32),
            pltpu.VMEM((SWEEPS - 1, cells, 6, width, length), f32),
            pltpu.VMEM((parts, depth + 2, breadth + 2, 2 * width, length), half),
            pltpu.VMEM((parts, depth, 4, 2 * width, length), half),
            pltpu.VMEM((parts, 4, breadth + 2, 2 * width, length), half),
            pltpu.VMEM((parts, depth, breadth, 2 * width, length), half),
            pltpu.VMEM((10, rhs, 4 * width), half),
            pltpu.VMEM(panel, f32),
            pltpu.VMEM((count,) + panel, f32),
            pltpu.VMEM((count * width, rhs), f32),
            field, field, field,
            pltpu.SemaphoreType.DMA,
            pltpu.SemaphoreType.DMA,
            pltpu.SemaphoreType.DMA,
            pltpu.SemaphoreType.DMA,
            pltpu.SemaphoreType.DMA,
            pltpu.SemaphoreType.DMA((slots,)),
            pltpu.SemaphoreType.DMA((slots,)),
        ],
        compiler_params=pltpu.CompilerParams(
            collective_id=0, has_side_effects=True, vmem_limit_bytes=60 * 1024 * 1024
        ),
    )(stiffness, phases, vectors, residuals)
    return deliver(solved, field_out)


def solution(mesh):
    return jax.shard_map(
        on_device,
        mesh=mesh,
        in_specs=(
            P(None, None, "gx", "yz", None),
            P(None, None, "gx", "yz", None),
            P("gx", "yz", None),
            P(),
        ),
        out_specs=(P(("gx", "yz"), None), P(None, None, "gx", "yz", None)),
        check_vma=False,
    )
```
